256 devices in a mesh: dom: 64 (over x, z_hi, y), blk: 4 (over z_lo, core).
Axes of the slice: x: 4, y: 4, z: 8 (z_hi: 4, z_lo: 2; z = z_hi * 2 + z_lo), core: 2. Of those that a mesh axis runs over, the one named last changes fastest.
Arguments:
- adjoint_start: float32 [1536, 3, 320], P('dom', None, 'blk'), may hold values from -6 to 6
- right_sides: float32 [1536, 3, 320], P('dom', None, 'blk'), may hold values from -6 to 6
- jac_blocks: bfloat16 [1536, 7, 320, 320], P('dom', None, 'blk'), may hold values from -0.125 to 0.125
- block_inverse: bfloat16 [1536, 320, 320], P('dom', 'blk'), may hold values from -0.15625 to 0.15625
- neighbours: int32 [1536, 6], P('dom'), may hold values from 0 to 1535, as said below
- pseudo_shift: float32 [1536], P('dom'), may hold values from 0.25 to 2
- shape_partials: bfloat16 [1536, 320, 192], P('dom', 'blk'), may hold values from -0.3125 to 0.3125
- node_ids: int32 [1536, 64], P('dom'), may hold values from 0 to 49151, as said below
Outputs:
- adjoint: float32 [1536, 3, 320], P('dom', None, 'blk')
- shape_gradient: float32 [9, 49152], P(None, ('dom', 'blk'))
The draws below stay inside these ranges and needn't reach their ends.
Inputs may be any that keep to these rules, and one draw needn't show every extreme that they name: `neighbours`: partition k holds elements k * 24 to (k + 1) * 24 - 1; every neighbour of an element lies in its own partition or in the partition just before or after it. `node_ids`: partition k owns mesh nodes k * 768 to (k + 1) * 768 - 1; every node of an element is owned by the element's partition or by the partition just before or after it.
All inputs are finite; a program needn't handle non-finite values.
Results may differ from the reference program's by a relative error of at most 0.0038.
Values may be sent and summed in bfloat16 or wider, within the bound.
A program may use at most 64 MiB of HBM per device.

```python
import math
import jax
import jax.numpy as jnp
from jax import lax

B = 320
FACES = 6
RHS = 3
SWEEPS = 2
ENODES = 64
E_DEV = 24
NQ = 192
NODE_DEV = 768
ELEMS = 1536
NODES = 49152


def draw_neighbours(key, part):
    part_total = ELEMS // E_DEV
    element = jnp.arange(ELEMS, dtype=jnp.int32)
    owner_part = element // E_DEV
    lowest = jnp.maximum(owner_part - 1, 0) * E_DEV
    highest = jnp.minimum(owner_part + 2, part_total) * E_DEV
    chosen = jax.random.randint(key, (ELEMS, FACES), lowest[:, None], highest[:, None], dtype=jnp.int32)
    chosen = chosen.at[0, 0].set(0)
    chosen = chosen.at[ELEMS - 1, FACES - 1].set(ELEMS - 1)
    return chosen


def draw_node_ids(key, part):
    part_total = ELEMS // E_DEV
    element = jnp.arange(ELEMS, dtype=jnp.int32)
    owner_part = element // E_DEV
    lowest = jnp.maximum(owner_part - 1, 0) * NODE_DEV
    highest = jnp.minimum(owner_part + 2, part_total) * NODE_DEV
    chosen = jax.random.randint(key, (ELEMS, ENODES), lowest[:, None], highest[:, None], dtype=jnp.int32)
    chosen = chosen.at[0, 0].set(0)
    chosen = chosen.at[ELEMS - 1, ENODES - 1].set(NODES - 1)
    return chosen


def block_scale(own_key, extent, pieces, low, top_value):
    level, own = 1.0, jax.random.fold_in(own_key, 6)
    for dim, shards_of in pieces:
        steps = jnp.exp(jax.random.uniform(jax.random.fold_in(own, dim), (shards_of,), jnp.float32, low / len(pieces), top_value / len(pieces)))
        level = level * jnp.repeat(steps, extent[dim] // shards_of).reshape([-1 if axis == dim else 1 for axis in range(len(extent))])
    return level


def gaussian(stream_key, dims, deviation, limit, split=(), kind=jnp.bfloat16):
    result = deviation * jax.random.normal(stream_key, dims, jnp.float32)
    if split:
        result = result * block_scale(stream_key, dims, split, -0.22, 0.18)
    return jnp.clip(result, -limit, limit).astype(kind)


def setup_inputs(seed: int = 0) -> dict:
    keys = jax.random.split(jax.random.key(seed), 9)
    return {
        "adjoint_start": gaussian(keys[0], (ELEMS, RHS, B), 1.0, 6.0, ((0, 64), (2, 4)), jnp.float32),
        "right_sides": gaussian(keys[1], (ELEMS, RHS, B), 1.0, 6.0, ((0, 64), (2, 4)), jnp.float32),
        "jac_blocks": gaussian(keys[2], (ELEMS, FACES + 1, B, B), (7 * B) ** -0.5, 0.125, ((0, 64), (2, 4))),
        "block_inverse": gaussian(keys[3], (ELEMS, B, B), (4 * B) ** -0.5, 0.15625, ((0, 64), (1, 4))),
        "neighbours": draw_neighbours(jax.random.fold_in(keys[8], 71), 0),
        "pseudo_shift": jnp.clip(jnp.exp(math.log(2.0) - 2.0794415 * jax.random.uniform(keys[5], (ELEMS,), jnp.float32) ** block_scale(keys[5], (ELEMS,), ((0, 64),), -0.2, 0.2)), 0.25, 2.0),
        "shape_partials": gaussian(keys[6], (ELEMS, B, NQ), B ** -0.5, 0.3125, ((0, 64), (1, 4))),
        "node_ids": draw_node_ids(jax.random.fold_in(keys[8], 71), 0),
    }


def reference(adjoint_start, right_sides, jac_blocks, block_inverse, neighbours, pseudo_shift, shape_partials, node_ids):
    part_total = ELEMS // E_DEV
    element = jnp.arange(ELEMS, dtype=jnp.int32)
    slots = jnp.concatenate([element[:, None], neighbours], axis=1)
    jac_parts = jac_blocks.reshape(part_total, E_DEV, FACES + 1, B, B)
    inv_parts = block_inverse.reshape(part_total, E_DEV, B, B)
    shape_parts = shape_partials.reshape(part_total, E_DEV, B, NQ)
    high = lax.Precision.HIGHEST

    def apply_jac(pair):
        blocks, picked = pair
        return jnp.einsum("ekrc,ekjc->ejr", blocks.astype(jnp.float32), picked.astype(jnp.float32), precision=high)

    def apply_inv(pair):
        blocks, resid = pair
        return jnp.einsum("erc,ejc->ejr", blocks.astype(jnp.float32), resid.astype(jnp.float32), precision=high)

    def apply_shape(pair):
        half, blocks = pair
        return jnp.einsum("ejr,erq->ejq", half.astype(jnp.float32), blocks.astype(jnp.float32), precision=high)

    adjoint = adjoint_start
    for sweep in range(SWEEPS):
        adj_half = adjoint.astype(jnp.bfloat16)
        picked = adj_half[slots].reshape(part_total, E_DEV, FACES + 1, RHS, B)
        product = lax.map(apply_jac, (jac_parts, picked)).reshape(ELEMS, RHS, B)
        image = pseudo_shift[:, None, None] * adjoint + product
        resid_half = (right_sides - image).astype(jnp.bfloat16)
        update = lax.map(apply_inv, (inv_parts, resid_half.reshape(part_total, E_DEV, RHS, B)))
        adjoint = adjoint + update.reshape(ELEMS, RHS, B)
    final_half = adjoint.astype(jnp.bfloat16)
    weighted = -lax.map(apply_shape, (final_half.reshape(part_total, E_DEV, RHS, B), shape_parts))
    weighted = weighted.reshape(ELEMS, RHS, ENODES, 3)
    values = jnp.transpose(weighted, (0, 2, 1, 3)).reshape(ELEMS * ENODES, RHS * 3)
    gradient = jax.ops.segment_sum(values, node_ids.reshape(-1), NODES)
    return adjoint, gradient.T
```

```python
import functools

import jax
import jax.numpy as jnp
from jax import lax
from jax.experimental import pallas as pl
from jax.experimental.pallas import tpu as pltpu
from jax.sharding import PartitionSpec as P

RHS = 3
SWEEPS = 2
NODE_DEV = 768
MESH = pl.DeviceIdType.MESH


def _halo_partners(nb):
    return [(delta, m) for delta in (-1, 0, 1) for m in range(nb) if (delta, m) != (0, 0)]


def _barrier(partners, in_range, d, b, nb):
    barrier = pltpu.get_barrier_semaphore()
    for delta, m in partners:
        @pl.when(in_range(d + delta))
        def _(delta=delta, m=m):
            pl.semaphore_signal(
                barrier, 1, device_id=(d + delta, (b + m) % nb), device_id_type=MESH
            )
    nd = lax.axis_size("dom")
    has_lower = (d + nd - 1) // nd
    has_upper = (2 * nd - 2 - d) // nd
    peers = [sum(1 for delta, _ in partners if delta == side) for side in (-1, 0, 1)]
    pl.semaphore_wait(barrier, peers[1] + peers[0] * has_lower + peers[2] * has_upper)


def _halo_gather_kernel(x_ref, out_ref, buf, send_sem, recv_sem):
    d, b = lax.axis_index("dom"), lax.axis_index("blk")
    nd, nb = lax.axis_size("dom"), lax.axis_size("blk")
    partners = _halo_partners(nb)

    def in_range(i):
        return (i >= 0) & (i < nd)

    _barrier(partners, in_range, d, b, nb)

    def outgoing(delta, m):
        return pltpu.make_async_remote_copy(
            src_ref=x_ref,
            dst_ref=buf.at[1 - delta, b],
            send_sem=send_sem.at[delta + 1, m],
            recv_sem=recv_sem.at[1 - delta, b],
            device_id=(d + delta, (b + m) % nb),
            device_id_type=MESH,
        )

    for delta, m in partners:
        pl.when(in_range(d + delta))(lambda delta=delta, m=m: outgoing(delta, m).start())
    buf[1, b] = x_ref[...]
    for side in (-1, 1):
        @pl.when(jnp.logical_not(in_range(d + side)))
        def _(side=side):
            buf[1 + side] = jnp.zeros(buf.shape[1:], buf.dtype)
    for delta, m in partners:
        pl.when(in_range(d + delta))(lambda delta=delta, m=m: outgoing(delta, m).wait_send())
    for delta, m in partners:
        p, s = 1 + delta, (b + m) % nb

        @pl.when(in_range(d + delta))
        def _(p=p, s=s):
            pltpu.make_async_remote_copy(
                src_ref=x_ref,
                dst_ref=buf.at[p, s],
                send_sem=send_sem.at[p, 0],
                recv_sem=recv_sem.at[p, s],
                device_id=(d + p - 1, s),
                device_id_type=MESH,
            ).wait_recv()

    out_ref[...] = buf[...]


def _blk_gather_kernel(x_ref, out_ref, buf, send_sem, recv_sem):
    d, b = lax.axis_index("dom"), lax.axis_index("blk")
    nd, nb = lax.axis_size("dom"), lax.axis_size("blk")
    partners = [(0, m) for m in range(1, nb)]
    _barrier(partners, lambda i: (i >= 0) & (i < nd), d, b, nb)

    def outgoing(m):
        return pltpu.make_async_remote_copy(
            src_ref=x_ref,
            dst_ref=buf.at[b],
            send_sem=send_sem.at[m],
            recv_sem=recv_sem.at[b],
            device_id=(d, (b + m) % nb),
            device_id_type=MESH,
        )

    for _, m in partners:
        outgoing(m).start()
    buf[b] = x_ref[...]
    for _, m in partners:
        outgoing(m).wait_send()
    for _, m in partners:
        s = (b + m) % nb
        pltpu.make_async_remote_copy(
            src_ref=x_ref,
            dst_ref=buf.at[s],
            send_sem=send_sem.at[0],
            recv_sem=recv_sem.at[s],
            device_id=(d, s),
            device_id_type=MESH,
        ).wait_recv()
    out_ref[...] = buf[...]


def _node_reduce_kernel(x_ref, out_ref, buf, send_sem, recv_sem):
    d, b = lax.axis_index("dom"), lax.axis_index("blk")
    nd, nb = lax.axis_size("dom"), lax.axis_size("blk")
    partners = _halo_partners(nb)

    def in_range(i):
        return (i >= 0) & (i < nd)

    _barrier(partners, in_range, d, b, nb)

    def outgoing(delta, m):
        p = 1 + delta
        return pltpu.make_async_remote_copy(
            src_ref=x_ref.at[p, (b + m) % nb],
            dst_ref=buf.at[p, b],
            send_sem=send_sem.at[p, m],
            recv_sem=recv_sem.at[p, b],
            device_id=(d + delta, (b + m) % nb),
            device_id_type=MESH,
        )

    for delta, m in partners:
        pl.when(in_range(d + delta))(lambda delta=delta, m=m: outgoing(delta, m).start())
    out_ref[...] = x_ref[1, b]
    for delta, m in partners:
        pl.when(in_range(d + delta))(lambda delta=delta, m=m: outgoing(delta, m).wait_send())
    for delta, m in partners:
        p, s = 1 + delta, (b + m) % nb

        @pl.when(in_range(d - delta))
        def _(p=p, s=s):
            pltpu.make_async_remote_copy(
                src_ref=x_ref.at[p, s],
                dst_ref=buf.at[p, s],
                send_sem=send_sem.at[p, 0],
                recv_sem=recv_sem.at[p, s],
                device_id=(d - delta, s),
                device_id_type=MESH,
            ).wait_recv()
            out_ref[...] += buf[p, s]


def _exchange(kernel, x, out_shape, buf_shape, sem_shape, collective_id):
    return pl.pallas_call(
        kernel,
        out_shape=jax.ShapeDtypeStruct(out_shape, x.dtype),
        in_specs=[pl.BlockSpec(memory_space=pltpu.VMEM)],
        out_specs=pl.BlockSpec(memory_space=pltpu.VMEM),
        scratch_shapes=[
            pltpu.VMEM(buf_shape, x.dtype),
            pltpu.SemaphoreType.DMA(sem_shape),
            pltpu.SemaphoreType.DMA(sem_shape),
        ],
        compiler_params=pltpu.CompilerParams(
            collective_id=collective_id, has_side_effects=True
        ),
    )(x)


def halo_gather(x, nb, collective_id):
    shape = (3, nb) + x.shape
    out = _exchange(_halo_gather_kernel, x, shape, shape, (3, nb), collective_id)
    e, r, c = x.shape
    return jnp.transpose(out, (0, 2, 3, 1, 4)).reshape(3 * e, r, nb * c)


def blk_gather(x, nb, collective_id):
    shape = (nb,) + x.shape
    out = _exchange(_blk_gather_kernel, x, shape, shape, (nb,), collective_id)
    e, r, c = x.shape
    return jnp.transpose(out, (1, 2, 0, 3)).reshape(e, r, nb * c)


def node_reduce(chunks, collective_id):
    nb = chunks.shape[1]
    return _exchange(
        _node_reduce_kernel, chunks, chunks.shape[2:], chunks.shape, (3, nb), collective_id
    )


def local(
    adjoint_start,
    right_sides,
    jac_blocks,
    block_inverse,
    neighbours,
    pseudo_shift,
    shape_partials,
    node_ids,
):
    local_count = neighbours.shape[0]
    nb = lax.axis_size("blk")
    part_index = lax.axis_index("dom")
    first_slot = (part_index - 1) * local_count
    self_slots = jnp.arange(local_count, dtype=jnp.int32)[:, None] + local_count
    slots = jnp.concatenate([self_slots, neighbours - first_slot], axis=1)
    adjoint = adjoint_start
    for sweep in range(SWEEPS):
        adj_half = adjoint.astype(jnp.bfloat16)
        extended = halo_gather(adj_half, nb, collective_id=2 * sweep)
        picked = extended[slots]
        product = jnp.einsum(
            "ekrc,ekjc->ejr", jac_blocks, picked, preferred_element_type=jnp.float32
        )
        image = pseudo_shift[:, None, None] * adjoint + product
        resid_half = (right_sides - image).astype(jnp.bfloat16)
        resid_full = blk_gather(resid_half, nb, collective_id=2 * sweep + 1)
        adjoint = adjoint + jnp.einsum(
            "erc,ejc->ejr", block_inverse, resid_full, preferred_element_type=jnp.float32
        )
    final_half = adjoint.astype(jnp.bfloat16)
    weighted = -jnp.einsum(
        "ejr,erq->ejq", final_half, shape_partials, preferred_element_type=jnp.float32
    )
    node_width = node_ids.shape[1]
    weighted = weighted.reshape(local_count, RHS, node_width, 3)
    values = jnp.transpose(weighted, (0, 2, 1, 3)).reshape(local_count * node_width, RHS * 3)
    node_slots = (node_ids - (part_index - 1) * NODE_DEV).reshape(-1)
    partial_sums = jax.ops.segment_sum(values, node_slots, 3 * NODE_DEV).T
    chunks = jnp.transpose(
        partial_sums.reshape(RHS * 3, 3, nb, NODE_DEV // nb), (1, 2, 0, 3)
    )
    shape_gradient = node_reduce(chunks, collective_id=2 * SWEEPS)
    return (adjoint, shape_gradient)


def solution(mesh):
    in_specs = (
        P("dom", None, "blk"),
        P("dom", None, "blk"),
        P("dom", None, "blk", None),
        P("dom", "blk", None),
        P("dom", None),
        P("dom"),
        P("dom", "blk", None),
        P("dom", None),
    )
    out_specs = (P("dom", None, "blk"), P(None, ("dom", "blk")))
    return jax.shard_map(local, mesh=mesh, in_specs=in_specs, out_specs=out_specs, check_vma=False)
```

```python
import functools

import jax
import jax.numpy as jnp
from jax import lax
from jax.experimental import pallas as pl
from jax.experimental.pallas import tpu as pltpu
from jax.sharding import PartitionSpec as P

RHS = 3
SWEEPS = 2
NODE_DEV = 768
MESH = pl.DeviceIdType.MESH


def _halo_partners(nb):
    return [(delta, m) for delta in (-1, 0, 1) for m in range(nb) if (delta, m) != (0, 0)]


def _barrier(partners, in_range, d, b, nb):
    barrier = pltpu.get_barrier_semaphore()
    for delta, m in partners:
        @pl.when(in_range(d + delta))
        def _(delta=delta, m=m):
            pl.semaphore_signal(
                barrier, 1, device_id=(d + delta, (b + m) % nb), device_id_type=MESH
            )
    nd = lax.axis_size("dom")
    has_lower = (d + nd - 1) // nd
    has_upper = (2 * nd - 2 - d) // nd
    peers = [sum(1 for delta, _ in partners if delta == side) for side in (-1, 0, 1)]
    pl.semaphore_wait(barrier, peers[1] + peers[0] * has_lower + peers[2] * has_upper)


def _halo_gather_kernel(x_ref, out_ref, buf, send_sem, recv_sem):
    d, b = lax.axis_index("dom"), lax.axis_index("blk")
    nd, nb = lax.axis_size("dom"), lax.axis_size("blk")
    partners = _halo_partners(nb)

    def in_range(i):
        return (i >= 0) & (i < nd)

    _barrier(partners, in_range, d, b, nb)

    def outgoing(delta, m):
        return pltpu.make_async_remote_copy(
            src_ref=x_ref,
            dst_ref=buf.at[1 - delta, b],
            send_sem=send_sem.at[delta + 1, m],
            recv_sem=recv_sem.at[1 - delta, b],
            device_id=(d + delta, (b + m) % nb),
            device_id_type=MESH,
        )

    for delta, m in partners:
        pl.when(in_range(d + delta))(lambda delta=delta, m=m: outgoing(delta, m).start())
    buf[1, b] = x_ref[...]
    for side in (-1, 1):
        @pl.when(jnp.logical_not(in_range(d + side)))
        def _(side=side):
            buf[1 + side] = jnp.zeros(buf.shape[1:], buf.dtype)
    for delta, m in partners:
        pl.when(in_range(d + delta))(lambda delta=delta, m=m: outgoing(delta, m).wait_send())
    for delta, m in partners:
        p, s = 1 + delta, (b + m) % nb

        @pl.when(in_range(d + delta))
        def _(p=p, s=s):
            pltpu.make_async_remote_copy(
                src_ref=x_ref,
                dst_ref=buf.at[p, s],
                send_sem=send_sem.at[p, 0],
                recv_sem=recv_sem.at[p, s],
                device_id=(d + p - 1, s),
                device_id_type=MESH,
            ).wait_recv()

    out_ref[...] = buf[...]


def _blk_gather_kernel(x_ref, out_ref, buf, send_sem, recv_sem):
    d, b = lax.axis_index("dom"), lax.axis_index("blk")
    nd, nb = lax.axis_size("dom"), lax.axis_size("blk")
    partners = [(0, m) for m in range(1, nb)]
    _barrier(partners, lambda i: (i >= 0) & (i < nd), d, b, nb)

    def outgoing(m):
        return pltpu.make_async_remote_copy(
            src_ref=x_ref,
            dst_ref=buf.at[b],
            send_sem=send_sem.at[m],
            recv_sem=recv_sem.at[b],
            device_id=(d, (b + m) % nb),
            device_id_type=MESH,
        )

    for _, m in partners:
        outgoing(m).start()
    buf[b] = x_ref[...]
    for _, m in partners:
        outgoing(m).wait_send()
    for _, m in partners:
        s = (b + m) % nb
        pltpu.make_async_remote_copy(
            src_ref=x_ref,
            dst_ref=buf.at[s],
            send_sem=send_sem.at[0],
            recv_sem=recv_sem.at[s],
            device_id=(d, s),
            device_id_type=MESH,
        ).wait_recv()
    out_ref[...] = buf[...]


def _node_reduce_kernel(x_ref, out_ref, buf, send_sem, recv_sem):
    d, b = lax.axis_index("dom"), lax.axis_index("blk")
    nd, nb = lax.axis_size("dom"), lax.axis_size("blk")
    partners = _halo_partners(nb)

    def in_range(i):
        return (i >= 0) & (i < nd)

    _barrier(partners, in_range, d, b, nb)

    def outgoing(delta, m):
        p = 1 + delta
        return pltpu.make_async_remote_copy(
            src_ref=x_ref.at[p, (b + m) % nb],
            dst_ref=buf.at[p, b],
            send_sem=send_sem.at[p, m],
            recv_sem=recv_sem.at[p, b],
            device_id=(d + delta, (b + m) % nb),
            device_id_type=MESH,
        )

    for delta, m in partners:
        pl.when(in_range(d + delta))(lambda delta=delta, m=m: outgoing(delta, m).start())
    out_ref[...] = x_ref[1, b]
    for delta, m in partners:
        pl.when(in_range(d + delta))(lambda delta=delta, m=m: outgoing(delta, m).wait_send())
    for delta, m in partners:
        p, s = 1 + delta, (b + m) % nb

        @pl.when(in_range(d - delta))
        def _(p=p, s=s):
            pltpu.make_async_remote_copy(
                src_ref=x_ref.at[p, s],
                dst_ref=buf.at[p, s],
                send_sem=send_sem.at[p, 0],
                recv_sem=recv_sem.at[p, s],
                device_id=(d - delta, s),
                device_id_type=MESH,
            ).wait_recv()
            out_ref[...] += buf[p, s]


def _exchange(kernel, x, out_shape, buf_shape, sem_shape, collective_id):
    return pl.pallas_call(
        kernel,
        out_shape=jax.ShapeDtypeStruct(out_shape, x.dtype),
        in_specs=[pl.BlockSpec(memory_space=pltpu.VMEM)],
        out_specs=pl.BlockSpec(memory_space=pltpu.VMEM),
        scratch_shapes=[
            pltpu.VMEM(buf_shape, x.dtype),
            pltpu.SemaphoreType.DMA(sem_shape),
            pltpu.SemaphoreType.DMA(sem_shape),
        ],
        compiler_params=pltpu.CompilerParams(
            collective_id=collective_id, has_side_effects=True
        ),
    )(x)


def halo_gather(x, nb, collective_id):
    shape = (3, nb) + x.shape
    out = _exchange(_halo_gather_kernel, x, shape, shape, (3, nb), collective_id)
    e, r, c = x.shape
    return jnp.transpose(out, (0, 2, 3, 1, 4)).reshape(3 * e, r, nb * c)


def blk_gather(x, nb, collective_id):
    shape = (nb,) + x.shape
    out = _exchange(_blk_gather_kernel, x, shape, shape, (nb,), collective_id)
    e, r, c = x.shape
    return jnp.transpose(out, (1, 2, 0, 3)).reshape(e, r, nb * c)


def node_reduce(chunks, collective_id):
    nb = chunks.shape[1]
    return _exchange(
        _node_reduce_kernel, chunks, chunks.shape[2:], chunks.shape, (3, nb), collective_id
    )


LANES = 128


def _sweeps_kernel(
    adj_ref, rs_ref, shift_ref, slot_ref, jac_hbm, inv_ref, out_ref,
    jac_v, send_a, halo, send_r, full_r, upd, jac_sem, hs_send, hs_recv, bk_send, bk_recv,
):
    d, b = lax.axis_index("dom"), lax.axis_index("blk")
    nd, nb = lax.axis_size("dom"), lax.axis_size("blk")
    rows = adj_ref.shape[0]
    elems = slot_ref.shape[0]
    faces = slot_ref.shape[1]
    partners = _halo_partners(nb)

    def in_range(i):
        return (i >= 0) & (i < nd)

    _barrier(partners, in_range, d, b, nb)
    jac_copy = pltpu.make_async_copy(jac_hbm, jac_v, jac_sem)
    jac_copy.start()
    lane = lax.broadcasted_iota(jnp.int32, (rows, LANES), 1)
    wide_lane = lax.broadcasted_iota(jnp.int32, (halo.shape[2], 2 * LANES), 1)
    own_rows = pl.ds(pl.multiple_of(b * rows, 16), rows)
    adjoint = adj_ref[...]
    for sweep in range(SWEEPS):
        send_a[sweep] = adjoint.astype(jnp.bfloat16)

        def halo_copy(delta, m, sweep=sweep):
            return pltpu.make_async_remote_copy(
                src_ref=send_a.at[sweep],
                dst_ref=halo.at[sweep, 1 - delta, own_rows],
                send_sem=hs_send.at[sweep, delta + 1, m],
                recv_sem=hs_recv.at[sweep, 1 - delta, b],
                device_id=(d + delta, (b + m) % nb),
                device_id_type=MESH,
            )

        for delta, m in partners:
            pl.when(in_range(d + delta))(lambda delta=delta, m=m: halo_copy(delta, m).start())
        halo[sweep, 1, own_rows] = send_a[sweep]
        for side in (-1, 1):
            @pl.when(jnp.logical_not(in_range(d + side)))
            def _(side=side, sweep=sweep):
                halo[sweep, 1 + side] = jnp.zeros(halo.shape[2:], halo.dtype)
        for delta, m in partners:
            pl.when(in_range(d + delta))(lambda delta=delta, m=m: halo_copy(delta, m).wait_send())
        for delta, m in partners:
            p, src_b = 1 + delta, (b + m) % nb

            @pl.when(in_range(d + delta))
            def _(p=p, src_b=src_b, sweep=sweep):
                pltpu.make_async_remote_copy(
                    src_ref=send_a.at[sweep],
                    dst_ref=halo.at[sweep, p, pl.ds(pl.multiple_of(src_b * rows, 16), rows)],
                    send_sem=hs_send.at[sweep, p, 0],
                    recv_sem=hs_recv.at[sweep, p, src_b],
                    device_id=(d + p - 1, src_b),
                    device_id_type=MESH,
                ).wait_recv()

        stride = elems * RHS
        combined = jnp.zeros((halo.shape[2], 2 * LANES), jnp.float32)
        for p in range(3):
            part = halo[sweep, p].astype(jnp.float32)
            part = jnp.concatenate([part, jnp.zeros_like(part)], axis=1)
            if p:
                part = pltpu.roll(part, p * stride, 1)
            combined = jnp.where(
                (wide_lane >= p * stride) & (wide_lane < (p + 1) * stride), part, combined
            )
        candidates = combined.astype(jnp.bfloat16)
        if sweep == 0:
            jac_copy.wait()

        def element(e, product, candidates=candidates):
            big = jnp.dot(jac_v[e], candidates, preferred_element_type=jnp.float32)
            acc = jnp.zeros((rows, 2 * LANES), jnp.float32)
            for k in range(faces + 1):
                slot = elems + e if k == 0 else slot_ref[e, k - 1]
                shift = (RHS * e - RHS * slot + 8 * LANES) % (2 * LANES)
                acc = acc + pltpu.roll(big[k * rows:(k + 1) * rows], shift, 1)
            mine = (lane >= RHS * e) & (lane < RHS * e + RHS)
            return product + jnp.where(mine, acc[:, :LANES], 0.0)

        product = lax.fori_loop(0, elems, element, jnp.zeros((rows, LANES), jnp.float32))
        image = shift_ref[...] * adjoint + product
        send_r[sweep] = (rs_ref[...] - image).astype(jnp.bfloat16)

        def blk_copy(m, sweep=sweep):
            return pltpu.make_async_remote_copy(
                src_ref=send_r.at[sweep],
                dst_ref=full_r.at[sweep, own_rows],
                send_sem=bk_send.at[sweep, m],
                recv_sem=bk_recv.at[sweep, b],
                device_id=(d, (b + m) % nb),
                device_id_type=MESH,
            )

        for m in range(1, nb):
            blk_copy(m).start()
        full_r[sweep, own_rows] = send_r[sweep]
        for m in range(1, nb):
            blk_copy(m).wait_send()
        for m in range(1, nb):
            src_b = (b + m) % nb
            pltpu.make_async_remote_copy(
                src_ref=send_r.at[sweep],
                dst_ref=full_r.at[sweep, pl.ds(pl.multiple_of(src_b * rows, 16), rows)],
                send_sem=bk_send.at[sweep, 0],
                recv_sem=bk_recv.at[sweep, src_b],
                device_id=(d, src_b),
                device_id_type=MESH,
            ).wait_recv()
        upd[...] = jnp.dot(
            inv_ref[...], full_r[sweep], preferred_element_type=jnp.float32
        ).reshape(upd.shape)
        update = jnp.zeros((rows, LANES), jnp.float32)
        for e in range(elems):
            mine = (lane >= RHS * e) & (lane < RHS * e + RHS)
            update = update + jnp.where(mine, upd[e], 0.0)
        adjoint = adjoint + update
    out_ref[...] = adjoint


def sweeps(adjoint_start, right_sides, pseudo_shift, slots, jac_blocks, block_inverse, nb):
    elems, rhs, rows = adjoint_start.shape
    cols = jac_blocks.shape[-1]
    faces = jac_blocks.shape[1]

    def transposed(x):
        x = jnp.transpose(x, (2, 0, 1)).reshape(rows, elems * rhs)
        return jnp.pad(x, ((0, 0), (0, LANES - elems * rhs)))

    shift = jnp.pad(jnp.repeat(pseudo_shift, rhs), (0, LANES - elems * rhs))[None, :]
    vmem = pl.BlockSpec(memory_space=pltpu.VMEM)
    out = pl.pallas_call(
        _sweeps_kernel,
        out_shape=jax.ShapeDtypeStruct((rows, LANES), jnp.float32),
        in_specs=[vmem, vmem, vmem, pl.BlockSpec(memory_space=pltpu.SMEM),
                  pl.BlockSpec(memory_space=pl.ANY), vmem],
        out_specs=vmem,
        scratch_shapes=[
            pltpu.VMEM((elems, faces * rows, cols), jnp.bfloat16),
            pltpu.VMEM((SWEEPS, rows, LANES), jnp.bfloat16),
            pltpu.VMEM((SWEEPS, 3, nb * rows, LANES), jnp.bfloat16),
            pltpu.VMEM((SWEEPS, rows, LANES), jnp.bfloat16),
            pltpu.VMEM((SWEEPS, nb * rows, LANES), jnp.bfloat16),
            pltpu.VMEM((elems, rows, LANES), jnp.float32),
            pltpu.SemaphoreType.DMA(()),
            pltpu.SemaphoreType.DMA((SWEEPS, 3, nb)),
            pltpu.SemaphoreType.DMA((SWEEPS, 3, nb)),
            pltpu.SemaphoreType.DMA((SWEEPS, nb)),
            pltpu.SemaphoreType.DMA((SWEEPS, nb)),
        ],
        compiler_params=pltpu.CompilerParams(
            collective_id=0, has_side_effects=True, vmem_limit_bytes=48 * 1024 * 1024
        ),
    )(
        transposed(adjoint_start),
        transposed(right_sides),
        shift,
        slots,
        jac_blocks.reshape(elems, faces * rows, cols),
        block_inverse.reshape(elems * rows, cols),
    )
    return jnp.transpose(out[:, : elems * rhs].reshape(rows, elems, rhs), (1, 2, 0))


def local(
    adjoint_start,
    right_sides,
    jac_blocks,
    block_inverse,
    neighbours,
    pseudo_shift,
    shape_partials,
    node_ids,
):
    local_count = neighbours.shape[0]
    nb = lax.axis_size("blk")
    part_index = lax.axis_index("dom")
    slots = neighbours - (part_index - 1) * local_count
    adjoint = sweeps(adjoint_start, right_sides, pseudo_shift, slots, jac_blocks, block_inverse, nb)
    final_half = adjoint.astype(jnp.bfloat16)
    weighted = -jnp.einsum(
        "ejr,erq->ejq", final_half, shape_partials, preferred_element_type=jnp.float32
    )
    node_width = node_ids.shape[1]
    weighted = weighted.reshape(local_count, RHS, node_width, 3)
    values = jnp.transpose(weighted, (0, 2, 1, 3)).reshape(local_count * node_width, RHS * 3)
    node_slots = (node_ids - (part_index - 1) * NODE_DEV).reshape(-1)
    partial_sums = jax.ops.segment_sum(values, node_slots, 3 * NODE_DEV).T
    chunks = jnp.transpose(
        partial_sums.reshape(RHS * 3, 3, nb, NODE_DEV // nb), (1, 2, 0, 3)
    )
    shape_gradient = node_reduce(chunks, collective_id=1)
    return (adjoint, shape_gradient)


def solution(mesh):
    in_specs = (
        P("dom", None, "blk"),
        P("dom", None, "blk"),
        P("dom", None, "blk", None),
        P("dom", "blk", None),
        P("dom", None),
        P("dom"),
        P("dom", "blk", None),
        P("dom", None),
    )
    out_specs = (P("dom", None, "blk"), P(None, ("dom", "blk")))
    return jax.shard_map(local, mesh=mesh, in_specs=in_specs, out_specs=out_specs, check_vma=False)
```

```python
import functools

import jax
import jax.numpy as jnp
from jax import lax
from jax.experimental import pallas as pl
from jax.experimental.pallas import tpu as pltpu
from jax.sharding import PartitionSpec as P

RHS = 3
SWEEPS = 2
NODE_DEV = 768
MESH = pl.DeviceIdType.MESH


def _halo_partners(nb):
    return [(delta, m) for delta in (-1, 0, 1) for m in range(nb) if (delta, m) != (0, 0)]


def _barrier(partners, in_range, d, b, nb):
    barrier = pltpu.get_barrier_semaphore()
    for delta, m in partners:
        @pl.when(in_range(d + delta))
        def _(delta=delta, m=m):
            pl.semaphore_signal(
                barrier, 1, device_id=(d + delta, (b + m) % nb), device_id_type=MESH
            )
    nd = lax.axis_size("dom")
    has_lower = (d + nd - 1) // nd
    has_upper = (2 * nd - 2 - d) // nd
    peers = [sum(1 for delta, _ in partners if delta == side) for side in (-1, 0, 1)]
    pl.semaphore_wait(barrier, peers[1] + peers[0] * has_lower + peers[2] * has_upper)


def _halo_gather_kernel(x_ref, out_ref, buf, send_sem, recv_sem):
    d, b = lax.axis_index("dom"), lax.axis_index("blk")
    nd, nb = lax.axis_size("dom"), lax.axis_size("blk")
    partners = _halo_partners(nb)

    def in_range(i):
        return (i >= 0) & (i < nd)

    _barrier(partners, in_range, d, b, nb)

    def outgoing(delta, m):
        return pltpu.make_async_remote_copy(
            src_ref=x_ref,
            dst_ref=buf.at[1 - delta, b],
            send_sem=send_sem.at[delta + 1, m],
            recv_sem=recv_sem.at[1 - delta, b],
            device_id=(d + delta, (b + m) % nb),
            device_id_type=MESH,
        )

    for delta, m in partners:
        pl.when(in_range(d + delta))(lambda delta=delta, m=m: outgoing(delta, m).start())
    buf[1, b] = x_ref[...]
    for side in (-1, 1):
        @pl.when(jnp.logical_not(in_range(d + side)))
        def _(side=side):
            buf[1 + side] = jnp.zeros(buf.shape[1:], buf.dtype)
    for delta, m in partners:
        pl.when(in_range(d + delta))(lambda delta=delta, m=m: outgoing(delta, m).wait_send())
    for delta, m in partners:
        p, s = 1 + delta, (b + m) % nb

        @pl.when(in_range(d + delta))
        def _(p=p, s=s):
            pltpu.make_async_remote_copy(
                src_ref=x_ref,
                dst_ref=buf.at[p, s],
                send_sem=send_sem.at[p, 0],
                recv_sem=recv_sem.at[p, s],
                device_id=(d + p - 1, s),
                device_id_type=MESH,
            ).wait_recv()

    out_ref[...] = buf[...]


def _blk_gather_kernel(x_ref, out_ref, buf, send_sem, recv_sem):
    d, b = lax.axis_index("dom"), lax.axis_index("blk")
    nd, nb = lax.axis_size("dom"), lax.axis_size("blk")
    partners = [(0, m) for m in range(1, nb)]
    _barrier(partners, lambda i: (i >= 0) & (i < nd), d, b, nb)

    def outgoing(m):
        return pltpu.make_async_remote_copy(
            src_ref=x_ref,
            dst_ref=buf.at[b],
            send_sem=send_sem.at[m],
            recv_sem=recv_sem.at[b],
            device_id=(d, (b + m) % nb),
            device_id_type=MESH,
        )

    for _, m in partners:
        outgoing(m).start()
    buf[b] = x_ref[...]
    for _, m in partners:
        outgoing(m).wait_send()
    for _, m in partners:
        s = (b + m) % nb
        pltpu.make_async_remote_copy(
            src_ref=x_ref,
            dst_ref=buf.at[s],
            send_sem=send_sem.at[0],
            recv_sem=recv_sem.at[s],
            device_id=(d, s),
            device_id_type=MESH,
        ).wait_recv()
    out_ref[...] = buf[...]


def _node_reduce_kernel(x_ref, out_ref, buf, send_sem, recv_sem):
    d, b = lax.axis_index("dom"), lax.axis_index("blk")
    nd, nb = lax.axis_size("dom"), lax.axis_size("blk")
    partners = _halo_partners(nb)

    def in_range(i):
        return (i >= 0) & (i < nd)

    _barrier(partners, in_range, d, b, nb)

    def outgoing(delta, m):
        p = 1 + delta
        return pltpu.make_async_remote_copy(
            src_ref=x_ref.at[p, (b + m) % nb],
            dst_ref=buf.at[p, b],
            send_sem=send_sem.at[p, m],
            recv_sem=recv_sem.at[p, b],
            device_id=(d + delta, (b + m) % nb),
            device_id_type=MESH,
        )

    for delta, m in partners:
        pl.when(in_range(d + delta))(lambda delta=delta, m=m: outgoing(delta, m).start())
    out_ref[...] = x_ref[1, b]
    for delta, m in partners:
        pl.when(in_range(d + delta))(lambda delta=delta, m=m: outgoing(delta, m).wait_send())
    for delta, m in partners:
        p, s = 1 + delta, (b + m) % nb

        @pl.when(in_range(d - delta))
        def _(p=p, s=s):
            pltpu.make_async_remote_copy(
                src_ref=x_ref.at[p, s],
                dst_ref=buf.at[p, s],
                send_sem=send_sem.at[p, 0],
                recv_sem=recv_sem.at[p, s],
                device_id=(d - delta, s),
                device_id_type=MESH,
            ).wait_recv()
            out_ref[...] += buf[p, s]


def _exchange(kernel, x, out_shape, buf_shape, sem_shape, collective_id):
    return pl.pallas_call(
        kernel,
        out_shape=jax.ShapeDtypeStruct(out_shape, x.dtype),
        in_specs=[pl.BlockSpec(memory_space=pltpu.VMEM)],
        out_specs=pl.BlockSpec(memory_space=pltpu.VMEM),
        scratch_shapes=[
            pltpu.VMEM(buf_shape, x.dtype),
            pltpu.SemaphoreType.DMA(sem_shape),
            pltpu.SemaphoreType.DMA(sem_shape),
        ],
        compiler_params=pltpu.CompilerParams(
            collective_id=collective_id, has_side_effects=True
        ),
    )(x)


def halo_gather(x, nb, collective_id):
    shape = (3, nb) + x.shape
    out = _exchange(_halo_gather_kernel, x, shape, shape, (3, nb), collective_id)
    e, r, c = x.shape
    return jnp.transpose(out, (0, 2, 3, 1, 4)).reshape(3 * e, r, nb * c)


def blk_gather(x, nb, collective_id):
    shape = (nb,) + x.shape
    out = _exchange(_blk_gather_kernel, x, shape, shape, (nb,), collective_id)
    e, r, c = x.shape
    return jnp.transpose(out, (1, 2, 0, 3)).reshape(e, r, nb * c)


def node_reduce(chunks, collective_id):
    nb = chunks.shape[1]
    return _exchange(
        _node_reduce_kernel, chunks, chunks.shape[2:], chunks.shape, (3, nb), collective_id
    )


LANES = 128


def _sweeps_kernel(
    adj_ref, rs_ref, shift_ref, slot_ref, jac_hbm, inv_ref, out_ref,
    jac_v, send_a, halo, send_r, full_r, upd, jac_sem, hs_send, hs_recv, bk_send, bk_recv,
    fw_send,
):
    d, b = lax.axis_index("dom"), lax.axis_index("blk")
    nd, nb = lax.axis_size("dom"), lax.axis_size("blk")
    rows = adj_ref.shape[0]
    elems = slot_ref.shape[0]
    faces = slot_ref.shape[1]

    def in_range(i):
        return (i >= 0) & (i < nd)

    partners = [(0, m) for m in range(1, nb)] + [(-1, 0), (1, 0)]
    _barrier(partners, in_range, d, b, nb)
    jac_copy = pltpu.make_async_copy(jac_hbm, jac_v, jac_sem)
    jac_copy.start()
    lane = lax.broadcasted_iota(jnp.int32, (rows, LANES), 1)
    wide_lane = lax.broadcasted_iota(jnp.int32, (halo.shape[2], 2 * LANES), 1)

    def row_block(i):
        return pl.ds(pl.multiple_of(i * rows, 16), rows)

    own_rows = row_block(b)
    adjoint = adj_ref[...]
    for sweep in range(SWEEPS):
        send_a[sweep] = adjoint.astype(jnp.bfloat16)

        def direct(delta, m, sweep=sweep):
            return pltpu.make_async_remote_copy(
                src_ref=send_a.at[sweep],
                dst_ref=halo.at[sweep, 1 - delta, own_rows],
                send_sem=hs_send.at[sweep, delta + 1, m],
                recv_sem=hs_recv.at[sweep, 1 - delta, b],
                device_id=(d + delta, (b + m) % nb),
                device_id_type=MESH,
            )

        def forward(p, m, sweep=sweep):
            return pltpu.make_async_remote_copy(
                src_ref=halo.at[sweep, p, own_rows],
                dst_ref=halo.at[sweep, p, own_rows],
                send_sem=fw_send.at[sweep, p // 2, m],
                recv_sem=hs_recv.at[sweep, p, b],
                device_id=(d, (b + m) % nb),
                device_id_type=MESH,
            )

        def arrival(p, src_b, sweep=sweep):
            return pltpu.make_async_remote_copy(
                src_ref=send_a.at[sweep],
                dst_ref=halo.at[sweep, p, row_block(src_b)],
                send_sem=hs_send.at[sweep, p, 0],
                recv_sem=hs_recv.at[sweep, p, src_b],
                device_id=(d, src_b),
                device_id_type=MESH,
            )

        for delta, m in partners:
            pl.when(in_range(d + delta))(lambda delta=delta, m=m: direct(delta, m).start())
        halo[sweep, 1, own_rows] = send_a[sweep]
        for side in (-1, 1):
            @pl.when(jnp.logical_not(in_range(d + side)))
            def _(side=side, sweep=sweep):
                halo[sweep, 1 + side] = jnp.zeros(halo.shape[2:], halo.dtype)
        for side in (-1, 1):
            p = 1 + side

            @pl.when(in_range(d + side))
            def _(p=p):
                arrival(p, b).wait_recv()
                for m in range(1, nb):
                    forward(p, m).start()
        for delta, m in partners:
            pl.when(in_range(d + delta))(lambda delta=delta, m=m: direct(delta, m).wait_send())
        for m in range(1, nb):
            arrival(1, (b + m) % nb).wait_recv()
        for side in (-1, 1):
            p = 1 + side

            @pl.when(in_range(d + side))
            def _(p=p):
                for m in range(1, nb):
                    forward(p, m).wait_send()
                for m in range(1, nb):
                    arrival(p, (b + m) % nb).wait_recv()

        stride = elems * RHS
        combined = jnp.zeros((halo.shape[2], 2 * LANES), jnp.float32)
        for p in range(3):
            part = halo[sweep, p].astype(jnp.float32)
            part = jnp.concatenate([part, jnp.zeros_like(part)], axis=1)
            if p:
                part = pltpu.roll(part, p * stride, 1)
            combined = jnp.where(
                (wide_lane >= p * stride) & (wide_lane < (p + 1) * stride), part, combined
            )
        candidates = combined.astype(jnp.bfloat16)
        if sweep == 0:
            jac_copy.wait()

        def element(e, product, candidates=candidates):
            big = jnp.dot(jac_v[e], candidates, preferred_element_type=jnp.float32)
            acc = jnp.zeros((rows, 2 * LANES), jnp.float32)
            for k in range(faces + 1):
                slot = elems + e if k == 0 else slot_ref[e, k - 1]
                shift = (RHS * e - RHS * slot + 8 * LANES) % (2 * LANES)
                acc = acc + pltpu.roll(big[k * rows:(k + 1) * rows], shift, 1)
            mine = (lane >= RHS * e) & (lane < RHS * e + RHS)
            return product + jnp.where(mine, acc[:, :LANES], 0.0)

        product = lax.fori_loop(0, elems, element, jnp.zeros((rows, LANES), jnp.float32))
        image = shift_ref[...] * adjoint + product
        send_r[sweep] = (rs_ref[...] - image).astype(jnp.bfloat16)

        def blk_copy(m, sweep=sweep):
            return pltpu.make_async_remote_copy(
                src_ref=send_r.at[sweep],
                dst_ref=full_r.at[sweep, own_rows],
                send_sem=bk_send.at[sweep, m],
                recv_sem=bk_recv.at[sweep, b],
                device_id=(d, (b + m) % nb),
                device_id_type=MESH,
            )

        for m in range(1, nb):
            blk_copy(m).start()
        full_r[sweep, own_rows] = send_r[sweep]
        for m in range(1, nb):
            blk_copy(m).wait_send()
        for m in range(1, nb):
            src_b = (b + m) % nb
            pltpu.make_async_remote_copy(
                src_ref=send_r.at[sweep],
                dst_ref=full_r.at[sweep, pl.ds(pl.multiple_of(src_b * rows, 16), rows)],
                send_sem=bk_send.at[sweep, 0],
                recv_sem=bk_recv.at[sweep, src_b],
                device_id=(d, src_b),
                device_id_type=MESH,
            ).wait_recv()
        upd[...] = jnp.dot(
            inv_ref[...], full_r[sweep], preferred_element_type=jnp.float32
        ).reshape(upd.shape)
        update = jnp.zeros((rows, LANES), jnp.float32)
        for e in range(elems):
            mine = (lane >= RHS * e) & (lane < RHS * e + RHS)
            update = update + jnp.where(mine, upd[e], 0.0)
        adjoint = adjoint + update
    out_ref[...] = adjoint


def sweeps(adjoint_start, right_sides, pseudo_shift, slots, jac_blocks, block_inverse, nb):
    elems, rhs, rows = adjoint_start.shape
    cols = jac_blocks.shape[-1]
    faces = jac_blocks.shape[1]

    def transposed(x):
        x = jnp.transpose(x, (2, 0, 1)).reshape(rows, elems * rhs)
        return jnp.pad(x, ((0, 0), (0, LANES - elems * rhs)))

    shift = jnp.pad(jnp.repeat(pseudo_shift, rhs), (0, LANES - elems * rhs))[None, :]
    vmem = pl.BlockSpec(memory_space=pltpu.VMEM)
    out = pl.pallas_call(
        _sweeps_kernel,
        out_shape=jax.ShapeDtypeStruct((rows, LANES), jnp.float32),
        in_specs=[vmem, vmem, vmem, pl.BlockSpec(memory_space=pltpu.SMEM),
                  pl.BlockSpec(memory_space=pl.ANY), vmem],
        out_specs=vmem,
        scratch_shapes=[
            pltpu.VMEM((elems, faces * rows, cols), jnp.bfloat16),
            pltpu.VMEM((SWEEPS, rows, LANES), jnp.bfloat16),
            pltpu.VMEM((SWEEPS, 3, nb * rows, LANES), jnp.bfloat16),
            pltpu.VMEM((SWEEPS, rows, LANES), jnp.bfloat16),
            pltpu.VMEM((SWEEPS, nb * rows, LANES), jnp.bfloat16),
            pltpu.VMEM((elems, rows, LANES), jnp.float32),
            pltpu.SemaphoreType.DMA(()),
            pltpu.SemaphoreType.DMA((SWEEPS, 3, nb)),
            pltpu.SemaphoreType.DMA((SWEEPS, 3, nb)),
            pltpu.SemaphoreType.DMA((SWEEPS, nb)),
            pltpu.SemaphoreType.DMA((SWEEPS, nb)),
            pltpu.SemaphoreType.DMA((SWEEPS, 2, nb)),
        ],
        compiler_params=pltpu.CompilerParams(
            collective_id=0, has_side_effects=True, vmem_limit_bytes=48 * 1024 * 1024
        ),
    )(
        transposed(adjoint_start),
        transposed(right_sides),
        shift,
        slots,
        jac_blocks.reshape(elems, faces * rows, cols),
        block_inverse.reshape(elems * rows, cols),
    )
    return jnp.transpose(out[:, : elems * rhs].reshape(rows, elems, rhs), (1, 2, 0))


def local(
    adjoint_start,
    right_sides,
    jac_blocks,
    block_inverse,
    neighbours,
    pseudo_shift,
    shape_partials,
    node_ids,
):
    local_count = neighbours.shape[0]
    nb = lax.axis_size("blk")
    part_index = lax.axis_index("dom")
    slots = neighbours - (part_index - 1) * local_count
    adjoint = sweeps(adjoint_start, right_sides, pseudo_shift, slots, jac_blocks, block_inverse, nb)
    final_half = adjoint.astype(jnp.bfloat16)
    weighted = -jnp.einsum(
        "ejr,erq->ejq", final_half, shape_partials, preferred_element_type=jnp.float32
    )
    node_width = node_ids.shape[1]
    weighted = weighted.reshape(local_count, RHS, node_width, 3)
    values = jnp.transpose(weighted, (0, 2, 1, 3)).reshape(local_count * node_width, RHS * 3)
    node_slots = (node_ids - (part_index - 1) * NODE_DEV).reshape(-1)
    partial_sums = jax.ops.segment_sum(values, node_slots, 3 * NODE_DEV).T
    chunks = jnp.transpose(
        partial_sums.reshape(RHS * 3, 3, nb, NODE_DEV // nb), (1, 2, 0, 3)
    )
    shape_gradient = node_reduce(chunks, collective_id=1)
    return (adjoint, shape_gradient)


def solution(mesh):
    in_specs = (
        P("dom", None, "blk"),
        P("dom", None, "blk"),
        P("dom", None, "blk", None),
        P("dom", "blk", None),
        P("dom", None),
        P("dom"),
        P("dom", "blk", None),
        P("dom", None),
    )
    out_specs = (P("dom", None, "blk"), P(None, ("dom", "blk")))
    return jax.shard_map(local, mesh=mesh, in_specs=in_specs, out_specs=out_specs, check_vma=False)
```

```python
import functools

import jax
import jax.numpy as jnp
from jax import lax
from jax.experimental import pallas as pl
from jax.experimental.pallas import tpu as pltpu
from jax.sharding import PartitionSpec as P

RHS = 3
SWEEPS = 2
NODE_DEV = 768
MESH = pl.DeviceIdType.MESH


def _halo_partners(nb):
    return [(delta, m) for delta in (-1, 0, 1) for m in range(nb) if (delta, m) != (0, 0)]


def _barrier(partners, in_range, d, b, nb):
    barrier = pltpu.get_barrier_semaphore()
    for delta, m in partners:
        @pl.when(in_range(d + delta))
        def _(delta=delta, m=m):
            pl.semaphore_signal(
                barrier, 1, device_id=(d + delta, (b + m) % nb), device_id_type=MESH
            )
    nd = lax.axis_size("dom")
    has_lower = (d + nd - 1) // nd
    has_upper = (2 * nd - 2 - d) // nd
    peers = [sum(1 for delta, _ in partners if delta == side) for side in (-1, 0, 1)]
    pl.semaphore_wait(barrier, peers[1] + peers[0] * has_lower + peers[2] * has_upper)


def _halo_gather_kernel(x_ref, out_ref, buf, send_sem, recv_sem):
    d, b = lax.axis_index("dom"), lax.axis_index("blk")
    nd, nb = lax.axis_size("dom"), lax.axis_size("blk")
    partners = _halo_partners(nb)

    def in_range(i):
        return (i >= 0) & (i < nd)

    _barrier(partners, in_range, d, b, nb)

    def outgoing(delta, m):
        return pltpu.make_async_remote_copy(
            src_ref=x_ref,
            dst_ref=buf.at[1 - delta, b],
            send_sem=send_sem.at[delta + 1, m],
            recv_sem=recv_sem.at[1 - delta, b],
            device_id=(d + delta, (b + m) % nb),
            device_id_type=MESH,
        )

    for delta, m in partners:
        pl.when(in_range(d + delta))(lambda delta=delta, m=m: outgoing(delta, m).start())
    buf[1, b] = x_ref[...]
    for side in (-1, 1):
        @pl.when(jnp.logical_not(in_range(d + side)))
        def _(side=side):
            buf[1 + side] = jnp.zeros(buf.shape[1:], buf.dtype)
    for delta, m in partners:
        pl.when(in_range(d + delta))(lambda delta=delta, m=m: outgoing(delta, m).wait_send())
    for delta, m in partners:
        p, s = 1 + delta, (b + m) % nb

        @pl.when(in_range(d + delta))
        def _(p=p, s=s):
            pltpu.make_async_remote_copy(
                src_ref=x_ref,
                dst_ref=buf.at[p, s],
                send_sem=send_sem.at[p, 0],
                recv_sem=recv_sem.at[p, s],
                device_id=(d + p - 1, s),
                device_id_type=MESH,
            ).wait_recv()

    out_ref[...] = buf[...]


def _blk_gather_kernel(x_ref, out_ref, buf, send_sem, recv_sem):
    d, b = lax.axis_index("dom"), lax.axis_index("blk")
    nd, nb = lax.axis_size("dom"), lax.axis_size("blk")
    partners = [(0, m) for m in range(1, nb)]
    _barrier(partners, lambda i: (i >= 0) & (i < nd), d, b, nb)

    def outgoing(m):
        return pltpu.make_async_remote_copy(
            src_ref=x_ref,
            dst_ref=buf.at[b],
            send_sem=send_sem.at[m],
            recv_sem=recv_sem.at[b],
            device_id=(d, (b + m) % nb),
            device_id_type=MESH,
        )

    for _, m in partners:
        outgoing(m).start()
    buf[b] = x_ref[...]
    for _, m in partners:
        outgoing(m).wait_send()
    for _, m in partners:
        s = (b + m) % nb
        pltpu.make_async_remote_copy(
            src_ref=x_ref,
            dst_ref=buf.at[s],
            send_sem=send_sem.at[0],
            recv_sem=recv_sem.at[s],
            device_id=(d, s),
            device_id_type=MESH,
        ).wait_recv()
    out_ref[...] = buf[...]


def _node_reduce_kernel(x_ref, out_ref, buf, send_sem, recv_sem):
    d, b = lax.axis_index("dom"), lax.axis_index("blk")
    nd, nb = lax.axis_size("dom"), lax.axis_size("blk")
    partners = _halo_partners(nb)

    def in_range(i):
        return (i >= 0) & (i < nd)

    _barrier(partners, in_range, d, b, nb)

    def outgoing(delta, m):
        p = 1 + delta
        return pltpu.make_async_remote_copy(
            src_ref=x_ref.at[p, (b + m) % nb],
            dst_ref=buf.at[p, b],
            send_sem=send_sem.at[p, m],
            recv_sem=recv_sem.at[p, b],
            device_id=(d + delta, (b + m) % nb),
            device_id_type=MESH,
        )

    for delta, m in partners:
        pl.when(in_range(d + delta))(lambda delta=delta, m=m: outgoing(delta, m).start())
    out_ref[...] = x_ref[1, b]
    for delta, m in partners:
        pl.when(in_range(d + delta))(lambda delta=delta, m=m: outgoing(delta, m).wait_send())
    for delta, m in partners:
        p, s = 1 + delta, (b + m) % nb

        @pl.when(in_range(d - delta))
        def _(p=p, s=s):
            pltpu.make_async_remote_copy(
                src_ref=x_ref.at[p, s],
                dst_ref=buf.at[p, s],
                send_sem=send_sem.at[p, 0],
                recv_sem=recv_sem.at[p, s],
                device_id=(d - delta, s),
                device_id_type=MESH,
            ).wait_recv()
            out_ref[...] += buf[p, s]


def _exchange(kernel, x, out_shape, buf_shape, sem_shape, collective_id):
    return pl.pallas_call(
        kernel,
        out_shape=jax.ShapeDtypeStruct(out_shape, x.dtype),
        in_specs=[pl.BlockSpec(memory_space=pltpu.VMEM)],
        out_specs=pl.BlockSpec(memory_space=pltpu.VMEM),
        scratch_shapes=[
            pltpu.VMEM(buf_shape, x.dtype),
            pltpu.SemaphoreType.DMA(sem_shape),
            pltpu.SemaphoreType.DMA(sem_shape),
        ],
        compiler_params=pltpu.CompilerParams(
            collective_id=collective_id, has_side_effects=True
        ),
    )(x)


def halo_gather(x, nb, collective_id):
    shape = (3, nb) + x.shape
    out = _exchange(_halo_gather_kernel, x, shape, shape, (3, nb), collective_id)
    e, r, c = x.shape
    return jnp.transpose(out, (0, 2, 3, 1, 4)).reshape(3 * e, r, nb * c)


def blk_gather(x, nb, collective_id):
    shape = (nb,) + x.shape
    out = _exchange(_blk_gather_kernel, x, shape, shape, (nb,), collective_id)
    e, r, c = x.shape
    return jnp.transpose(out, (1, 2, 0, 3)).reshape(e, r, nb * c)


def node_reduce(chunks, collective_id):
    nb = chunks.shape[1]
    return _exchange(
        _node_reduce_kernel, chunks, chunks.shape[2:], chunks.shape, (3, nb), collective_id
    )


LANES = 128


def _sweeps_kernel(
    adj_ref, rs_ref, shift_ref, target_ref, jac_hbm, inv_ref, out_ref,
    jac_v, select, send_a, halo, send_r, full_r, upd, jac_sem, hs_send, hs_recv, bk_send, bk_recv,
    fw_send,
):
    d, b = lax.axis_index("dom"), lax.axis_index("blk")
    nd, nb = lax.axis_size("dom"), lax.axis_size("blk")
    rows = adj_ref.shape[0]
    elems = jac_v.shape[0]
    faces = jac_v.shape[1]

    def in_range(i):
        return (i >= 0) & (i < nd)

    partners = [(0, m) for m in range(1, nb)] + [(-1, 0), (1, 0)]
    _barrier(partners, in_range, d, b, nb)
    jac_copy = pltpu.make_async_copy(jac_hbm, jac_v, jac_sem)
    jac_copy.start()
    lane = lax.broadcasted_iota(jnp.int32, (rows, LANES), 1)
    cand_row = lax.broadcasted_iota(jnp.int32, (3 * LANES, LANES), 0)
    for k in range(faces):
        select[k] = (cand_row == target_ref[pl.ds(k, 1), :]).astype(jnp.bfloat16)

    def row_block(i):
        return pl.ds(pl.multiple_of(i * rows, 16), rows)

    own_rows = row_block(b)
    adjoint = adj_ref[...]
    for sweep in range(SWEEPS):
        send_a[sweep] = adjoint.astype(jnp.bfloat16)

        def direct(delta, m, sweep=sweep):
            return pltpu.make_async_remote_copy(
                src_ref=send_a.at[sweep],
                dst_ref=halo.at[sweep, 1 - delta, own_rows],
                send_sem=hs_send.at[sweep, delta + 1, m],
                recv_sem=hs_recv.at[sweep, 1 - delta, b],
                device_id=(d + delta, (b + m) % nb),
                device_id_type=MESH,
            )

        def forward(p, m, sweep=sweep):
            return pltpu.make_async_remote_copy(
                src_ref=halo.at[sweep, p, own_rows],
                dst_ref=halo.at[sweep, p, own_rows],
                send_sem=fw_send.at[sweep, p // 2, m],
                recv_sem=hs_recv.at[sweep, p, b],
                device_id=(d, (b + m) % nb),
                device_id_type=MESH,
            )

        def arrival(p, src_b, sweep=sweep):
            return pltpu.make_async_remote_copy(
                src_ref=send_a.at[sweep],
                dst_ref=halo.at[sweep, p, row_block(src_b)],
                send_sem=hs_send.at[sweep, p, 0],
                recv_sem=hs_recv.at[sweep, p, src_b],
                device_id=(d, src_b),
                device_id_type=MESH,
            )

        for delta, m in partners:
            pl.when(in_range(d + delta))(lambda delta=delta, m=m: direct(delta, m).start())
        halo[sweep, 1, own_rows] = send_a[sweep]
        for side in (-1, 1):
            @pl.when(jnp.logical_not(in_range(d + side)))
            def _(side=side, sweep=sweep):
                halo[sweep, 1 + side] = jnp.zeros(halo.shape[2:], halo.dtype)
        for side in (-1, 1):
            p = 1 + side

            @pl.when(in_range(d + side))
            def _(p=p):
                arrival(p, b).wait_recv()
                for m in range(1, nb):
                    forward(p, m).start()
        for delta, m in partners:
            pl.when(in_range(d + delta))(lambda delta=delta, m=m: direct(delta, m).wait_send())
        for m in range(1, nb):
            arrival(1, (b + m) % nb).wait_recv()
        for side in (-1, 1):
            p = 1 + side

            @pl.when(in_range(d + side))
            def _(p=p):
                for m in range(1, nb):
                    forward(p, m).wait_send()
                for m in range(1, nb):
                    arrival(p, (b + m) % nb).wait_recv()

        candidates = jnp.concatenate([halo[sweep, p] for p in range(3)], axis=1)
        if sweep == 0:
            jac_copy.wait()
        acc = jnp.zeros((elems * rows, LANES), jnp.float32)
        for k in range(faces):
            picked = jnp.dot(candidates, select[k], preferred_element_type=jnp.float32)
            acc = acc + jnp.dot(
                jac_v[:, k].reshape(elems * rows, -1),
                picked.astype(jnp.bfloat16),
                preferred_element_type=jnp.float32,
            )
        upd[...] = acc.reshape(upd.shape)
        product = jnp.zeros((rows, LANES), jnp.float32)
        for e in range(elems):
            mine = (lane >= RHS * e) & (lane < RHS * e + RHS)
            product = product + jnp.where(mine, upd[e], 0.0)
        image = shift_ref[...] * adjoint + product
        send_r[sweep] = (rs_ref[...] - image).astype(jnp.bfloat16)

        def blk_copy(m, sweep=sweep):
            return pltpu.make_async_remote_copy(
                src_ref=send_r.at[sweep],
                dst_ref=full_r.at[sweep, own_rows],
                send_sem=bk_send.at[sweep, m],
                recv_sem=bk_recv.at[sweep, b],
                device_id=(d, (b + m) % nb),
                device_id_type=MESH,
            )

        for m in range(1, nb):
            blk_copy(m).start()
        full_r[sweep, own_rows] = send_r[sweep]
        for m in range(1, nb):
            blk_copy(m).wait_send()
        for m in range(1, nb):
            src_b = (b + m) % nb
            pltpu.make_async_remote_copy(
                src_ref=send_r.at[sweep],
                dst_ref=full_r.at[sweep, pl.ds(pl.multiple_of(src_b * rows, 16), rows)],
                send_sem=bk_send.at[sweep, 0],
                recv_sem=bk_recv.at[sweep, src_b],
                device_id=(d, src_b),
                device_id_type=MESH,
            ).wait_recv()
        upd[...] = jnp.dot(
            inv_ref[...], full_r[sweep], preferred_element_type=jnp.float32
        ).reshape(upd.shape)
        update = jnp.zeros((rows, LANES), jnp.float32)
        for e in range(elems):
            mine = (lane >= RHS * e) & (lane < RHS * e + RHS)
            update = update + jnp.where(mine, upd[e], 0.0)
        adjoint = adjoint + update
    out_ref[...] = adjoint


def sweeps(adjoint_start, right_sides, pseudo_shift, slots, jac_blocks, block_inverse, nb):
    elems, rhs, rows = adjoint_start.shape
    cols = jac_blocks.shape[-1]
    faces = jac_blocks.shape[1]

    def transposed(x):
        x = jnp.transpose(x, (2, 0, 1)).reshape(rows, elems * rhs)
        return jnp.pad(x, ((0, 0), (0, LANES - elems * rhs)))

    shift = jnp.pad(jnp.repeat(pseudo_shift, rhs), (0, LANES - elems * rhs))[None, :]
    part, within = slots // elems, slots % elems
    lanes = (part * LANES + within * rhs)[:, :, None] + jnp.arange(rhs, dtype=jnp.int32)
    target = jnp.transpose(lanes, (1, 0, 2)).reshape(faces, elems * rhs)
    target = jnp.pad(target, ((0, 8 - faces), (0, LANES - elems * rhs)), constant_values=-1)
    vmem = pl.BlockSpec(memory_space=pltpu.VMEM)
    out = pl.pallas_call(
        _sweeps_kernel,
        out_shape=jax.ShapeDtypeStruct((rows, LANES), jnp.float32),
        in_specs=[vmem, vmem, vmem, vmem, pl.BlockSpec(memory_space=pl.ANY), vmem],
        out_specs=vmem,
        scratch_shapes=[
            pltpu.VMEM((elems, faces, rows, cols), jnp.bfloat16),
            pltpu.VMEM((faces, 3 * LANES, LANES), jnp.bfloat16),
            pltpu.VMEM((SWEEPS, rows, LANES), jnp.bfloat16),
            pltpu.VMEM((SWEEPS, 3, nb * rows, LANES), jnp.bfloat16),
            pltpu.VMEM((SWEEPS, rows, LANES), jnp.bfloat16),
            pltpu.VMEM((SWEEPS, nb * rows, LANES), jnp.bfloat16),
            pltpu.VMEM((elems, rows, LANES), jnp.float32),
            pltpu.SemaphoreType.DMA(()),
            pltpu.SemaphoreType.DMA((SWEEPS, 3, nb)),
            pltpu.SemaphoreType.DMA((SWEEPS, 3, nb)),
            pltpu.SemaphoreType.DMA((SWEEPS, nb)),
            pltpu.SemaphoreType.DMA((SWEEPS, nb)),
            pltpu.SemaphoreType.DMA((SWEEPS, 2, nb)),
        ],
        compiler_params=pltpu.CompilerParams(
            collective_id=0, has_side_effects=True, vmem_limit_bytes=48 * 1024 * 1024
        ),
    )(
        transposed(adjoint_start),
        transposed(right_sides),
        shift,
        target,
        jac_blocks,
        block_inverse.reshape(elems * rows, cols),
    )
    return jnp.transpose(out[:, : elems * rhs].reshape(rows, elems, rhs), (1, 2, 0))


def local(
    adjoint_start,
    right_sides,
    jac_blocks,
    block_inverse,
    neighbours,
    pseudo_shift,
    shape_partials,
    node_ids,
):
    local_count = neighbours.shape[0]
    nb = lax.axis_size("blk")
    part_index = lax.axis_index("dom")
    own = jnp.arange(local_count, dtype=jnp.int32)[:, None] + local_count
    slots = jnp.concatenate([own, neighbours - (part_index - 1) * local_count], axis=1)
    adjoint = sweeps(adjoint_start, right_sides, pseudo_shift, slots, jac_blocks, block_inverse, nb)
    final_half = adjoint.astype(jnp.bfloat16)
    weighted = -jnp.einsum(
        "ejr,erq->ejq", final_half, shape_partials, preferred_element_type=jnp.float32
    )
    node_width = node_ids.shape[1]
    weighted = weighted.reshape(local_count, RHS, node_width, 3)
    values = jnp.transpose(weighted, (0, 2, 1, 3)).reshape(local_count * node_width, RHS * 3)
    node_slots = (node_ids - (part_index - 1) * NODE_DEV).reshape(-1)
    partial_sums = jax.ops.segment_sum(values, node_slots, 3 * NODE_DEV).T
    chunks = jnp.transpose(
        partial_sums.reshape(RHS * 3, 3, nb, NODE_DEV // nb), (1, 2, 0, 3)
    )
    shape_gradient = node_reduce(chunks, collective_id=1)
    return (adjoint, shape_gradient)


def solution(mesh):
    in_specs = (
        P("dom", None, "blk"),
        P("dom", None, "blk"),
        P("dom", None, "blk", None),
        P("dom", "blk", None),
        P("dom", None),
        P("dom"),
        P("dom", "blk", None),
        P("dom", None),
    )
    out_specs = (P("dom", None, "blk"), P(None, ("dom", "blk")))
    return jax.shard_map(local, mesh=mesh, in_specs=in_specs, out_specs=out_specs, check_vma=False)
```

```python
import functools

import jax
import jax.numpy as jnp
from jax import lax
from jax.experimental import pallas as pl
from jax.experimental.pallas import tpu as pltpu
from jax.sharding import PartitionSpec as P

RHS = 3
SWEEPS = 2
NODE_DEV = 768
MESH = pl.DeviceIdType.MESH


def _halo_partners(nb):
    return [(delta, m) for delta in (-1, 0, 1) for m in range(nb) if (delta, m) != (0, 0)]


def _barrier(partners, in_range, d, b, nb):
    barrier = pltpu.get_barrier_semaphore()
    for delta, m in partners:
        @pl.when(in_range(d + delta))
        def _(delta=delta, m=m):
            pl.semaphore_signal(
                barrier, 1, device_id=(d + delta, (b + m) % nb), device_id_type=MESH
            )
    nd = lax.axis_size("dom")
    has_lower = (d + nd - 1) // nd
    has_upper = (2 * nd - 2 - d) // nd
    peers = [sum(1 for delta, _ in partners if delta == side) for side in (-1, 0, 1)]
    pl.semaphore_wait(barrier, peers[1] + peers[0] * has_lower + peers[2] * has_upper)


def _halo_gather_kernel(x_ref, out_ref, buf, send_sem, recv_sem):
    d, b = lax.axis_index("dom"), lax.axis_index("blk")
    nd, nb = lax.axis_size("dom"), lax.axis_size("blk")
    partners = _halo_partners(nb)

    def in_range(i):
        return (i >= 0) & (i < nd)

    _barrier(partners, in_range, d, b, nb)

    def outgoing(delta, m):
        return pltpu.make_async_remote_copy(
            src_ref=x_ref,
            dst_ref=buf.at[1 - delta, b],
            send_sem=send_sem.at[delta + 1, m],
            recv_sem=recv_sem.at[1 - delta, b],
            device_id=(d + delta, (b + m) % nb),
            device_id_type=MESH,
        )

    for delta, m in partners:
        pl.when(in_range(d + delta))(lambda delta=delta, m=m: outgoing(delta, m).start())
    buf[1, b] = x_ref[...]
    for side in (-1, 1):
        @pl.when(jnp.logical_not(in_range(d + side)))
        def _(side=side):
            buf[1 + side] = jnp.zeros(buf.shape[1:], buf.dtype)
    for delta, m in partners:
        pl.when(in_range(d + delta))(lambda delta=delta, m=m: outgoing(delta, m).wait_send())
    for delta, m in partners:
        p, s = 1 + delta, (b + m) % nb

        @pl.when(in_range(d + delta))
        def _(p=p, s=s):
            pltpu.make_async_remote_copy(
                src_ref=x_ref,
                dst_ref=buf.at[p, s],
                send_sem=send_sem.at[p, 0],
                recv_sem=recv_sem.at[p, s],
                device_id=(d + p - 1, s),
                device_id_type=MESH,
            ).wait_recv()

    out_ref[...] = buf[...]


def _blk_gather_kernel(x_ref, out_ref, buf, send_sem, recv_sem):
    d, b = lax.axis_index("dom"), lax.axis_index("blk")
    nd, nb = lax.axis_size("dom"), lax.axis_size("blk")
    partners = [(0, m) for m in range(1, nb)]
    _barrier(partners, lambda i: (i >= 0) & (i < nd), d, b, nb)

    def outgoing(m):
        return pltpu.make_async_remote_copy(
            src_ref=x_ref,
            dst_ref=buf.at[b],
            send_sem=send_sem.at[m],
            recv_sem=recv_sem.at[b],
            device_id=(d, (b + m) % nb),
            device_id_type=MESH,
        )

    for _, m in partners:
        outgoing(m).start()
    buf[b] = x_ref[...]
    for _, m in partners:
        outgoing(m).wait_send()
    for _, m in partners:
        s = (b + m) % nb
        pltpu.make_async_remote_copy(
            src_ref=x_ref,
            dst_ref=buf.at[s],
            send_sem=send_sem.at[0],
            recv_sem=recv_sem.at[s],
            device_id=(d, s),
            device_id_type=MESH,
        ).wait_recv()
    out_ref[...] = buf[...]


def _node_reduce_kernel(x_ref, out_ref, buf, send_sem, recv_sem):
    d, b = lax.axis_index("dom"), lax.axis_index("blk")
    nd, nb = lax.axis_size("dom"), lax.axis_size("blk")
    partners = _halo_partners(nb)

    def in_range(i):
        return (i >= 0) & (i < nd)

    _barrier(partners, in_range, d, b, nb)

    def outgoing(delta, m):
        p = 1 + delta
        return pltpu.make_async_remote_copy(
            src_ref=x_ref.at[p, (b + m) % nb],
            dst_ref=buf.at[p, b],
            send_sem=send_sem.at[p, m],
            recv_sem=recv_sem.at[p, b],
            device_id=(d + delta, (b + m) % nb),
            device_id_type=MESH,
        )

    for delta, m in partners:
        pl.when(in_range(d + delta))(lambda delta=delta, m=m: outgoing(delta, m).start())
    out_ref[...] = x_ref[1, b]
    for delta, m in partners:
        pl.when(in_range(d + delta))(lambda delta=delta, m=m: outgoing(delta, m).wait_send())
    for delta, m in partners:
        p, s = 1 + delta, (b + m) % nb

        @pl.when(in_range(d - delta))
        def _(p=p, s=s):
            pltpu.make_async_remote_copy(
                src_ref=x_ref.at[p, s],
                dst_ref=buf.at[p, s],
                send_sem=send_sem.at[p, 0],
                recv_sem=recv_sem.at[p, s],
                device_id=(d - delta, s),
                device_id_type=MESH,
            ).wait_recv()
            out_ref[...] += buf[p, s]


def _exchange(kernel, x, out_shape, buf_shape, sem_shape, collective_id):
    return pl.pallas_call(
        kernel,
        out_shape=jax.ShapeDtypeStruct(out_shape, x.dtype),
        in_specs=[pl.BlockSpec(memory_space=pltpu.VMEM)],
        out_specs=pl.BlockSpec(memory_space=pltpu.VMEM),
        scratch_shapes=[
            pltpu.VMEM(buf_shape, x.dtype),
            pltpu.SemaphoreType.DMA(sem_shape),
            pltpu.SemaphoreType.DMA(sem_shape),
        ],
        compiler_params=pltpu.CompilerParams(
            collective_id=collective_id, has_side_effects=True
        ),
    )(x)


def halo_gather(x, nb, collective_id):
    shape = (3, nb) + x.shape
    out = _exchange(_halo_gather_kernel, x, shape, shape, (3, nb), collective_id)
    e, r, c = x.shape
    return jnp.transpose(out, (0, 2, 3, 1, 4)).reshape(3 * e, r, nb * c)


def blk_gather(x, nb, collective_id):
    shape = (nb,) + x.shape
    out = _exchange(_blk_gather_kernel, x, shape, shape, (nb,), collective_id)
    e, r, c = x.shape
    return jnp.transpose(out, (1, 2, 0, 3)).reshape(e, r, nb * c)


def node_reduce(chunks, collective_id):
    nb = chunks.shape[1]
    return _exchange(
        _node_reduce_kernel, chunks, chunks.shape[2:], chunks.shape, (3, nb), collective_id
    )


LANES = 128


def _sweeps_kernel(
    adj_ref, rs_ref, shift_ref, target_ref, jac_hbm, inv_ref, shape_ref, out_ref, wsum_ref,
    jac_v, select, send_a, halo, send_r, full_r, upd, jac_sem, hs_send, hs_recv, bk_send, bk_recv,
    fw_send, wpart, ws_send, ws_recv,
):
    d, b = lax.axis_index("dom"), lax.axis_index("blk")
    nd, nb = lax.axis_size("dom"), lax.axis_size("blk")
    rows = adj_ref.shape[0]
    elems = jac_v.shape[0]
    faces = jac_v.shape[1]

    def in_range(i):
        return (i >= 0) & (i < nd)

    partners = [(0, m) for m in range(1, nb)] + [(-1, 0), (1, 0)]
    _barrier(partners, in_range, d, b, nb)
    jac_copy = pltpu.make_async_copy(jac_hbm, jac_v, jac_sem)
    jac_copy.start()
    lane = lax.broadcasted_iota(jnp.int32, (rows, LANES), 1)
    cand_row = lax.broadcasted_iota(jnp.int32, (3 * LANES, LANES), 0)
    for k in range(faces):
        select[k] = (cand_row == target_ref[pl.ds(k, 1), :]).astype(jnp.bfloat16)

    def row_block(i):
        return pl.ds(pl.multiple_of(i * rows, 16), rows)

    own_rows = row_block(b)
    adjoint = adj_ref[...]
    for sweep in range(SWEEPS):
        send_a[sweep] = adjoint.astype(jnp.bfloat16)

        def direct(delta, m, sweep=sweep):
            return pltpu.make_async_remote_copy(
                src_ref=send_a.at[sweep],
                dst_ref=halo.at[sweep, 1 - delta, own_rows],
                send_sem=hs_send.at[sweep, delta + 1, m],
                recv_sem=hs_recv.at[sweep, 1 - delta, b],
                device_id=(d + delta, (b + m) % nb),
                device_id_type=MESH,
            )

        def forward(p, m, sweep=sweep):
            return pltpu.make_async_remote_copy(
                src_ref=halo.at[sweep, p, own_rows],
                dst_ref=halo.at[sweep, p, own_rows],
                send_sem=fw_send.at[sweep, p // 2, m],
                recv_sem=hs_recv.at[sweep, p, b],
                device_id=(d, (b + m) % nb),
                device_id_type=MESH,
            )

        def arrival(p, src_b, sweep=sweep):
            return pltpu.make_async_remote_copy(
                src_ref=send_a.at[sweep],
                dst_ref=halo.at[sweep, p, row_block(src_b)],
                send_sem=hs_send.at[sweep, p, 0],
                recv_sem=hs_recv.at[sweep, p, src_b],
                device_id=(d, src_b),
                device_id_type=MESH,
            )

        for delta, m in partners:
            pl.when(in_range(d + delta))(lambda delta=delta, m=m: direct(delta, m).start())
        halo[sweep, 1, own_rows] = send_a[sweep]
        for side in (-1, 1):
            @pl.when(jnp.logical_not(in_range(d + side)))
            def _(side=side, sweep=sweep):
                halo[sweep, 1 + side] = jnp.zeros(halo.shape[2:], halo.dtype)
        for side in (-1, 1):
            p = 1 + side

            @pl.when(in_range(d + side))
            def _(p=p):
                arrival(p, b).wait_recv()
                for m in range(1, nb):
                    forward(p, m).start()
        for delta, m in partners:
            pl.when(in_range(d + delta))(lambda delta=delta, m=m: direct(delta, m).wait_send())
        for m in range(1, nb):
            arrival(1, (b + m) % nb).wait_recv()
        for side in (-1, 1):
            p = 1 + side

            @pl.when(in_range(d + side))
            def _(p=p):
                for m in range(1, nb):
                    forward(p, m).wait_send()
                for m in range(1, nb):
                    arrival(p, (b + m) % nb).wait_recv()

        candidates = jnp.concatenate([halo[sweep, p] for p in range(3)], axis=1)
        if sweep == 0:
            jac_copy.wait()
        acc = jnp.zeros((elems * rows, LANES), jnp.float32)
        for k in range(faces):
            picked = jnp.dot(candidates, select[k], preferred_element_type=jnp.float32)
            acc = acc + jnp.dot(
                jac_v[:, k].reshape(elems * rows, -1),
                picked.astype(jnp.bfloat16),
                preferred_element_type=jnp.float32,
            )
        upd[...] = acc.reshape(upd.shape)
        product = jnp.zeros((rows, LANES), jnp.float32)
        for e in range(elems):
            mine = (lane >= RHS * e) & (lane < RHS * e + RHS)
            product = product + jnp.where(mine, upd[e], 0.0)
        image = shift_ref[...] * adjoint + product
        send_r[sweep] = (rs_ref[...] - image).astype(jnp.bfloat16)

        def blk_copy(m, sweep=sweep):
            return pltpu.make_async_remote_copy(
                src_ref=send_r.at[sweep],
                dst_ref=full_r.at[sweep, own_rows],
                send_sem=bk_send.at[sweep, m],
                recv_sem=bk_recv.at[sweep, b],
                device_id=(d, (b + m) % nb),
                device_id_type=MESH,
            )

        for m in range(1, nb):
            blk_copy(m).start()
        full_r[sweep, own_rows] = send_r[sweep]
        for m in range(1, nb):
            blk_copy(m).wait_send()
        for m in range(1, nb):
            src_b = (b + m) % nb
            pltpu.make_async_remote_copy(
                src_ref=send_r.at[sweep],
                dst_ref=full_r.at[sweep, pl.ds(pl.multiple_of(src_b * rows, 16), rows)],
                send_sem=bk_send.at[sweep, 0],
                recv_sem=bk_recv.at[sweep, src_b],
                device_id=(d, src_b),
                device_id_type=MESH,
            ).wait_recv()
        upd[...] = jnp.dot(
            inv_ref[...], full_r[sweep], preferred_element_type=jnp.float32
        ).reshape(upd.shape)
        update = jnp.zeros((rows, LANES), jnp.float32)
        for e in range(elems):
            mine = (lane >= RHS * e) & (lane < RHS * e + RHS)
            update = update + jnp.where(mine, upd[e], 0.0)
        adjoint = adjoint + update
    out_ref[...] = adjoint

    square = jnp.concatenate([adjoint, jnp.zeros((LANES - rows, LANES), jnp.float32)], axis=0)
    final_half = jnp.transpose(square)[:, :rows].astype(jnp.bfloat16)
    row = lax.broadcasted_iota(jnp.int32, (LANES, shape_ref.shape[2]), 0)
    weighted = jnp.zeros((LANES, shape_ref.shape[2]), jnp.float32)
    for e in range(elems):
        part = jnp.dot(final_half, shape_ref[e], preferred_element_type=jnp.float32)
        weighted = weighted + jnp.where((row >= RHS * e) & (row < RHS * e + RHS), part, 0.0)
    wpart[pl.ds(0, LANES)] = -weighted
    chunk = wsum_ref.shape[0]
    owners = pl.cdiv(elems * RHS, chunk)

    def wcopy(c, src_b):
        return pltpu.make_async_remote_copy(
            src_ref=wpart.at[pl.ds(c * chunk, chunk)],
            dst_ref=wpart.at[pl.ds(LANES + src_b * chunk, chunk)],
            send_sem=ws_send.at[c],
            recv_sem=ws_recv.at[src_b],
            device_id=(d, c),
            device_id_type=MESH,
        )

    for m in range(1, nb):
        c = (b + m) % nb
        pl.when(c < owners)(lambda c=c: wcopy(c, b).start())
    for m in range(1, nb):
        c = (b + m) % nb
        pl.when(c < owners)(lambda c=c: wcopy(c, b).wait_send())
    total = jnp.zeros(wsum_ref.shape, jnp.float32)
    for m in range(1, nb):
        src_b = (b + m) % nb

        @pl.when(b < owners)
        def _(src_b=src_b):
            wcopy(b, src_b).wait_recv()

    @pl.when(b < owners)
    def _():
        acc = wpart[pl.ds(pl.multiple_of(b * chunk, 8), chunk)]
        for m in range(1, nb):
            src_b = (b + m) % nb
            acc = acc + wpart[pl.ds(pl.multiple_of(LANES + src_b * chunk, 8), chunk)]
        wsum_ref[...] = acc

    @pl.when(b >= owners)
    def _():
        wsum_ref[...] = jnp.zeros(wsum_ref.shape, jnp.float32)


def sweeps(adjoint_start, right_sides, pseudo_shift, slots, jac_blocks, block_inverse,
           shape_partials, nb):
    elems, rhs, rows = adjoint_start.shape
    cols = jac_blocks.shape[-1]
    faces = jac_blocks.shape[1]

    def transposed(x):
        x = jnp.transpose(x, (2, 0, 1)).reshape(rows, elems * rhs)
        return jnp.pad(x, ((0, 0), (0, LANES - elems * rhs)))

    shift = jnp.pad(jnp.repeat(pseudo_shift, rhs), (0, LANES - elems * rhs))[None, :]
    part, within = slots // elems, slots % elems
    lanes = (part * LANES + within * rhs)[:, :, None] + jnp.arange(rhs, dtype=jnp.int32)
    target = jnp.transpose(lanes, (1, 0, 2)).reshape(faces, elems * rhs)
    target = jnp.pad(target, ((0, 8 - faces), (0, LANES - elems * rhs)), constant_values=-1)
    vmem = pl.BlockSpec(memory_space=pltpu.VMEM)
    chunk = 8 * rhs
    out, wsum = pl.pallas_call(
        _sweeps_kernel,
        out_shape=(
            jax.ShapeDtypeStruct((rows, LANES), jnp.float32),
            jax.ShapeDtypeStruct((chunk, shape_partials.shape[2]), jnp.float32),
        ),
        in_specs=[vmem, vmem, vmem, vmem, pl.BlockSpec(memory_space=pl.ANY), vmem, vmem],
        out_specs=(vmem, vmem),
        scratch_shapes=[
            pltpu.VMEM((elems, faces, rows, cols), jnp.bfloat16),
            pltpu.VMEM((faces, 3 * LANES, LANES), jnp.bfloat16),
            pltpu.VMEM((SWEEPS, rows, LANES), jnp.bfloat16),
            pltpu.VMEM((SWEEPS, 3, nb * rows, LANES), jnp.bfloat16),
            pltpu.VMEM((SWEEPS, rows, LANES), jnp.bfloat16),
            pltpu.VMEM((SWEEPS, nb * rows, LANES), jnp.bfloat16),
            pltpu.VMEM((elems, rows, LANES), jnp.float32),
            pltpu.SemaphoreType.DMA(()),
            pltpu.SemaphoreType.DMA((SWEEPS, 3, nb)),
            pltpu.SemaphoreType.DMA((SWEEPS, 3, nb)),
            pltpu.SemaphoreType.DMA((SWEEPS, nb)),
            pltpu.SemaphoreType.DMA((SWEEPS, nb)),
            pltpu.SemaphoreType.DMA((SWEEPS, 2, nb)),
            pltpu.VMEM((LANES + nb * chunk, shape_partials.shape[2]), jnp.float32),
            pltpu.SemaphoreType.DMA((nb,)),
            pltpu.SemaphoreType.DMA((nb,)),
        ],
        compiler_params=pltpu.CompilerParams(
            collective_id=0, has_side_effects=True, vmem_limit_bytes=48 * 1024 * 1024
        ),
    )(
        transposed(adjoint_start),
        transposed(right_sides),
        shift,
        target,
        jac_blocks,
        block_inverse.reshape(elems * rows, cols),
        shape_partials,
    )
    adjoint = jnp.transpose(out[:, : elems * rhs].reshape(rows, elems, rhs), (1, 2, 0))
    return adjoint, wsum


def local(
    adjoint_start,
    right_sides,
    jac_blocks,
    block_inverse,
    neighbours,
    pseudo_shift,
    shape_partials,
    node_ids,
):
    local_count = neighbours.shape[0]
    nb = lax.axis_size("blk")
    part_index = lax.axis_index("dom")
    own = jnp.arange(local_count, dtype=jnp.int32)[:, None] + local_count
    slots = jnp.concatenate([own, neighbours - (part_index - 1) * local_count], axis=1)
    adjoint, wsum = sweeps(
        adjoint_start, right_sides, pseudo_shift, slots, jac_blocks, block_inverse,
        shape_partials, nb,
    )
    node_width = node_ids.shape[1]
    chunk_elems = wsum.shape[0] // RHS
    values = wsum.reshape(chunk_elems, RHS, node_width, 3)
    values = jnp.transpose(values, (0, 2, 1, 3)).reshape(chunk_elems * node_width, RHS * 3)
    my_nodes = lax.dynamic_slice_in_dim(
        node_ids, jnp.minimum(lax.axis_index("blk") * chunk_elems, local_count - chunk_elems),
        chunk_elems,
    )
    node_slots = (my_nodes - (part_index - 1) * NODE_DEV).reshape(-1)
    partial_sums = jax.ops.segment_sum(values, node_slots, 3 * NODE_DEV).T
    chunks = jnp.transpose(
        partial_sums.reshape(RHS * 3, 3, nb, NODE_DEV // nb), (1, 2, 0, 3)
    )
    shape_gradient = node_reduce(chunks, collective_id=1)
    return (adjoint, shape_gradient)


def solution(mesh):
    in_specs = (
        P("dom", None, "blk"),
        P("dom", None, "blk"),
        P("dom", None, "blk", None),
        P("dom", "blk", None),
        P("dom", None),
        P("dom"),
        P("dom", "blk", None),
        P("dom", None),
    )
    out_specs = (P("dom", None, "blk"), P(None, ("dom", "blk")))
    return jax.shard_map(local, mesh=mesh, in_specs=in_specs, out_specs=out_specs, check_vma=False)
```

```python
import functools

import jax
import jax.numpy as jnp
from jax import lax
from jax.experimental import pallas as pl
from jax.experimental.pallas import tpu as pltpu
from jax.sharding import PartitionSpec as P

RHS = 3
SWEEPS = 2
NODE_DEV = 768
MESH = pl.DeviceIdType.MESH


def _halo_partners(nb):
    return [(delta, m) for delta in (-1, 0, 1) for m in range(nb) if (delta, m) != (0, 0)]


def _barrier(partners, in_range, d, b, nb):
    barrier = pltpu.get_barrier_semaphore()
    for delta, m in partners:
        @pl.when(in_range(d + delta))
        def _(delta=delta, m=m):
            pl.semaphore_signal(
                barrier, 1, device_id=(d + delta, (b + m) % nb), device_id_type=MESH
            )
    nd = lax.axis_size("dom")
    has_lower = (d + nd - 1) // nd
    has_upper = (2 * nd - 2 - d) // nd
    peers = [sum(1 for delta, _ in partners if delta == side) for side in (-1, 0, 1)]
    pl.semaphore_wait(barrier, peers[1] + peers[0] * has_lower + peers[2] * has_upper)


def _halo_gather_kernel(x_ref, out_ref, buf, send_sem, recv_sem):
    d, b = lax.axis_index("dom"), lax.axis_index("blk")
    nd, nb = lax.axis_size("dom"), lax.axis_size("blk")
    partners = _halo_partners(nb)

    def in_range(i):
        return (i >= 0) & (i < nd)

    _barrier(partners, in_range, d, b, nb)

    def outgoing(delta, m):
        return pltpu.make_async_remote_copy(
            src_ref=x_ref,
            dst_ref=buf.at[1 - delta, b],
            send_sem=send_sem.at[delta + 1, m],
            recv_sem=recv_sem.at[1 - delta, b],
            device_id=(d + delta, (b + m) % nb),
            device_id_type=MESH,
        )

    for delta, m in partners:
        pl.when(in_range(d + delta))(lambda delta=delta, m=m: outgoing(delta, m).start())
    buf[1, b] = x_ref[...]
    for side in (-1, 1):
        @pl.when(jnp.logical_not(in_range(d + side)))
        def _(side=side):
            buf[1 + side] = jnp.zeros(buf.shape[1:], buf.dtype)
    for delta, m in partners:
        pl.when(in_range(d + delta))(lambda delta=delta, m=m: outgoing(delta, m).wait_send())
    for delta, m in partners:
        p, s = 1 + delta, (b + m) % nb

        @pl.when(in_range(d + delta))
        def _(p=p, s=s):
            pltpu.make_async_remote_copy(
                src_ref=x_ref,
                dst_ref=buf.at[p, s],
                send_sem=send_sem.at[p, 0],
                recv_sem=recv_sem.at[p, s],
                device_id=(d + p - 1, s),
                device_id_type=MESH,
            ).wait_recv()

    out_ref[...] = buf[...]


def _blk_gather_kernel(x_ref, out_ref, buf, send_sem, recv_sem):
    d, b = lax.axis_index("dom"), lax.axis_index("blk")
    nd, nb = lax.axis_size("dom"), lax.axis_size("blk")
    partners = [(0, m) for m in range(1, nb)]
    _barrier(partners, lambda i: (i >= 0) & (i < nd), d, b, nb)

    def outgoing(m):
        return pltpu.make_async_remote_copy(
            src_ref=x_ref,
            dst_ref=buf.at[b],
            send_sem=send_sem.at[m],
            recv_sem=recv_sem.at[b],
            device_id=(d, (b + m) % nb),
            device_id_type=MESH,
        )

    for _, m in partners:
        outgoing(m).start()
    buf[b] = x_ref[...]
    for _, m in partners:
        outgoing(m).wait_send()
    for _, m in partners:
        s = (b + m) % nb
        pltpu.make_async_remote_copy(
            src_ref=x_ref,
            dst_ref=buf.at[s],
            send_sem=send_sem.at[0],
            recv_sem=recv_sem.at[s],
            device_id=(d, s),
            device_id_type=MESH,
        ).wait_recv()
    out_ref[...] = buf[...]


def _node_reduce_kernel(x_ref, out_ref, buf, send_sem, recv_sem):
    d, b = lax.axis_index("dom"), lax.axis_index("blk")
    nd, nb = lax.axis_size("dom"), lax.axis_size("blk")
    partners = _halo_partners(nb)

    def in_range(i):
        return (i >= 0) & (i < nd)

    _barrier(partners, in_range, d, b, nb)

    def outgoing(delta, m):
        p = 1 + delta
        return pltpu.make_async_remote_copy(
            src_ref=x_ref.at[p, (b + m) % nb],
            dst_ref=buf.at[p, b],
            send_sem=send_sem.at[p, m],
            recv_sem=recv_sem.at[p, b],
            device_id=(d + delta, (b + m) % nb),
            device_id_type=MESH,
        )

    for delta, m in partners:
        pl.when(in_range(d + delta))(lambda delta=delta, m=m: outgoing(delta, m).start())
    out_ref[...] = x_ref[1, b]
    for delta, m in partners:
        pl.when(in_range(d + delta))(lambda delta=delta, m=m: outgoing(delta, m).wait_send())
    for delta, m in partners:
        p, s = 1 + delta, (b + m) % nb

        @pl.when(in_range(d - delta))
        def _(p=p, s=s):
            pltpu.make_async_remote_copy(
                src_ref=x_ref.at[p, s],
                dst_ref=buf.at[p, s],
                send_sem=send_sem.at[p, 0],
                recv_sem=recv_sem.at[p, s],
                device_id=(d - delta, s),
                device_id_type=MESH,
            ).wait_recv()
            out_ref[...] += buf[p, s]


def _exchange(kernel, x, out_shape, buf_shape, sem_shape, collective_id):
    return pl.pallas_call(
        kernel,
        out_shape=jax.ShapeDtypeStruct(out_shape, x.dtype),
        in_specs=[pl.BlockSpec(memory_space=pltpu.VMEM)],
        out_specs=pl.BlockSpec(memory_space=pltpu.VMEM),
        scratch_shapes=[
            pltpu.VMEM(buf_shape, x.dtype),
            pltpu.SemaphoreType.DMA(sem_shape),
            pltpu.SemaphoreType.DMA(sem_shape),
        ],
        compiler_params=pltpu.CompilerParams(
            collective_id=collective_id, has_side_effects=True
        ),
    )(x)


def halo_gather(x, nb, collective_id):
    shape = (3, nb) + x.shape
    out = _exchange(_halo_gather_kernel, x, shape, shape, (3, nb), collective_id)
    e, r, c = x.shape
    return jnp.transpose(out, (0, 2, 3, 1, 4)).reshape(3 * e, r, nb * c)


def blk_gather(x, nb, collective_id):
    shape = (nb,) + x.shape
    out = _exchange(_blk_gather_kernel, x, shape, shape, (nb,), collective_id)
    e, r, c = x.shape
    return jnp.transpose(out, (1, 2, 0, 3)).reshape(e, r, nb * c)


def node_reduce(chunks, collective_id):
    nb = chunks.shape[1]
    return _exchange(
        _node_reduce_kernel, chunks, chunks.shape[2:], chunks.shape, (3, nb), collective_id
    )


LANES = 128


def _sweeps_kernel(
    start_ref, shift_ref, target_ref, jac_hbm, inv_hbm, shape_hbm, out_ref, wsum_ref,
    jac_v, inv_ref, shape_ref, select, send_a, halo, send_r, full_r, upd, jac_sem, hs_send, hs_recv, bk_send, bk_recv,
    fw_send, wpart, ws_send, ws_recv,
):
    d, b = lax.axis_index("dom"), lax.axis_index("blk")
    nd, nb = lax.axis_size("dom"), lax.axis_size("blk")
    rows = start_ref.shape[1]
    elems = jac_v.shape[0]
    faces = jac_v.shape[1]

    def in_range(i):
        return (i >= 0) & (i < nd)

    partners = [(0, m) for m in range(1, nb)] + [(-1, 0), (1, 0)]
    _barrier(partners, in_range, d, b, nb)
    jac_copy = pltpu.make_async_copy(jac_hbm, jac_v, jac_sem.at[0])
    inv_copy = pltpu.make_async_copy(inv_hbm, inv_ref, jac_sem.at[1])
    shape_copy = pltpu.make_async_copy(shape_hbm, shape_ref, jac_sem.at[2])
    jac_copy.start()
    inv_copy.start()
    shape_copy.start()
    lane = lax.broadcasted_iota(jnp.int32, (rows, LANES), 1)
    cand_row = lax.broadcasted_iota(jnp.int32, (3 * LANES, LANES), 0)
    for k in range(faces):
        select[k] = (cand_row == target_ref[pl.ds(k, 1), :]).astype(jnp.bfloat16)

    def row_block(i):
        return pl.ds(pl.multiple_of(i * rows, 16), rows)

    own_rows = row_block(b)
    adjoint = start_ref[0]
    for sweep in range(SWEEPS):
        send_a[sweep] = adjoint.astype(jnp.bfloat16)

        def direct(delta, m, sweep=sweep):
            return pltpu.make_async_remote_copy(
                src_ref=send_a.at[sweep],
                dst_ref=halo.at[sweep, 1 - delta, own_rows],
                send_sem=hs_send.at[sweep, delta + 1, m],
                recv_sem=hs_recv.at[sweep, 1 - delta, b],
                device_id=(d + delta, (b + m) % nb),
                device_id_type=MESH,
            )

        def forward(p, m, sweep=sweep):
            return pltpu.make_async_remote_copy(
                src_ref=halo.at[sweep, p, own_rows],
                dst_ref=halo.at[sweep, p, own_rows],
                send_sem=fw_send.at[sweep, p // 2, m],
                recv_sem=hs_recv.at[sweep, p, b],
                device_id=(d, (b + m) % nb),
                device_id_type=MESH,
            )

        def arrival(p, src_b, sweep=sweep):
            return pltpu.make_async_remote_copy(
                src_ref=send_a.at[sweep],
                dst_ref=halo.at[sweep, p, row_block(src_b)],
                send_sem=hs_send.at[sweep, p, 0],
                recv_sem=hs_recv.at[sweep, p, src_b],
                device_id=(d, src_b),
                device_id_type=MESH,
            )

        for delta, m in partners:
            pl.when(in_range(d + delta))(lambda delta=delta, m=m: direct(delta, m).start())
        halo[sweep, 1, own_rows] = send_a[sweep]
        for side in (-1, 1):
            @pl.when(jnp.logical_not(in_range(d + side)))
            def _(side=side, sweep=sweep):
                halo[sweep, 1 + side] = jnp.zeros(halo.shape[2:], halo.dtype)
        for side in (-1, 1):
            p = 1 + side

            @pl.when(in_range(d + side))
            def _(p=p):
                arrival(p, b).wait_recv()
                for m in range(1, nb):
                    forward(p, m).start()
        for delta, m in partners:
            pl.when(in_range(d + delta))(lambda delta=delta, m=m: direct(delta, m).wait_send())
        for m in range(1, nb):
            arrival(1, (b + m) % nb).wait_recv()
        for side in (-1, 1):
            p = 1 + side

            @pl.when(in_range(d + side))
            def _(p=p):
                for m in range(1, nb):
                    forward(p, m).wait_send()
                for m in range(1, nb):
                    arrival(p, (b + m) % nb).wait_recv()

        candidates = jnp.concatenate([halo[sweep, p] for p in range(3)], axis=1)
        if sweep == 0:
            jac_copy.wait()
        acc = jnp.zeros((elems * rows, LANES), jnp.float32)
        for k in range(faces):
            picked = jnp.dot(candidates, select[k], preferred_element_type=jnp.float32)
            acc = acc + jnp.dot(
                jac_v[:, k].reshape(elems * rows, -1),
                picked.astype(jnp.bfloat16),
                preferred_element_type=jnp.float32,
            )
        upd[...] = acc.reshape(upd.shape)
        product = jnp.zeros((rows, LANES), jnp.float32)
        for e in range(elems):
            mine = (lane >= RHS * e) & (lane < RHS * e + RHS)
            product = product + jnp.where(mine, upd[e], 0.0)
        image = shift_ref[...] * adjoint + product
        send_r[sweep] = (start_ref[1] - image).astype(jnp.bfloat16)

        def blk_copy(m, sweep=sweep):
            return pltpu.make_async_remote_copy(
                src_ref=send_r.at[sweep],
                dst_ref=full_r.at[sweep, own_rows],
                send_sem=bk_send.at[sweep, m],
                recv_sem=bk_recv.at[sweep, b],
                device_id=(d, (b + m) % nb),
                device_id_type=MESH,
            )

        for m in range(1, nb):
            blk_copy(m).start()
        full_r[sweep, own_rows] = send_r[sweep]
        for m in range(1, nb):
            blk_copy(m).wait_send()
        for m in range(1, nb):
            src_b = (b + m) % nb
            pltpu.make_async_remote_copy(
                src_ref=send_r.at[sweep],
                dst_ref=full_r.at[sweep, pl.ds(pl.multiple_of(src_b * rows, 16), rows)],
                send_sem=bk_send.at[sweep, 0],
                recv_sem=bk_recv.at[sweep, src_b],
                device_id=(d, src_b),
                device_id_type=MESH,
            ).wait_recv()
        if sweep == 0:
            inv_copy.wait()
        upd[...] = jnp.dot(
            inv_ref[...], full_r[sweep], preferred_element_type=jnp.float32
        ).reshape(upd.shape)
        update = jnp.zeros((rows, LANES), jnp.float32)
        for e in range(elems):
            mine = (lane >= RHS * e) & (lane < RHS * e + RHS)
            update = update + jnp.where(mine, upd[e], 0.0)
        adjoint = adjoint + update
    out_ref[...] = adjoint

    square = jnp.concatenate([adjoint, jnp.zeros((LANES - rows, LANES), jnp.float32)], axis=0)
    final_f32 = jnp.transpose(square)[:, :rows]
    window = 16
    row = lax.broadcasted_iota(jnp.int32, (window, shape_ref.shape[2]), 0)
    wpart[pl.ds(0, LANES)] = jnp.zeros((LANES, shape_ref.shape[2]), jnp.float32)
    shape_copy.wait()
    for e in range(elems):
        low = (RHS * e) // 8 * 8
        part = jnp.dot(
            final_f32[low:low + window].astype(jnp.bfloat16),
            shape_ref[e],
            preferred_element_type=jnp.float32,
        )
        mine = (row + low >= RHS * e) & (row + low < RHS * e + RHS)
        wpart[pl.ds(low, window)] = wpart[pl.ds(low, window)] - jnp.where(mine, part, 0.0)
    chunk = wsum_ref.shape[0]
    owners = pl.cdiv(elems * RHS, chunk)

    def wcopy(c, src_b):
        return pltpu.make_async_remote_copy(
            src_ref=wpart.at[pl.ds(c * chunk, chunk)],
            dst_ref=wpart.at[pl.ds(LANES + src_b * chunk, chunk)],
            send_sem=ws_send.at[c],
            recv_sem=ws_recv.at[src_b],
            device_id=(d, c),
            device_id_type=MESH,
        )

    for m in range(1, nb):
        c = (b + m) % nb
        pl.when(c < owners)(lambda c=c: wcopy(c, b).start())
    for m in range(1, nb):
        c = (b + m) % nb
        pl.when(c < owners)(lambda c=c: wcopy(c, b).wait_send())
    total = jnp.zeros(wsum_ref.shape, jnp.float32)
    for m in range(1, nb):
        src_b = (b + m) % nb

        @pl.when(b < owners)
        def _(src_b=src_b):
            wcopy(b, src_b).wait_recv()

    @pl.when(b < owners)
    def _():
        acc = wpart[pl.ds(pl.multiple_of(b * chunk, 8), chunk)]
        for m in range(1, nb):
            src_b = (b + m) % nb
            acc = acc + wpart[pl.ds(pl.multiple_of(LANES + src_b * chunk, 8), chunk)]
        wsum_ref[...] = acc

    @pl.when(b >= owners)
    def _():
        wsum_ref[...] = jnp.zeros(wsum_ref.shape, jnp.float32)


def sweeps(adjoint_start, right_sides, pseudo_shift, slots, jac_blocks, block_inverse,
           shape_partials, nb):
    elems, rhs, rows = adjoint_start.shape
    cols = jac_blocks.shape[-1]
    faces = jac_blocks.shape[1]

    def transposed(x):
        x = jnp.transpose(x, (0, 3, 1, 2)).reshape(x.shape[0], rows, elems * rhs)
        return jnp.pad(x, ((0, 0), (0, 0), (0, LANES - elems * rhs)))

    shift = jnp.pad(jnp.repeat(pseudo_shift, rhs), (0, LANES - elems * rhs))[None, :]
    part, within = slots // elems, slots % elems
    lanes = (part * LANES + within * rhs)[:, :, None] + jnp.arange(rhs, dtype=jnp.int32)
    target = jnp.transpose(lanes, (1, 0, 2)).reshape(faces, elems * rhs)
    target = jnp.pad(target, ((0, 8 - faces), (0, LANES - elems * rhs)), constant_values=-1)
    vmem = pl.BlockSpec(memory_space=pltpu.VMEM)
    hbm = pl.BlockSpec(memory_space=pl.ANY)
    chunk = 8 * rhs
    out, wsum = pl.pallas_call(
        _sweeps_kernel,
        out_shape=(
            jax.ShapeDtypeStruct((rows, LANES), jnp.float32),
            jax.ShapeDtypeStruct((chunk, shape_partials.shape[2]), jnp.float32),
        ),
        in_specs=[vmem, vmem, vmem, hbm, hbm, hbm],
        out_specs=(vmem, vmem),
        scratch_shapes=[
            pltpu.VMEM((elems, faces, rows, cols), jnp.bfloat16),
            pltpu.VMEM((elems * rows, cols), jnp.bfloat16),
            pltpu.VMEM(shape_partials.shape, shape_partials.dtype),
            pltpu.VMEM((faces, 3 * LANES, LANES), jnp.bfloat16),
            pltpu.VMEM((SWEEPS, rows, LANES), jnp.bfloat16),
            pltpu.VMEM((SWEEPS, 3, nb * rows, LANES), jnp.bfloat16),
            pltpu.VMEM((SWEEPS, rows, LANES), jnp.bfloat16),
            pltpu.VMEM((SWEEPS, nb * rows, LANES), jnp.bfloat16),
            pltpu.VMEM((elems, rows, LANES), jnp.float32),
            pltpu.SemaphoreType.DMA((3,)),
            pltpu.SemaphoreType.DMA((SWEEPS, 3, nb)),
            pltpu.SemaphoreType.DMA((SWEEPS, 3, nb)),
            pltpu.SemaphoreType.DMA((SWEEPS, nb)),
            pltpu.SemaphoreType.DMA((SWEEPS, nb)),
            pltpu.SemaphoreType.DMA((SWEEPS, 2, nb)),
            pltpu.VMEM((LANES + nb * chunk, shape_partials.shape[2]), jnp.float32),
            pltpu.SemaphoreType.DMA((nb,)),
            pltpu.SemaphoreType.DMA((nb,)),
        ],
        compiler_params=pltpu.CompilerParams(
            collective_id=0, has_side_effects=True, vmem_limit_bytes=48 * 1024 * 1024
        ),
    )(
        transposed(jnp.stack([adjoint_start, right_sides])),
        shift,
        target,
        jac_blocks,
        block_inverse.reshape(elems * rows, cols),
        shape_partials,
    )
    adjoint = jnp.transpose(out[:, : elems * rhs].reshape(rows, elems, rhs), (1, 2, 0))
    return adjoint, wsum


def local(
    adjoint_start,
    right_sides,
    jac_blocks,
    block_inverse,
    neighbours,
    pseudo_shift,
    shape_partials,
    node_ids,
):
    local_count = neighbours.shape[0]
    nb = lax.axis_size("blk")
    part_index = lax.axis_index("dom")
    own = jnp.arange(local_count, dtype=jnp.int32)[:, None] + local_count
    slots = jnp.concatenate([own, neighbours - (part_index - 1) * local_count], axis=1)
    adjoint, wsum = sweeps(
        adjoint_start, right_sides, pseudo_shift, slots, jac_blocks, block_inverse,
        shape_partials, nb,
    )
    node_width = node_ids.shape[1]
    chunk_elems = wsum.shape[0] // RHS
    values = wsum.reshape(chunk_elems, RHS, node_width, 3)
    values = jnp.transpose(values, (0, 2, 1, 3)).reshape(chunk_elems * node_width, RHS * 3)
    my_nodes = lax.dynamic_slice_in_dim(
        node_ids, jnp.minimum(lax.axis_index("blk") * chunk_elems, local_count - chunk_elems),
        chunk_elems,
    )
    node_slots = (my_nodes - (part_index - 1) * NODE_DEV).reshape(-1)
    partial_sums = jax.ops.segment_sum(values, node_slots, 3 * NODE_DEV).T
    chunks = jnp.transpose(
        partial_sums.reshape(RHS * 3, 3, nb, NODE_DEV // nb), (1, 2, 0, 3)
    )
    shape_gradient = node_reduce(chunks, collective_id=1)
    return (adjoint, shape_gradient)


def solution(mesh):
    in_specs = (
        P("dom", None, "blk"),
        P("dom", None, "blk"),
        P("dom", None, "blk", None),
        P("dom", "blk", None),
        P("dom", None),
        P("dom"),
        P("dom", "blk", None),
        P("dom", None),
    )
    out_specs = (P("dom", None, "blk"), P(None, ("dom", "blk")))
    return jax.shard_map(local, mesh=mesh, in_specs=in_specs, out_specs=out_specs, check_vma=False)
```

```python
import functools

import jax
import jax.numpy as jnp
from jax import lax
from jax.experimental import pallas as pl
from jax.experimental.pallas import tpu as pltpu
from jax.sharding import PartitionSpec as P

RHS = 3
SWEEPS = 2
NODE_DEV = 768
MESH = pl.DeviceIdType.MESH


def _halo_partners(nb):
    return [(delta, m) for delta in (-1, 0, 1) for m in range(nb) if (delta, m) != (0, 0)]


def _barrier(partners, in_range, d, b, nb):
    barrier = pltpu.get_barrier_semaphore()
    for delta, m in partners:
        @pl.when(in_range(d + delta))
        def _(delta=delta, m=m):
            pl.semaphore_signal(
                barrier, 1, device_id=(d + delta, (b + m) % nb), device_id_type=MESH
            )
    nd = lax.axis_size("dom")
    has_lower = (d + nd - 1) // nd
    has_upper = (2 * nd - 2 - d) // nd
    peers = [sum(1 for delta, _ in partners if delta == side) for side in (-1, 0, 1)]
    pl.semaphore_wait(barrier, peers[1] + peers[0] * has_lower + peers[2] * has_upper)


def _halo_gather_kernel(x_ref, out_ref, buf, send_sem, recv_sem):
    d, b = lax.axis_index("dom"), lax.axis_index("blk")
    nd, nb = lax.axis_size("dom"), lax.axis_size("blk")
    partners = _halo_partners(nb)

    def in_range(i):
        return (i >= 0) & (i < nd)

    _barrier(partners, in_range, d, b, nb)

    def outgoing(delta, m):
        return pltpu.make_async_remote_copy(
            src_ref=x_ref,
            dst_ref=buf.at[1 - delta, b],
            send_sem=send_sem.at[delta + 1, m],
            recv_sem=recv_sem.at[1 - delta, b],
            device_id=(d + delta, (b + m) % nb),
            device_id_type=MESH,
        )

    for delta, m in partners:
        pl.when(in_range(d + delta))(lambda delta=delta, m=m: outgoing(delta, m).start())
    buf[1, b] = x_ref[...]
    for side in (-1, 1):
        @pl.when(jnp.logical_not(in_range(d + side)))
        def _(side=side):
            buf[1 + side] = jnp.zeros(buf.shape[1:], buf.dtype)
    for delta, m in partners:
        pl.when(in_range(d + delta))(lambda delta=delta, m=m: outgoing(delta, m).wait_send())
    for delta, m in partners:
        p, s = 1 + delta, (b + m) % nb

        @pl.when(in_range(d + delta))
        def _(p=p, s=s):
            pltpu.make_async_remote_copy(
                src_ref=x_ref,
                dst_ref=buf.at[p, s],
                send_sem=send_sem.at[p, 0],
                recv_sem=recv_sem.at[p, s],
                device_id=(d + p - 1, s),
                device_id_type=MESH,
            ).wait_recv()

    out_ref[...] = buf[...]


def _blk_gather_kernel(x_ref, out_ref, buf, send_sem, recv_sem):
    d, b = lax.axis_index("dom"), lax.axis_index("blk")
    nd, nb = lax.axis_size("dom"), lax.axis_size("blk")
    partners = [(0, m) for m in range(1, nb)]
    _barrier(partners, lambda i: (i >= 0) & (i < nd), d, b, nb)

    def outgoing(m):
        return pltpu.make_async_remote_copy(
            src_ref=x_ref,
            dst_ref=buf.at[b],
            send_sem=send_sem.at[m],
            recv_sem=recv_sem.at[b],
            device_id=(d, (b + m) % nb),
            device_id_type=MESH,
        )

    for _, m in partners:
        outgoing(m).start()
    buf[b] = x_ref[...]
    for _, m in partners:
        outgoing(m).wait_send()
    for _, m in partners:
        s = (b + m) % nb
        pltpu.make_async_remote_copy(
            src_ref=x_ref,
            dst_ref=buf.at[s],
            send_sem=send_sem.at[0],
            recv_sem=recv_sem.at[s],
            device_id=(d, s),
            device_id_type=MESH,
        ).wait_recv()
    out_ref[...] = buf[...]


def _node_reduce_kernel(x_ref, out_ref, buf, send_sem, recv_sem):
    d, b = lax.axis_index("dom"), lax.axis_index("blk")
    nd, nb = lax.axis_size("dom"), lax.axis_size("blk")
    partners = _halo_partners(nb)

    def in_range(i):
        return (i >= 0) & (i < nd)

    _barrier(partners, in_range, d, b, nb)

    def outgoing(delta, m):
        p = 1 + delta
        return pltpu.make_async_remote_copy(
            src_ref=x_ref.at[p, (b + m) % nb],
            dst_ref=buf.at[p, b],
            send_sem=send_sem.at[p, m],
            recv_sem=recv_sem.at[p, b],
            device_id=(d + delta, (b + m) % nb),
            device_id_type=MESH,
        )

    for delta, m in partners:
        pl.when(in_range(d + delta))(lambda delta=delta, m=m: outgoing(delta, m).start())
    out_ref[...] = x_ref[1, b]
    for delta, m in partners:
        pl.when(in_range(d + delta))(lambda delta=delta, m=m: outgoing(delta, m).wait_send())
    for delta, m in partners:
        p, s = 1 + delta, (b + m) % nb

        @pl.when(in_range(d - delta))
        def _(p=p, s=s):
            pltpu.make_async_remote_copy(
                src_ref=x_ref.at[p, s],
                dst_ref=buf.at[p, s],
                send_sem=send_sem.at[p, 0],
                recv_sem=recv_sem.at[p, s],
                device_id=(d - delta, s),
                device_id_type=MESH,
            ).wait_recv()
            out_ref[...] += buf[p, s]


def _exchange(kernel, x, out_shape, buf_shape, sem_shape, collective_id):
    return pl.pallas_call(
        kernel,
        out_shape=jax.ShapeDtypeStruct(out_shape, x.dtype),
        in_specs=[pl.BlockSpec(memory_space=pltpu.VMEM)],
        out_specs=pl.BlockSpec(memory_space=pltpu.VMEM),
        scratch_shapes=[
            pltpu.VMEM(buf_shape, x.dtype),
            pltpu.SemaphoreType.DMA(sem_shape),
            pltpu.SemaphoreType.DMA(sem_shape),
        ],
        compiler_params=pltpu.CompilerParams(
            collective_id=collective_id, has_side_effects=True
        ),
    )(x)


def halo_gather(x, nb, collective_id):
    shape = (3, nb) + x.shape
    out = _exchange(_halo_gather_kernel, x, shape, shape, (3, nb), collective_id)
    e, r, c = x.shape
    return jnp.transpose(out, (0, 2, 3, 1, 4)).reshape(3 * e, r, nb * c)


def blk_gather(x, nb, collective_id):
    shape = (nb,) + x.shape
    out = _exchange(_blk_gather_kernel, x, shape, shape, (nb,), collective_id)
    e, r, c = x.shape
    return jnp.transpose(out, (1, 2, 0, 3)).reshape(e, r, nb * c)


def node_reduce(chunks, collective_id):
    nb = chunks.shape[1]
    return _exchange(
        _node_reduce_kernel, chunks, chunks.shape[2:], chunks.shape, (3, nb), collective_id
    )


LANES = 128


def _sweeps_kernel(
    start_ref, shift_ref, slot_ref, jac_hbm, inv_hbm, shape_hbm, out_ref, wsum_ref,
    jac_v, inv_ref, shape_ref, select, send_a, halo, send_r, full_r, upd, jac_sem, hs_send, hs_recv, bk_send, bk_recv,
    fw_send, wpart, ws_send, ws_recv,
):
    d, b = lax.axis_index("dom"), lax.axis_index("blk")
    nd, nb = lax.axis_size("dom"), lax.axis_size("blk")
    rows = start_ref.shape[1]
    elems = jac_v.shape[0]
    faces = jac_v.shape[1]

    def in_range(i):
        return (i >= 0) & (i < nd)

    partners = [(0, m) for m in range(1, nb)] + [(-1, 0), (1, 0)]
    _barrier(partners, in_range, d, b, nb)
    jac_copy = pltpu.make_async_copy(jac_hbm, jac_v, jac_sem.at[0])
    inv_copy = pltpu.make_async_copy(inv_hbm, inv_ref, jac_sem.at[1])
    shape_copy = pltpu.make_async_copy(shape_hbm, shape_ref, jac_sem.at[2])
    jac_copy.start()
    inv_copy.start()
    shape_copy.start()
    lane = lax.broadcasted_iota(jnp.int32, (rows, LANES), 1)
    sub = lax.broadcasted_iota(jnp.int32, (8, LANES), 0)
    lane8 = lax.broadcasted_iota(jnp.int32, (8, LANES), 1)
    target = jnp.full((8, LANES), -1, jnp.int32)
    shift = jnp.zeros((8, LANES), jnp.float32)
    for e in range(elems):
        mine = lane8 // RHS == e
        shift = jnp.where(mine, shift_ref[e], shift)
        for k in range(faces):
            slot = elems + e if k == 0 else slot_ref[e, k - 1] - (d - 1) * elems
            base = slot // elems * LANES + slot % elems * RHS
            target = jnp.where(mine & (sub == k), base + lane8 % RHS, target)
    shift = shift[0:1]
    cand_row = lax.broadcasted_iota(jnp.int32, (3 * LANES, LANES), 0)
    for k in range(faces):
        select[k] = (cand_row == target[k:k + 1]).astype(jnp.bfloat16)

    def row_block(i):
        return pl.ds(pl.multiple_of(i * rows, 16), rows)

    own_rows = row_block(b)
    adjoint = start_ref[0]
    for sweep in range(SWEEPS):
        send_a[sweep] = adjoint.astype(jnp.bfloat16)

        def direct(delta, m, sweep=sweep):
            return pltpu.make_async_remote_copy(
                src_ref=send_a.at[sweep],
                dst_ref=halo.at[sweep, 1 - delta, own_rows],
                send_sem=hs_send.at[sweep, delta + 1, m],
                recv_sem=hs_recv.at[sweep, 1 - delta, b],
                device_id=(d + delta, (b + m) % nb),
                device_id_type=MESH,
            )

        def forward(p, m, sweep=sweep):
            return pltpu.make_async_remote_copy(
                src_ref=halo.at[sweep, p, own_rows],
                dst_ref=halo.at[sweep, p, own_rows],
                send_sem=fw_send.at[sweep, p // 2, m],
                recv_sem=hs_recv.at[sweep, p, b],
                device_id=(d, (b + m) % nb),
                device_id_type=MESH,
            )

        def arrival(p, src_b, sweep=sweep):
            return pltpu.make_async_remote_copy(
                src_ref=send_a.at[sweep],
                dst_ref=halo.at[sweep, p, row_block(src_b)],
                send_sem=hs_send.at[sweep, p, 0],
                recv_sem=hs_recv.at[sweep, p, src_b],
                device_id=(d, src_b),
                device_id_type=MESH,
            )

        for delta, m in partners:
            pl.when(in_range(d + delta))(lambda delta=delta, m=m: direct(delta, m).start())
        halo[sweep, 1, own_rows] = send_a[sweep]
        for side in (-1, 1):
            @pl.when(jnp.logical_not(in_range(d + side)))
            def _(side=side, sweep=sweep):
                halo[sweep, 1 + side] = jnp.zeros(halo.shape[2:], halo.dtype)
        for side in (-1, 1):
            p = 1 + side

            @pl.when(in_range(d + side))
            def _(p=p):
                arrival(p, b).wait_recv()
                for m in range(1, nb):
                    forward(p, m).start()
        for delta, m in partners:
            pl.when(in_range(d + delta))(lambda delta=delta, m=m: direct(delta, m).wait_send())
        for m in range(1, nb):
            arrival(1, (b + m) % nb).wait_recv()
        for side in (-1, 1):
            p = 1 + side

            @pl.when(in_range(d + side))
            def _(p=p):
                for m in range(1, nb):
                    forward(p, m).wait_send()
                for m in range(1, nb):
                    arrival(p, (b + m) % nb).wait_recv()

        candidates = jnp.concatenate([halo[sweep, p] for p in range(3)], axis=1)
        if sweep == 0:
            jac_copy.wait()
        acc = jnp.zeros((elems * rows, LANES), jnp.float32)
        for k in range(faces):
            picked = jnp.dot(candidates, select[k], preferred_element_type=jnp.float32)
            acc = acc + jnp.dot(
                jac_v[:, k].reshape(elems * rows, -1),
                picked.astype(jnp.bfloat16),
                preferred_element_type=jnp.float32,
            )
        upd[...] = acc.reshape(upd.shape)
        product = jnp.zeros((rows, LANES), jnp.float32)
        for e in range(elems):
            mine = (lane >= RHS * e) & (lane < RHS * e + RHS)
            product = product + jnp.where(mine, upd[e], 0.0)
        image = shift * adjoint + product
        send_r[sweep] = (start_ref[1] - image).astype(jnp.bfloat16)

        def blk_copy(m, sweep=sweep):
            return pltpu.make_async_remote_copy(
                src_ref=send_r.at[sweep],
                dst_ref=full_r.at[sweep, own_rows],
                send_sem=bk_send.at[sweep, m],
                recv_sem=bk_recv.at[sweep, b],
                device_id=(d, (b + m) % nb),
                device_id_type=MESH,
            )

        for m in range(1, nb):
            blk_copy(m).start()
        full_r[sweep, own_rows] = send_r[sweep]
        for m in range(1, nb):
            blk_copy(m).wait_send()
        for m in range(1, nb):
            src_b = (b + m) % nb
            pltpu.make_async_remote_copy(
                src_ref=send_r.at[sweep],
                dst_ref=full_r.at[sweep, pl.ds(pl.multiple_of(src_b * rows, 16), rows)],
                send_sem=bk_send.at[sweep, 0],
                recv_sem=bk_recv.at[sweep, src_b],
                device_id=(d, src_b),
                device_id_type=MESH,
            ).wait_recv()
        if sweep == 0:
            inv_copy.wait()
        upd[...] = jnp.dot(
            inv_ref[...], full_r[sweep], preferred_element_type=jnp.float32
        ).reshape(upd.shape)
        update = jnp.zeros((rows, LANES), jnp.float32)
        for e in range(elems):
            mine = (lane >= RHS * e) & (lane < RHS * e + RHS)
            update = update + jnp.where(mine, upd[e], 0.0)
        adjoint = adjoint + update
    out_ref[...] = adjoint

    square = jnp.concatenate([adjoint, jnp.zeros((LANES - rows, LANES), jnp.float32)], axis=0)
    final_f32 = jnp.transpose(square)[:, :rows]
    window = 16
    row = lax.broadcasted_iota(jnp.int32, (window, shape_ref.shape[2]), 0)
    wpart[pl.ds(0, LANES)] = jnp.zeros((LANES, shape_ref.shape[2]), jnp.float32)
    shape_copy.wait()
    for e in range(elems):
        low = (RHS * e) // 8 * 8
        part = jnp.dot(
            final_f32[low:low + window].astype(jnp.bfloat16),
            shape_ref[e],
            preferred_element_type=jnp.float32,
        )
        mine = (row + low >= RHS * e) & (row + low < RHS * e + RHS)
        wpart[pl.ds(low, window)] = wpart[pl.ds(low, window)] - jnp.where(mine, part, 0.0)
    chunk = wsum_ref.shape[0]
    owners = pl.cdiv(elems * RHS, chunk)

    def wcopy(c, src_b):
        return pltpu.make_async_remote_copy(
            src_ref=wpart.at[pl.ds(c * chunk, chunk)],
            dst_ref=wpart.at[pl.ds(LANES + src_b * chunk, chunk)],
            send_sem=ws_send.at[c],
            recv_sem=ws_recv.at[src_b],
            device_id=(d, c),
            device_id_type=MESH,
        )

    for m in range(1, nb):
        c = (b + m) % nb
        pl.when(c < owners)(lambda c=c: wcopy(c, b).start())
    for m in range(1, nb):
        c = (b + m) % nb
        pl.when(c < owners)(lambda c=c: wcopy(c, b).wait_send())
    total = jnp.zeros(wsum_ref.shape, jnp.float32)
    for m in range(1, nb):
        src_b = (b + m) % nb

        @pl.when(b < owners)
        def _(src_b=src_b):
            wcopy(b, src_b).wait_recv()

    @pl.when(b < owners)
    def _():
        acc = wpart[pl.ds(pl.multiple_of(b * chunk, 8), chunk)]
        for m in range(1, nb):
            src_b = (b + m) % nb
            acc = acc + wpart[pl.ds(pl.multiple_of(LANES + src_b * chunk, 8), chunk)]
        wsum_ref[...] = acc

    @pl.when(b >= owners)
    def _():
        wsum_ref[...] = jnp.zeros(wsum_ref.shape, jnp.float32)


def sweeps(adjoint_start, right_sides, pseudo_shift, neighbours, jac_blocks, block_inverse,
           shape_partials, nb):
    elems, rhs, rows = adjoint_start.shape
    cols = jac_blocks.shape[-1]
    faces = jac_blocks.shape[1]

    def transposed(x):
        x = jnp.transpose(x, (0, 3, 1, 2)).reshape(x.shape[0], rows, elems * rhs)
        return jnp.pad(x, ((0, 0), (0, 0), (0, LANES - elems * rhs)))

    vmem = pl.BlockSpec(memory_space=pltpu.VMEM)
    hbm = pl.BlockSpec(memory_space=pl.ANY)
    smem = pl.BlockSpec(memory_space=pltpu.SMEM)
    chunk = 8 * rhs
    out, wsum = pl.pallas_call(
        _sweeps_kernel,
        out_shape=(
            jax.ShapeDtypeStruct((rows, LANES), jnp.float32),
            jax.ShapeDtypeStruct((chunk, shape_partials.shape[2]), jnp.float32),
        ),
        in_specs=[vmem, smem, smem, hbm, hbm, hbm],
        out_specs=(vmem, vmem),
        scratch_shapes=[
            pltpu.VMEM((elems, faces, rows, cols), jnp.bfloat16),
            pltpu.VMEM((elems * rows, cols), jnp.bfloat16),
            pltpu.VMEM(shape_partials.shape, shape_partials.dtype),
            pltpu.VMEM((faces, 3 * LANES, LANES), jnp.bfloat16),
            pltpu.VMEM((SWEEPS, rows, LANES), jnp.bfloat16),
            pltpu.VMEM((SWEEPS, 3, nb * rows, LANES), jnp.bfloat16),
            pltpu.VMEM((SWEEPS, rows, LANES), jnp.bfloat16),
            pltpu.VMEM((SWEEPS, nb * rows, LANES), jnp.bfloat16),
            pltpu.VMEM((elems, rows, LANES), jnp.float32),
            pltpu.SemaphoreType.DMA((3,)),
            pltpu.SemaphoreType.DMA((SWEEPS, 3, nb)),
            pltpu.SemaphoreType.DMA((SWEEPS, 3, nb)),
            pltpu.SemaphoreType.DMA((SWEEPS, nb)),
            pltpu.SemaphoreType.DMA((SWEEPS, nb)),
            pltpu.SemaphoreType.DMA((SWEEPS, 2, nb)),
            pltpu.VMEM((LANES + nb * chunk, shape_partials.shape[2]), jnp.float32),
            pltpu.SemaphoreType.DMA((nb,)),
            pltpu.SemaphoreType.DMA((nb,)),
        ],
        compiler_params=pltpu.CompilerParams(
            collective_id=0, has_side_effects=True, vmem_limit_bytes=67043328
        ),
    )(
        transposed(jnp.stack([adjoint_start, right_sides])),
        pseudo_shift,
        neighbours,
        jac_blocks,
        block_inverse.reshape(elems * rows, cols),
        shape_partials,
    )
    adjoint = jnp.transpose(out[:, : elems * rhs].reshape(rows, elems, rhs), (1, 2, 0))
    return adjoint, wsum


def local(
    adjoint_start,
    right_sides,
    jac_blocks,
    block_inverse,
    neighbours,
    pseudo_shift,
    shape_partials,
    node_ids,
):
    local_count = neighbours.shape[0]
    nb = lax.axis_size("blk")
    part_index = lax.axis_index("dom")
    adjoint, wsum = sweeps(
        adjoint_start, right_sides, pseudo_shift, neighbours, jac_blocks, block_inverse,
        shape_partials, nb,
    )
    node_width = node_ids.shape[1]
    chunk_elems = wsum.shape[0] // RHS
    values = wsum.reshape(chunk_elems, RHS, node_width, 3)
    values = jnp.transpose(values, (0, 2, 1, 3)).reshape(chunk_elems * node_width, RHS * 3)
    my_nodes = lax.dynamic_slice_in_dim(
        node_ids, jnp.minimum(lax.axis_index("blk") * chunk_elems, local_count - chunk_elems),
        chunk_elems,
    )
    node_slots = (my_nodes - (part_index - 1) * NODE_DEV).reshape(-1)
    partial_sums = jax.ops.segment_sum(values, node_slots, 3 * NODE_DEV).T
    chunks = jnp.transpose(
        partial_sums.reshape(RHS * 3, 3, nb, NODE_DEV // nb), (1, 2, 0, 3)
    )
    shape_gradient = node_reduce(chunks, collective_id=1)
    return (adjoint, shape_gradient)


def solution(mesh):
    in_specs = (
        P("dom", None, "blk"),
        P("dom", None, "blk"),
        P("dom", None, "blk", None),
        P("dom", "blk", None),
        P("dom", None),
        P("dom"),
        P("dom", "blk", None),
        P("dom", None),
    )
    out_specs = (P("dom", None, "blk"), P(None, ("dom", "blk")))
    return jax.shard_map(local, mesh=mesh, in_specs=in_specs, out_specs=out_specs, check_vma=False)
```

```python
import functools

import jax
import jax.numpy as jnp
from jax import lax
from jax.experimental import pallas as pl
from jax.experimental.pallas import tpu as pltpu
from jax.sharding import PartitionSpec as P

RHS = 3
SWEEPS = 2
NODE_DEV = 768
MESH = pl.DeviceIdType.MESH


def _halo_partners(nb):
    return [(delta, m) for delta in (-1, 0, 1) for m in range(nb) if (delta, m) != (0, 0)]


def _barrier(partners, in_range, d, b, nb):
    barrier = pltpu.get_barrier_semaphore()
    for delta, m in partners:
        @pl.when(in_range(d + delta))
        def _(delta=delta, m=m):
            pl.semaphore_signal(
                barrier, 1, device_id=(d + delta, (b + m) % nb), device_id_type=MESH
            )
    nd = lax.axis_size("dom")
    has_lower = (d + nd - 1) // nd
    has_upper = (2 * nd - 2 - d) // nd
    peers = [sum(1 for delta, _ in partners if delta == side) for side in (-1, 0, 1)]
    pl.semaphore_wait(barrier, peers[1] + peers[0] * has_lower + peers[2] * has_upper)


def _halo_gather_kernel(x_ref, out_ref, buf, send_sem, recv_sem):
    d, b = lax.axis_index("dom"), lax.axis_index("blk")
    nd, nb = lax.axis_size("dom"), lax.axis_size("blk")
    partners = _halo_partners(nb)

    def in_range(i):
        return (i >= 0) & (i < nd)

    _barrier(partners, in_range, d, b, nb)

    def outgoing(delta, m):
        return pltpu.make_async_remote_copy(
            src_ref=x_ref,
            dst_ref=buf.at[1 - delta, b],
            send_sem=send_sem.at[delta + 1, m],
            recv_sem=recv_sem.at[1 - delta, b],
            device_id=(d + delta, (b + m) % nb),
            device_id_type=MESH,
        )

    for delta, m in partners:
        pl.when(in_range(d + delta))(lambda delta=delta, m=m: outgoing(delta, m).start())
    buf[1, b] = x_ref[...]
    for side in (-1, 1):
        @pl.when(jnp.logical_not(in_range(d + side)))
        def _(side=side):
            buf[1 + side] = jnp.zeros(buf.shape[1:], buf.dtype)
    for delta, m in partners:
        pl.when(in_range(d + delta))(lambda delta=delta, m=m: outgoing(delta, m).wait_send())
    for delta, m in partners:
        p, s = 1 + delta, (b + m) % nb

        @pl.when(in_range(d + delta))
        def _(p=p, s=s):
            pltpu.make_async_remote_copy(
                src_ref=x_ref,
                dst_ref=buf.at[p, s],
                send_sem=send_sem.at[p, 0],
                recv_sem=recv_sem.at[p, s],
                device_id=(d + p - 1, s),
                device_id_type=MESH,
            ).wait_recv()

    out_ref[...] = buf[...]


def _blk_gather_kernel(x_ref, out_ref, buf, send_sem, recv_sem):
    d, b = lax.axis_index("dom"), lax.axis_index("blk")
    nd, nb = lax.axis_size("dom"), lax.axis_size("blk")
    partners = [(0, m) for m in range(1, nb)]
    _barrier(partners, lambda i: (i >= 0) & (i < nd), d, b, nb)

    def outgoing(m):
        return pltpu.make_async_remote_copy(
            src_ref=x_ref,
            dst_ref=buf.at[b],
            send_sem=send_sem.at[m],
            recv_sem=recv_sem.at[b],
            device_id=(d, (b + m) % nb),
            device_id_type=MESH,
        )

    for _, m in partners:
        outgoing(m).start()
    buf[b] = x_ref[...]
    for _, m in partners:
        outgoing(m).wait_send()
    for _, m in partners:
        s = (b + m) % nb
        pltpu.make_async_remote_copy(
            src_ref=x_ref,
            dst_ref=buf.at[s],
            send_sem=send_sem.at[0],
            recv_sem=recv_sem.at[s],
            device_id=(d, s),
            device_id_type=MESH,
        ).wait_recv()
    out_ref[...] = buf[...]


def _node_reduce_kernel(x_ref, out_ref, buf, send_sem, recv_sem):
    d, b = lax.axis_index("dom"), lax.axis_index("blk")
    nd, nb = lax.axis_size("dom"), lax.axis_size("blk")
    partners = _halo_partners(nb)

    def in_range(i):
        return (i >= 0) & (i < nd)

    _barrier(partners, in_range, d, b, nb)

    def outgoing(delta, m):
        p = 1 + delta
        return pltpu.make_async_remote_copy(
            src_ref=x_ref.at[p, (b + m) % nb],
            dst_ref=buf.at[p, b],
            send_sem=send_sem.at[p, m],
            recv_sem=recv_sem.at[p, b],
            device_id=(d + delta, (b + m) % nb),
            device_id_type=MESH,
        )

    for delta, m in partners:
        pl.when(in_range(d + delta))(lambda delta=delta, m=m: outgoing(delta, m).start())
    out_ref[...] = x_ref[1, b]
    for delta, m in partners:
        pl.when(in_range(d + delta))(lambda delta=delta, m=m: outgoing(delta, m).wait_send())
    for delta, m in partners:
        p, s = 1 + delta, (b + m) % nb

        @pl.when(in_range(d - delta))
        def _(p=p, s=s):
            pltpu.make_async_remote_copy(
                src_ref=x_ref.at[p, s],
                dst_ref=buf.at[p, s],
                send_sem=send_sem.at[p, 0],
                recv_sem=recv_sem.at[p, s],
                device_id=(d - delta, s),
                device_id_type=MESH,
            ).wait_recv()
            out_ref[...] += buf[p, s]


def _exchange(kernel, x, out_shape, buf_shape, sem_shape, collective_id):
    return pl.pallas_call(
        kernel,
        out_shape=jax.ShapeDtypeStruct(out_shape, x.dtype),
        in_specs=[pl.BlockSpec(memory_space=pltpu.VMEM)],
        out_specs=pl.BlockSpec(memory_space=pltpu.VMEM),
        scratch_shapes=[
            pltpu.VMEM(buf_shape, x.dtype),
            pltpu.SemaphoreType.DMA(sem_shape),
            pltpu.SemaphoreType.DMA(sem_shape),
        ],
        compiler_params=pltpu.CompilerParams(
            collective_id=collective_id, has_side_effects=True
        ),
    )(x)


def halo_gather(x, nb, collective_id):
    shape = (3, nb) + x.shape
    out = _exchange(_halo_gather_kernel, x, shape, shape, (3, nb), collective_id)
    e, r, c = x.shape
    return jnp.transpose(out, (0, 2, 3, 1, 4)).reshape(3 * e, r, nb * c)


def blk_gather(x, nb, collective_id):
    shape = (nb,) + x.shape
    out = _exchange(_blk_gather_kernel, x, shape, shape, (nb,), collective_id)
    e, r, c = x.shape
    return jnp.transpose(out, (1, 2, 0, 3)).reshape(e, r, nb * c)


def node_reduce(chunks, collective_id):
    nb = chunks.shape[1]
    return _exchange(
        _node_reduce_kernel, chunks, chunks.shape[2:], chunks.shape, (3, nb), collective_id
    )


LANES = 128


def _sweeps_kernel(
    start_ref, shift_ref, target_ref, jac_hbm, inv_hbm, shape_hbm, out_ref, wsum_ref,
    jac_v, inv_ref, shape_ref, select, send_a, halo, send_r, full_r, upd, jac_sem, hs_send, hs_recv, bk_send, bk_recv,
    fw_send, wpart, ws_send, ws_recv,
):
    d, b = lax.axis_index("dom"), lax.axis_index("blk")
    nd, nb = lax.axis_size("dom"), lax.axis_size("blk")
    rows = start_ref.shape[1]
    elems = jac_v.shape[0]
    faces = jac_v.shape[1]

    def in_range(i):
        return (i >= 0) & (i < nd)

    partners = [(0, m) for m in range(1, nb)] + [(-1, 0), (1, 0)]
    _barrier(partners, in_range, d, b, nb)
    jac_copy = pltpu.make_async_copy(jac_hbm, jac_v, jac_sem.at[0])
    inv_copy = pltpu.make_async_copy(inv_hbm, inv_ref, jac_sem.at[1])
    shape_copy = pltpu.make_async_copy(shape_hbm, shape_ref, jac_sem.at[2])
    jac_copy.start()
    inv_copy.start()
    shape_copy.start()
    lane = lax.broadcasted_iota(jnp.int32, (rows, LANES), 1)
    cand_row = lax.broadcasted_iota(jnp.int32, (3 * LANES, LANES), 0)
    for k in range(faces):
        select[k] = (cand_row == target_ref[pl.ds(k, 1), :]).astype(jnp.bfloat16)

    def row_block(i):
        return pl.ds(pl.multiple_of(i * rows, 16), rows)

    own_rows = row_block(b)
    adjoint = start_ref[0]
    for sweep in range(SWEEPS):
        send_a[sweep] = adjoint.astype(jnp.bfloat16)

        def direct(delta, m, sweep=sweep):
            return pltpu.make_async_remote_copy(
                src_ref=send_a.at[sweep],
                dst_ref=halo.at[sweep, 1 - delta, own_rows],
                send_sem=hs_send.at[sweep, delta + 1, m],
                recv_sem=hs_recv.at[sweep, 1 - delta, b],
                device_id=(d + delta, (b + m) % nb),
                device_id_type=MESH,
            )

        def forward(p, m, sweep=sweep):
            return pltpu.make_async_remote_copy(
                src_ref=halo.at[sweep, p, own_rows],
                dst_ref=halo.at[sweep, p, own_rows],
                send_sem=fw_send.at[sweep, p // 2, m],
                recv_sem=hs_recv.at[sweep, p, b],
                device_id=(d, (b + m) % nb),
                device_id_type=MESH,
            )

        def arrival(p, src_b, sweep=sweep):
            return pltpu.make_async_remote_copy(
                src_ref=send_a.at[sweep],
                dst_ref=halo.at[sweep, p, row_block(src_b)],
                send_sem=hs_send.at[sweep, p, 0],
                recv_sem=hs_recv.at[sweep, p, src_b],
                device_id=(d, src_b),
                device_id_type=MESH,
            )

        for delta, m in partners:
            pl.when(in_range(d + delta))(lambda delta=delta, m=m: direct(delta, m).start())
        halo[sweep, 1, own_rows] = send_a[sweep]
        for side in (-1, 1):
            @pl.when(jnp.logical_not(in_range(d + side)))
            def _(side=side, sweep=sweep):
                halo[sweep, 1 + side] = jnp.zeros(halo.shape[2:], halo.dtype)
        for side in (-1, 1):
            p = 1 + side

            @pl.when(in_range(d + side))
            def _(p=p):
                arrival(p, b).wait_recv()
                for m in range(1, nb):
                    forward(p, m).start()
        for delta, m in partners:
            pl.when(in_range(d + delta))(lambda delta=delta, m=m: direct(delta, m).wait_send())
        for m in range(1, nb):
            arrival(1, (b + m) % nb).wait_recv()
        for side in (-1, 1):
            p = 1 + side

            @pl.when(in_range(d + side))
            def _(p=p):
                for m in range(1, nb):
                    forward(p, m).wait_send()
                for m in range(1, nb):
                    arrival(p, (b + m) % nb).wait_recv()

        candidates = jnp.concatenate([halo[sweep, p] for p in range(3)], axis=1)
        if sweep == 0:
            jac_copy.wait()
        acc = jnp.zeros((elems * rows, LANES), jnp.float32)
        for k in range(faces):
            picked = jnp.dot(candidates, select[k], preferred_element_type=jnp.float32)
            acc = acc + jnp.dot(
                jac_v[:, k].reshape(elems * rows, -1),
                picked.astype(jnp.bfloat16),
                preferred_element_type=jnp.float32,
            )
        upd[...] = acc.reshape(upd.shape)
        product = jnp.zeros((rows, LANES), jnp.float32)
        for e in range(elems):
            mine = (lane >= RHS * e) & (lane < RHS * e + RHS)
            product = product + jnp.where(mine, upd[e], 0.0)
        image = shift_ref[...] * adjoint + product
        send_r[sweep] = (start_ref[1] - image).astype(jnp.bfloat16)

        def blk_copy(m, sweep=sweep):
            return pltpu.make_async_remote_copy(
                src_ref=send_r.at[sweep],
                dst_ref=full_r.at[sweep, own_rows],
                send_sem=bk_send.at[sweep, m],
                recv_sem=bk_recv.at[sweep, b],
                device_id=(d, (b + m) % nb),
                device_id_type=MESH,
            )

        for m in range(1, nb):
            blk_copy(m).start()
        full_r[sweep, own_rows] = send_r[sweep]
        for m in range(1, nb):
            blk_copy(m).wait_send()
        for m in range(1, nb):
            src_b = (b + m) % nb
            pltpu.make_async_remote_copy(
                src_ref=send_r.at[sweep],
                dst_ref=full_r.at[sweep, pl.ds(pl.multiple_of(src_b * rows, 16), rows)],
                send_sem=bk_send.at[sweep, 0],
                recv_sem=bk_recv.at[sweep, src_b],
                device_id=(d, src_b),
                device_id_type=MESH,
            ).wait_recv()
        if sweep == 0:
            inv_copy.wait()
        upd[...] = jnp.dot(
            inv_ref[...], full_r[sweep], preferred_element_type=jnp.float32
        ).reshape(upd.shape)
        update = jnp.zeros((rows, LANES), jnp.float32)
        for e in range(elems):
            mine = (lane >= RHS * e) & (lane < RHS * e + RHS)
            update = update + jnp.where(mine, upd[e], 0.0)
        adjoint = adjoint + update
    out_ref[...] = adjoint

    square = jnp.concatenate([adjoint, jnp.zeros((LANES - rows, LANES), jnp.float32)], axis=0)
    final_f32 = jnp.transpose(square)[:, :rows]
    window = 16
    row = lax.broadcasted_iota(jnp.int32, (window, shape_ref.shape[2]), 0)
    wpart[pl.ds(0, LANES)] = jnp.zeros((LANES, shape_ref.shape[2]), jnp.float32)
    shape_copy.wait()
    for e in range(elems):
        low = (RHS * e) // 8 * 8
        part = jnp.dot(
            final_f32[low:low + window].astype(jnp.bfloat16),
            shape_ref[e],
            preferred_element_type=jnp.float32,
        )
        mine = (row + low >= RHS * e) & (row + low < RHS * e + RHS)
        wpart[pl.ds(low, window)] = wpart[pl.ds(low, window)] - jnp.where(mine, part, 0.0)
    chunk = wsum_ref.shape[0]
    owners = pl.cdiv(elems * RHS, chunk)

    def wcopy(c, src_b):
        return pltpu.make_async_remote_copy(
            src_ref=wpart.at[pl.ds(c * chunk, chunk)],
            dst_ref=wpart.at[pl.ds(LANES + src_b * chunk, chunk)],
            send_sem=ws_send.at[c],
            recv_sem=ws_recv.at[src_b],
            device_id=(d, c),
            device_id_type=MESH,
        )

    for m in range(1, nb):
        c = (b + m) % nb
        pl.when(c < owners)(lambda c=c: wcopy(c, b).start())
    for m in range(1, nb):
        c = (b + m) % nb
        pl.when(c < owners)(lambda c=c: wcopy(c, b).wait_send())
    total = jnp.zeros(wsum_ref.shape, jnp.float32)
    for m in range(1, nb):
        src_b = (b + m) % nb

        @pl.when(b < owners)
        def _(src_b=src_b):
            wcopy(b, src_b).wait_recv()

    @pl.when(b < owners)
    def _():
        acc = wpart[pl.ds(pl.multiple_of(b * chunk, 8), chunk)]
        for m in range(1, nb):
            src_b = (b + m) % nb
            acc = acc + wpart[pl.ds(pl.multiple_of(LANES + src_b * chunk, 8), chunk)]
        wsum_ref[...] = acc

    @pl.when(b >= owners)
    def _():
        wsum_ref[...] = jnp.zeros(wsum_ref.shape, jnp.float32)


def sweeps(adjoint_start, right_sides, pseudo_shift, slots, jac_blocks, block_inverse,
           shape_partials, nb):
    elems, rhs, rows = adjoint_start.shape
    cols = jac_blocks.shape[-1]
    faces = jac_blocks.shape[1]

    def transposed(x):
        x = jnp.transpose(x, (0, 3, 1, 2)).reshape(x.shape[0], rows, elems * rhs)
        return jnp.pad(x, ((0, 0), (0, 0), (0, LANES - elems * rhs)))

    shift = jnp.pad(jnp.repeat(pseudo_shift, rhs), (0, LANES - elems * rhs))[None, :]
    part, within = slots // elems, slots % elems
    lanes = (part * LANES + within * rhs)[:, :, None] + jnp.arange(rhs, dtype=jnp.int32)
    target = jnp.transpose(lanes, (1, 0, 2)).reshape(faces, elems * rhs)
    target = jnp.pad(target, ((0, 8 - faces), (0, LANES - elems * rhs)), constant_values=-1)
    vmem = pl.BlockSpec(memory_space=pltpu.VMEM)
    hbm = pl.BlockSpec(memory_space=pl.ANY)
    chunk = 8 * rhs
    out, wsum = pl.pallas_call(
        _sweeps_kernel,
        out_shape=(
            jax.ShapeDtypeStruct((rows, LANES), jnp.float32),
            jax.ShapeDtypeStruct((chunk, shape_partials.shape[2]), jnp.float32),
        ),
        in_specs=[vmem, vmem, vmem, hbm, hbm, hbm],
        out_specs=(vmem, vmem),
        scratch_shapes=[
            pltpu.VMEM((elems, faces, rows, cols), jnp.bfloat16),
            pltpu.VMEM((elems * rows, cols), jnp.bfloat16),
            pltpu.VMEM(shape_partials.shape, shape_partials.dtype),
            pltpu.VMEM((faces, 3 * LANES, LANES), jnp.bfloat16),
            pltpu.VMEM((SWEEPS, rows, LANES), jnp.bfloat16),
            pltpu.VMEM((SWEEPS, 3, nb * rows, LANES), jnp.bfloat16),
            pltpu.VMEM((SWEEPS, rows, LANES), jnp.bfloat16),
            pltpu.VMEM((SWEEPS, nb * rows, LANES), jnp.bfloat16),
            pltpu.VMEM((elems, rows, LANES), jnp.float32),
            pltpu.SemaphoreType.DMA((3,)),
            pltpu.SemaphoreType.DMA((SWEEPS, 3, nb)),
            pltpu.SemaphoreType.DMA((SWEEPS, 3, nb)),
            pltpu.SemaphoreType.DMA((SWEEPS, nb)),
            pltpu.SemaphoreType.DMA((SWEEPS, nb)),
            pltpu.SemaphoreType.DMA((SWEEPS, 2, nb)),
            pltpu.VMEM((LANES + nb * chunk, shape_partials.shape[2]), jnp.float32),
            pltpu.SemaphoreType.DMA((nb,)),
            pltpu.SemaphoreType.DMA((nb,)),
        ],
        compiler_params=pltpu.CompilerParams(
            collective_id=0, has_side_effects=True, vmem_limit_bytes=67043328
        ),
    )(
        transposed(jnp.stack([adjoint_start, right_sides])),
        shift,
        target,
        jac_blocks,
        block_inverse.reshape(elems * rows, cols),
        shape_partials,
    )
    adjoint = jnp.transpose(out[:, : elems * rhs].reshape(rows, elems, rhs), (1, 2, 0))
    return adjoint, wsum


def local(
    adjoint_start,
    right_sides,
    jac_blocks,
    block_inverse,
    neighbours,
    pseudo_shift,
    shape_partials,
    node_ids,
):
    local_count = neighbours.shape[0]
    nb = lax.axis_size("blk")
    part_index = lax.axis_index("dom")
    own = jnp.arange(local_count, dtype=jnp.int32)[:, None] + local_count
    slots = jnp.concatenate([own, neighbours - (part_index - 1) * local_count], axis=1)
    adjoint, wsum = sweeps(
        adjoint_start, right_sides, pseudo_shift, slots, jac_blocks, block_inverse,
        shape_partials, nb,
    )
    node_width = node_ids.shape[1]
    chunk_elems = wsum.shape[0] // RHS
    values = wsum.reshape(chunk_elems, RHS, node_width, 3)
    values = jnp.transpose(values, (0, 2, 1, 3)).reshape(chunk_elems * node_width, RHS * 3)
    my_nodes = lax.dynamic_slice_in_dim(
        node_ids, jnp.minimum(lax.axis_index("blk") * chunk_elems, local_count - chunk_elems),
        chunk_elems,
    )
    node_slots = (my_nodes - (part_index - 1) * NODE_DEV).reshape(-1)
    partial_sums = jax.ops.segment_sum(values, node_slots, 3 * NODE_DEV).T
    chunks = jnp.transpose(
        partial_sums.reshape(RHS * 3, 3, nb, NODE_DEV // nb), (1, 2, 0, 3)
    )
    shape_gradient = node_reduce(chunks, collective_id=1)
    return (adjoint, shape_gradient)


def solution(mesh):
    in_specs = (
        P("dom", None, "blk"),
        P("dom", None, "blk"),
        P("dom", None, "blk", None),
        P("dom", "blk", None),
        P("dom", None),
        P("dom"),
        P("dom", "blk", None),
        P("dom", None),
    )
    out_specs = (P("dom", None, "blk"), P(None, ("dom", "blk")))
    return jax.shard_map(local, mesh=mesh, in_specs=in_specs, out_specs=out_specs, check_vma=False)
```

```python
import functools

import jax
import jax.numpy as jnp
from jax import lax
from jax.experimental import pallas as pl
from jax.experimental.pallas import tpu as pltpu
from jax.sharding import PartitionSpec as P

RHS = 3
SWEEPS = 2
NODE_DEV = 768
MESH = pl.DeviceIdType.MESH


def _halo_partners(nb):
    return [(delta, m) for delta in (-1, 0, 1) for m in range(nb) if (delta, m) != (0, 0)]


def _barrier(partners, in_range, d, b, nb):
    barrier = pltpu.get_barrier_semaphore()
    for delta, m in partners:
        @pl.when(in_range(d + delta))
        def _(delta=delta, m=m):
            pl.semaphore_signal(
                barrier, 1, device_id=(d + delta, (b + m) % nb), device_id_type=MESH
            )
    nd = lax.axis_size("dom")
    has_lower = (d + nd - 1) // nd
    has_upper = (2 * nd - 2 - d) // nd
    peers = [sum(1 for delta, _ in partners if delta == side) for side in (-1, 0, 1)]
    pl.semaphore_wait(barrier, peers[1] + peers[0] * has_lower + peers[2] * has_upper)


def _halo_gather_kernel(x_ref, out_ref, buf, send_sem, recv_sem):
    d, b = lax.axis_index("dom"), lax.axis_index("blk")
    nd, nb = lax.axis_size("dom"), lax.axis_size("blk")
    partners = _halo_partners(nb)

    def in_range(i):
        return (i >= 0) & (i < nd)

    _barrier(partners, in_range, d, b, nb)

    def outgoing(delta, m):
        return pltpu.make_async_remote_copy(
            src_ref=x_ref,
            dst_ref=buf.at[1 - delta, b],
            send_sem=send_sem.at[delta + 1, m],
            recv_sem=recv_sem.at[1 - delta, b],
            device_id=(d + delta, (b + m) % nb),
            device_id_type=MESH,
        )

    for delta, m in partners:
        pl.when(in_range(d + delta))(lambda delta=delta, m=m: outgoing(delta, m).start())
    buf[1, b] = x_ref[...]
    for side in (-1, 1):
        @pl.when(jnp.logical_not(in_range(d + side)))
        def _(side=side):
            buf[1 + side] = jnp.zeros(buf.shape[1:], buf.dtype)
    for delta, m in partners:
        pl.when(in_range(d + delta))(lambda delta=delta, m=m: outgoing(delta, m).wait_send())
    for delta, m in partners:
        p, s = 1 + delta, (b + m) % nb

        @pl.when(in_range(d + delta))
        def _(p=p, s=s):
            pltpu.make_async_remote_copy(
                src_ref=x_ref,
                dst_ref=buf.at[p, s],
                send_sem=send_sem.at[p, 0],
                recv_sem=recv_sem.at[p, s],
                device_id=(d + p - 1, s),
                device_id_type=MESH,
            ).wait_recv()

    out_ref[...] = buf[...]


def _blk_gather_kernel(x_ref, out_ref, buf, send_sem, recv_sem):
    d, b = lax.axis_index("dom"), lax.axis_index("blk")
    nd, nb = lax.axis_size("dom"), lax.axis_size("blk")
    partners = [(0, m) for m in range(1, nb)]
    _barrier(partners, lambda i: (i >= 0) & (i < nd), d, b, nb)

    def outgoing(m):
        return pltpu.make_async_remote_copy(
            src_ref=x_ref,
            dst_ref=buf.at[b],
            send_sem=send_sem.at[m],
            recv_sem=recv_sem.at[b],
            device_id=(d, (b + m) % nb),
            device_id_type=MESH,
        )

    for _, m in partners:
        outgoing(m).start()
    buf[b] = x_ref[...]
    for _, m in partners:
        outgoing(m).wait_send()
    for _, m in partners:
        s = (b + m) % nb
        pltpu.make_async_remote_copy(
            src_ref=x_ref,
            dst_ref=buf.at[s],
            send_sem=send_sem.at[0],
            recv_sem=recv_sem.at[s],
            device_id=(d, s),
            device_id_type=MESH,
        ).wait_recv()
    out_ref[...] = buf[...]


def _node_reduce_kernel(x_ref, out_ref, buf, send_sem, recv_sem):
    d, b = lax.axis_index("dom"), lax.axis_index("blk")
    nd, nb = lax.axis_size("dom"), lax.axis_size("blk")
    partners = _halo_partners(nb)

    def in_range(i):
        return (i >= 0) & (i < nd)

    _barrier(partners, in_range, d, b, nb)

    def outgoing(delta, m):
        p = 1 + delta
        return pltpu.make_async_remote_copy(
            src_ref=x_ref.at[p, (b + m) % nb],
            dst_ref=buf.at[p, b],
            send_sem=send_sem.at[p, m],
            recv_sem=recv_sem.at[p, b],
            device_id=(d + delta, (b + m) % nb),
            device_id_type=MESH,
        )

    for delta, m in partners:
        pl.when(in_range(d + delta))(lambda delta=delta, m=m: outgoing(delta, m).start())
    out_ref[...] = x_ref[1, b]
    for delta, m in partners:
        pl.when(in_range(d + delta))(lambda delta=delta, m=m: outgoing(delta, m).wait_send())
    for delta, m in partners:
        p, s = 1 + delta, (b + m) % nb

        @pl.when(in_range(d - delta))
        def _(p=p, s=s):
            pltpu.make_async_remote_copy(
                src_ref=x_ref.at[p, s],
                dst_ref=buf.at[p, s],
                send_sem=send_sem.at[p, 0],
                recv_sem=recv_sem.at[p, s],
                device_id=(d - delta, s),
                device_id_type=MESH,
            ).wait_recv()
            out_ref[...] += buf[p, s]


def _exchange(kernel, x, out_shape, buf_shape, sem_shape, collective_id):
    return pl.pallas_call(
        kernel,
        out_shape=jax.ShapeDtypeStruct(out_shape, x.dtype),
        in_specs=[pl.BlockSpec(memory_space=pltpu.VMEM)],
        out_specs=pl.BlockSpec(memory_space=pltpu.VMEM),
        scratch_shapes=[
            pltpu.VMEM(buf_shape, x.dtype),
            pltpu.SemaphoreType.DMA(sem_shape),
            pltpu.SemaphoreType.DMA(sem_shape),
        ],
        compiler_params=pltpu.CompilerParams(
            collective_id=collective_id, has_side_effects=True
        ),
    )(x)


def halo_gather(x, nb, collective_id):
    shape = (3, nb) + x.shape
    out = _exchange(_halo_gather_kernel, x, shape, shape, (3, nb), collective_id)
    e, r, c = x.shape
    return jnp.transpose(out, (0, 2, 3, 1, 4)).reshape(3 * e, r, nb * c)


def blk_gather(x, nb, collective_id):
    shape = (nb,) + x.shape
    out = _exchange(_blk_gather_kernel, x, shape, shape, (nb,), collective_id)
    e, r, c = x.shape
    return jnp.transpose(out, (1, 2, 0, 3)).reshape(e, r, nb * c)


def node_reduce(chunks, collective_id):
    nb = chunks.shape[1]
    return _exchange(
        _node_reduce_kernel, chunks, chunks.shape[2:], chunks.shape, (3, nb), collective_id
    )


LANES = 128


def _sweeps_kernel(
    start_ref, target_ref, jac_hbm, inv_ref, shape_ref, out_ref, wsum_ref,
    jac_v, select, send_a, halo, send_r, full_r, upd, jac_sem, hs_send, hs_recv, bk_send, bk_recv,
    fw_send, wpart, ws_send, ws_recv,
):
    d, b = lax.axis_index("dom"), lax.axis_index("blk")
    nd, nb = lax.axis_size("dom"), lax.axis_size("blk")
    rows = start_ref.shape[1]
    elems = jac_v.shape[0]
    faces = jac_v.shape[1]

    def in_range(i):
        return (i >= 0) & (i < nd)

    partners = [(0, m) for m in range(1, nb)] + [(-1, 0), (1, 0)]
    _barrier(partners, in_range, d, b, nb)
    jac_copy = pltpu.make_async_copy(jac_hbm, jac_v, jac_sem)
    jac_copy.start()
    lane = lax.broadcasted_iota(jnp.int32, (rows, LANES), 1)
    cand_row = lax.broadcasted_iota(jnp.int32, (3 * LANES, LANES), 0)
    for k in range(faces):
        select[k] = (cand_row == target_ref[pl.ds(k, 1), :]).astype(jnp.bfloat16)

    def row_block(i):
        return pl.ds(pl.multiple_of(i * rows, 16), rows)

    own_rows = row_block(b)
    adjoint = start_ref[0]
    for sweep in range(SWEEPS):
        send_a[sweep] = adjoint.astype(jnp.bfloat16)

        def direct(delta, m, sweep=sweep):
            return pltpu.make_async_remote_copy(
                src_ref=send_a.at[sweep],
                dst_ref=halo.at[sweep, 1 - delta, own_rows],
                send_sem=hs_send.at[sweep, delta + 1, m],
                recv_sem=hs_recv.at[sweep, 1 - delta, b],
                device_id=(d + delta, (b + m) % nb),
                device_id_type=MESH,
            )

        def forward(p, m, sweep=sweep):
            return pltpu.make_async_remote_copy(
                src_ref=halo.at[sweep, p, own_rows],
                dst_ref=halo.at[sweep, p, own_rows],
                send_sem=fw_send.at[sweep, p // 2, m],
                recv_sem=hs_recv.at[sweep, p, b],
                device_id=(d, (b + m) % nb),
                device_id_type=MESH,
            )

        def arrival(p, src_b, sweep=sweep):
            return pltpu.make_async_remote_copy(
                src_ref=send_a.at[sweep],
                dst_ref=halo.at[sweep, p, row_block(src_b)],
                send_sem=hs_send.at[sweep, p, 0],
                recv_sem=hs_recv.at[sweep, p, src_b],
                device_id=(d, src_b),
                device_id_type=MESH,
            )

        for delta, m in partners:
            pl.when(in_range(d + delta))(lambda delta=delta, m=m: direct(delta, m).start())
        halo[sweep, 1, own_rows] = send_a[sweep]
        for side in (-1, 1):
            @pl.when(jnp.logical_not(in_range(d + side)))
            def _(side=side, sweep=sweep):
                halo[sweep, 1 + side] = jnp.zeros(halo.shape[2:], halo.dtype)
        for side in (-1, 1):
            p = 1 + side

            @pl.when(in_range(d + side))
            def _(p=p):
                arrival(p, b).wait_recv()
                for m in range(1, nb):
                    forward(p, m).start()
        for delta, m in partners:
            pl.when(in_range(d + delta))(lambda delta=delta, m=m: direct(delta, m).wait_send())
        for m in range(1, nb):
            arrival(1, (b + m) % nb).wait_recv()
        for side in (-1, 1):
            p = 1 + side

            @pl.when(in_range(d + side))
            def _(p=p):
                for m in range(1, nb):
                    forward(p, m).wait_send()
                for m in range(1, nb):
                    arrival(p, (b + m) % nb).wait_recv()

        candidates = jnp.concatenate([halo[sweep, p] for p in range(3)], axis=1)
        if sweep == 0:
            jac_copy.wait()
        acc = jnp.zeros((elems * rows, LANES), jnp.float32)
        for k in range(faces):
            picked = jnp.dot(candidates, select[k], preferred_element_type=jnp.float32)
            acc = acc + jnp.dot(
                jac_v[:, k].reshape(elems * rows, -1),
                picked.astype(jnp.bfloat16),
                preferred_element_type=jnp.float32,
            )
        upd[...] = acc.reshape(upd.shape)
        product = jnp.zeros((rows, LANES), jnp.float32)
        for e in range(elems):
            mine = (lane >= RHS * e) & (lane < RHS * e + RHS)
            product = product + jnp.where(mine, upd[e], 0.0)
        image = start_ref[2] * adjoint + product
        send_r[sweep] = (start_ref[1] - image).astype(jnp.bfloat16)

        def blk_copy(m, sweep=sweep):
            return pltpu.make_async_remote_copy(
                src_ref=send_r.at[sweep],
                dst_ref=full_r.at[sweep, own_rows],
                send_sem=bk_send.at[sweep, m],
                recv_sem=bk_recv.at[sweep, b],
                device_id=(d, (b + m) % nb),
                device_id_type=MESH,
            )

        for m in range(1, nb):
            blk_copy(m).start()
        full_r[sweep, own_rows] = send_r[sweep]
        for m in range(1, nb):
            blk_copy(m).wait_send()
        for m in range(1, nb):
            src_b = (b + m) % nb
            pltpu.make_async_remote_copy(
                src_ref=send_r.at[sweep],
                dst_ref=full_r.at[sweep, pl.ds(pl.multiple_of(src_b * rows, 16), rows)],
                send_sem=bk_send.at[sweep, 0],
                recv_sem=bk_recv.at[sweep, src_b],
                device_id=(d, src_b),
                device_id_type=MESH,
            ).wait_recv()
        upd[...] = jnp.dot(
            inv_ref[...], full_r[sweep], preferred_element_type=jnp.float32
        ).reshape(upd.shape)
        update = jnp.zeros((rows, LANES), jnp.float32)
        for e in range(elems):
            mine = (lane >= RHS * e) & (lane < RHS * e + RHS)
            update = update + jnp.where(mine, upd[e], 0.0)
        adjoint = adjoint + update
    out_ref[...] = adjoint

    square = jnp.concatenate([adjoint, jnp.zeros((LANES - rows, LANES), jnp.float32)], axis=0)
    final_half = jnp.transpose(square)[:, :rows].astype(jnp.bfloat16)
    row = lax.broadcasted_iota(jnp.int32, (LANES, shape_ref.shape[2]), 0)
    weighted = jnp.zeros((LANES, shape_ref.shape[2]), jnp.float32)
    for e in range(elems):
        part = jnp.dot(final_half, shape_ref[e], preferred_element_type=jnp.float32)
        weighted = weighted + jnp.where((row >= RHS * e) & (row < RHS * e + RHS), part, 0.0)
    wpart[pl.ds(0, LANES)] = -weighted
    chunk = wsum_ref.shape[0]
    owners = pl.cdiv(elems * RHS, chunk)

    def wcopy(c, src_b):
        return pltpu.make_async_remote_copy(
            src_ref=wpart.at[pl.ds(c * chunk, chunk)],
            dst_ref=wpart.at[pl.ds(LANES + src_b * chunk, chunk)],
            send_sem=ws_send.at[c],
            recv_sem=ws_recv.at[src_b],
            device_id=(d, c),
            device_id_type=MESH,
        )

    for m in range(1, nb):
        c = (b + m) % nb
        pl.when(c < owners)(lambda c=c: wcopy(c, b).start())
    for m in range(1, nb):
        c = (b + m) % nb
        pl.when(c < owners)(lambda c=c: wcopy(c, b).wait_send())
    total = jnp.zeros(wsum_ref.shape, jnp.float32)
    for m in range(1, nb):
        src_b = (b + m) % nb

        @pl.when(b < owners)
        def _(src_b=src_b):
            wcopy(b, src_b).wait_recv()

    @pl.when(b < owners)
    def _():
        acc = wpart[pl.ds(pl.multiple_of(b * chunk, 8), chunk)]
        for m in range(1, nb):
            src_b = (b + m) % nb
            acc = acc + wpart[pl.ds(pl.multiple_of(LANES + src_b * chunk, 8), chunk)]
        wsum_ref[...] = acc

    @pl.when(b >= owners)
    def _():
        wsum_ref[...] = jnp.zeros(wsum_ref.shape, jnp.float32)


def sweeps(adjoint_start, right_sides, pseudo_shift, slots, jac_blocks, block_inverse,
           shape_partials, nb):
    elems, rhs, rows = adjoint_start.shape
    cols = jac_blocks.shape[-1]
    faces = jac_blocks.shape[1]

    stacked = jnp.stack([
        adjoint_start,
        right_sides,
        jnp.broadcast_to(pseudo_shift[:, None, None], adjoint_start.shape),
    ])
    stacked = jnp.transpose(stacked, (0, 3, 1, 2)).reshape(3, rows, elems * rhs)
    stacked = jnp.pad(stacked, ((0, 0), (0, 0), (0, LANES - elems * rhs)))
    part, within = slots // elems, slots % elems
    lanes = (part * LANES + within * rhs)[:, :, None] + jnp.arange(rhs, dtype=jnp.int32)
    target = jnp.transpose(lanes, (1, 0, 2)).reshape(faces, elems * rhs)
    target = jnp.pad(target, ((0, 8 - faces), (0, LANES - elems * rhs)), constant_values=-1)
    vmem = pl.BlockSpec(memory_space=pltpu.VMEM)
    chunk = 8 * rhs
    out, wsum = pl.pallas_call(
        _sweeps_kernel,
        out_shape=(
            jax.ShapeDtypeStruct((rows, LANES), jnp.float32),
            jax.ShapeDtypeStruct((chunk, shape_partials.shape[2]), jnp.float32),
        ),
        in_specs=[vmem, vmem, pl.BlockSpec(memory_space=pl.ANY), vmem, vmem],
        out_specs=(vmem, vmem),
        scratch_shapes=[
            pltpu.VMEM((elems, faces, rows, cols), jnp.bfloat16),
            pltpu.VMEM((faces, 3 * LANES, LANES), jnp.bfloat16),
            pltpu.VMEM((SWEEPS, rows, LANES), jnp.bfloat16),
            pltpu.VMEM((SWEEPS, 3, nb * rows, LANES), jnp.bfloat16),
            pltpu.VMEM((SWEEPS, rows, LANES), jnp.bfloat16),
            pltpu.VMEM((SWEEPS, nb * rows, LANES), jnp.bfloat16),
            pltpu.VMEM((elems, rows, LANES), jnp.float32),
            pltpu.SemaphoreType.DMA(()),
            pltpu.SemaphoreType.DMA((SWEEPS, 3, nb)),
            pltpu.SemaphoreType.DMA((SWEEPS, 3, nb)),
            pltpu.SemaphoreType.DMA((SWEEPS, nb)),
            pltpu.SemaphoreType.DMA((SWEEPS, nb)),
            pltpu.SemaphoreType.DMA((SWEEPS, 2, nb)),
            pltpu.VMEM((LANES + nb * chunk, shape_partials.shape[2]), jnp.float32),
            pltpu.SemaphoreType.DMA((nb,)),
            pltpu.SemaphoreType.DMA((nb,)),
        ],
        compiler_params=pltpu.CompilerParams(
            collective_id=0, has_side_effects=True, vmem_limit_bytes=48 * 1024 * 1024
        ),
    )(
        stacked,
        target,
        jac_blocks,
        block_inverse.reshape(elems * rows, cols),
        shape_partials,
    )
    adjoint = jnp.transpose(out[:, : elems * rhs].reshape(rows, elems, rhs), (1, 2, 0))
    return adjoint, wsum


def local(
    adjoint_start,
    right_sides,
    jac_blocks,
    block_inverse,
    neighbours,
    pseudo_shift,
    shape_partials,
    node_ids,
):
    local_count = neighbours.shape[0]
    nb = lax.axis_size("blk")
    part_index = lax.axis_index("dom")
    own = jnp.arange(local_count, dtype=jnp.int32)[:, None] + local_count
    slots = jnp.concatenate([own, neighbours - (part_index - 1) * local_count], axis=1)
    adjoint, wsum = sweeps(
        adjoint_start, right_sides, pseudo_shift, slots, jac_blocks, block_inverse,
        shape_partials, nb,
    )
    node_width = node_ids.shape[1]
    chunk_elems = wsum.shape[0] // RHS
    values = wsum.reshape(chunk_elems, RHS, node_width, 3)
    values = jnp.transpose(values, (0, 2, 1, 3)).reshape(chunk_elems * node_width, RHS * 3)
    my_nodes = lax.dynamic_slice_in_dim(
        node_ids, jnp.minimum(lax.axis_index("blk") * chunk_elems, local_count - chunk_elems),
        chunk_elems,
    )
    node_slots = (my_nodes - (part_index - 1) * NODE_DEV).reshape(-1)
    partial_sums = jax.ops.segment_sum(values, node_slots, 3 * NODE_DEV).T
    chunks = jnp.transpose(
        partial_sums.reshape(RHS * 3, 3, nb, NODE_DEV // nb), (1, 2, 0, 3)
    )
    shape_gradient = node_reduce(chunks, collective_id=1)
    return (adjoint, shape_gradient)


def solution(mesh):
    in_specs = (
        P("dom", None, "blk"),
        P("dom", None, "blk"),
        P("dom", None, "blk", None),
        P("dom", "blk", None),
        P("dom", None),
        P("dom"),
        P("dom", "blk", None),
        P("dom", None),
    )
    out_specs = (P("dom", None, "blk"), P(None, ("dom", "blk")))
    return jax.shard_map(local, mesh=mesh, in_specs=in_specs, out_specs=out_specs, check_vma=False)
```

```python
import functools

import jax
import jax.numpy as jnp
from jax import lax
from jax.experimental import pallas as pl
from jax.experimental.pallas import tpu as pltpu
from jax.sharding import PartitionSpec as P

RHS = 3
SWEEPS = 2
NODE_DEV = 768
MESH = pl.DeviceIdType.MESH


def _halo_partners(nb):
    return [(delta, m) for delta in (-1, 0, 1) for m in range(nb) if (delta, m) != (0, 0)]


def _barrier(partners, in_range, d, b, nb):
    barrier = pltpu.get_barrier_semaphore()
    for delta, m in partners:
        @pl.when(in_range(d + delta))
        def _(delta=delta, m=m):
            pl.semaphore_signal(
                barrier, 1, device_id=(d + delta, (b + m) % nb), device_id_type=MESH
            )
    nd = lax.axis_size("dom")
    has_lower = (d + nd - 1) // nd
    has_upper = (2 * nd - 2 - d) // nd
    peers = [sum(1 for delta, _ in partners if delta == side) for side in (-1, 0, 1)]
    pl.semaphore_wait(barrier, peers[1] + peers[0] * has_lower + peers[2] * has_upper)


def _halo_gather_kernel(x_ref, out_ref, buf, send_sem, recv_sem):
    d, b = lax.axis_index("dom"), lax.axis_index("blk")
    nd, nb = lax.axis_size("dom"), lax.axis_size("blk")
    partners = _halo_partners(nb)

    def in_range(i):
        return (i >= 0) & (i < nd)

    _barrier(partners, in_range, d, b, nb)

    def outgoing(delta, m):
        return pltpu.make_async_remote_copy(
            src_ref=x_ref,
            dst_ref=buf.at[1 - delta, b],
            send_sem=send_sem.at[delta + 1, m],
            recv_sem=recv_sem.at[1 - delta, b],
            device_id=(d + delta, (b + m) % nb),
            device_id_type=MESH,
        )

    for delta, m in partners:
        pl.when(in_range(d + delta))(lambda delta=delta, m=m: outgoing(delta, m).start())
    buf[1, b] = x_ref[...]
    for side in (-1, 1):
        @pl.when(jnp.logical_not(in_range(d + side)))
        def _(side=side):
            buf[1 + side] = jnp.zeros(buf.shape[1:], buf.dtype)
    for delta, m in partners:
        pl.when(in_range(d + delta))(lambda delta=delta, m=m: outgoing(delta, m).wait_send())
    for delta, m in partners:
        p, s = 1 + delta, (b + m) % nb

        @pl.when(in_range(d + delta))
        def _(p=p, s=s):
            pltpu.make_async_remote_copy(
                src_ref=x_ref,
                dst_ref=buf.at[p, s],
                send_sem=send_sem.at[p, 0],
                recv_sem=recv_sem.at[p, s],
                device_id=(d + p - 1, s),
                device_id_type=MESH,
            ).wait_recv()

    out_ref[...] = buf[...]


def _blk_gather_kernel(x_ref, out_ref, buf, send_sem, recv_sem):
    d, b = lax.axis_index("dom"), lax.axis_index("blk")
    nd, nb = lax.axis_size("dom"), lax.axis_size("blk")
    partners = [(0, m) for m in range(1, nb)]
    _barrier(partners, lambda i: (i >= 0) & (i < nd), d, b, nb)

    def outgoing(m):
        return pltpu.make_async_remote_copy(
            src_ref=x_ref,
            dst_ref=buf.at[b],
            send_sem=send_sem.at[m],
            recv_sem=recv_sem.at[b],
            device_id=(d, (b + m) % nb),
            device_id_type=MESH,
        )

    for _, m in partners:
        outgoing(m).start()
    buf[b] = x_ref[...]
    for _, m in partners:
        outgoing(m).wait_send()
    for _, m in partners:
        s = (b + m) % nb
        pltpu.make_async_remote_copy(
            src_ref=x_ref,
            dst_ref=buf.at[s],
            send_sem=send_sem.at[0],
            recv_sem=recv_sem.at[s],
            device_id=(d, s),
            device_id_type=MESH,
        ).wait_recv()
    out_ref[...] = buf[...]


def _node_reduce_kernel(x_ref, out_ref, buf, send_sem, recv_sem):
    d, b = lax.axis_index("dom"), lax.axis_index("blk")
    nd, nb = lax.axis_size("dom"), lax.axis_size("blk")
    partners = _halo_partners(nb)

    def in_range(i):
        return (i >= 0) & (i < nd)

    _barrier(partners, in_range, d, b, nb)

    def outgoing(delta, m):
        p = 1 + delta
        return pltpu.make_async_remote_copy(
            src_ref=x_ref.at[p, (b + m) % nb],
            dst_ref=buf.at[p, b],
            send_sem=send_sem.at[p, m],
            recv_sem=recv_sem.at[p, b],
            device_id=(d + delta, (b + m) % nb),
            device_id_type=MESH,
        )

    for delta, m in partners:
        pl.when(in_range(d + delta))(lambda delta=delta, m=m: outgoing(delta, m).start())
    buf[1, b] = x_ref[1, b]
    for side in (-1, 1):
        @pl.when(jnp.logical_not(in_range(d + side)))
        def _(side=side):
            buf[1 - side] = jnp.zeros(buf.shape[1:], buf.dtype)
    for delta, m in partners:
        pl.when(in_range(d + delta))(lambda delta=delta, m=m: outgoing(delta, m).wait_send())
    for delta, m in partners:
        p, s = 1 + delta, (b + m) % nb

        @pl.when(in_range(d - delta))
        def _(p=p, s=s):
            pltpu.make_async_remote_copy(
                src_ref=x_ref.at[p, s],
                dst_ref=buf.at[p, s],
                send_sem=send_sem.at[p, 0],
                recv_sem=recv_sem.at[p, s],
                device_id=(d - delta, s),
                device_id_type=MESH,
            ).wait_recv()
    out_ref[...] = buf[...]


def _exchange(kernel, x, out_shape, buf_shape, sem_shape, collective_id):
    return pl.pallas_call(
        kernel,
        out_shape=jax.ShapeDtypeStruct(out_shape, x.dtype),
        in_specs=[pl.BlockSpec(memory_space=pltpu.VMEM)],
        out_specs=pl.BlockSpec(memory_space=pltpu.VMEM),
        scratch_shapes=[
            pltpu.VMEM(buf_shape, x.dtype),
            pltpu.SemaphoreType.DMA(sem_shape),
            pltpu.SemaphoreType.DMA(sem_shape),
        ],
        compiler_params=pltpu.CompilerParams(
            collective_id=collective_id, has_side_effects=True
        ),
    )(x)


def halo_gather(x, nb, collective_id):
    shape = (3, nb) + x.shape
    out = _exchange(_halo_gather_kernel, x, shape, shape, (3, nb), collective_id)
    e, r, c = x.shape
    return jnp.transpose(out, (0, 2, 3, 1, 4)).reshape(3 * e, r, nb * c)


def blk_gather(x, nb, collective_id):
    shape = (nb,) + x.shape
    out = _exchange(_blk_gather_kernel, x, shape, shape, (nb,), collective_id)
    e, r, c = x.shape
    return jnp.transpose(out, (1, 2, 0, 3)).reshape(e, r, nb * c)


def node_reduce(chunks, collective_id):
    nb = chunks.shape[1]
    received = _exchange(
        _node_reduce_kernel, chunks, chunks.shape, chunks.shape, (3, nb), collective_id
    )
    return jnp.sum(received, axis=(0, 1))


LANES = 128


def _sweeps_kernel(
    start_ref, target_ref, jac_hbm, inv_ref, shape_ref, out_ref, wsum_ref,
    jac_v, select, send_a, halo, send_r, full_r, upd, jac_sem, hs_send, hs_recv, bk_send, bk_recv,
    fw_send, wpart, ws_send, ws_recv,
):
    d, b = lax.axis_index("dom"), lax.axis_index("blk")
    nd, nb = lax.axis_size("dom"), lax.axis_size("blk")
    rows = start_ref.shape[1]
    elems = jac_v.shape[0]
    faces = jac_v.shape[1]

    def in_range(i):
        return (i >= 0) & (i < nd)

    partners = [(0, m) for m in range(1, nb)] + [(-1, 0), (1, 0)]
    _barrier(partners, in_range, d, b, nb)
    jac_copy = pltpu.make_async_copy(jac_hbm, jac_v, jac_sem)
    jac_copy.start()
    lane = lax.broadcasted_iota(jnp.int32, (rows, LANES), 1)
    cand_row = lax.broadcasted_iota(jnp.int32, (3 * LANES, LANES), 0)
    for k in range(faces):
        select[k] = (cand_row == target_ref[pl.ds(k, 1), :]).astype(jnp.bfloat16)

    def row_block(i):
        return pl.ds(pl.multiple_of(i * rows, 16), rows)

    own_rows = row_block(b)
    adjoint = start_ref[0]
    for sweep in range(SWEEPS):
        send_a[sweep] = adjoint.astype(jnp.bfloat16)

        def direct(delta, m, sweep=sweep):
            return pltpu.make_async_remote_copy(
                src_ref=send_a.at[sweep],
                dst_ref=halo.at[sweep, 1 - delta, own_rows],
                send_sem=hs_send.at[sweep, delta + 1, m],
                recv_sem=hs_recv.at[sweep, 1 - delta, b],
                device_id=(d + delta, (b + m) % nb),
                device_id_type=MESH,
            )

        def forward(p, m, sweep=sweep):
            return pltpu.make_async_remote_copy(
                src_ref=halo.at[sweep, p, own_rows],
                dst_ref=halo.at[sweep, p, own_rows],
                send_sem=fw_send.at[sweep, p // 2, m],
                recv_sem=hs_recv.at[sweep, p, b],
                device_id=(d, (b + m) % nb),
                device_id_type=MESH,
            )

        def arrival(p, src_b, sweep=sweep):
            return pltpu.make_async_remote_copy(
                src_ref=send_a.at[sweep],
                dst_ref=halo.at[sweep, p, row_block(src_b)],
                send_sem=hs_send.at[sweep, p, 0],
                recv_sem=hs_recv.at[sweep, p, src_b],
                device_id=(d, src_b),
                device_id_type=MESH,
            )

        for delta, m in partners:
            pl.when(in_range(d + delta))(lambda delta=delta, m=m: direct(delta, m).start())
        halo[sweep, 1, own_rows] = send_a[sweep]
        for side in (-1, 1):
            @pl.when(jnp.logical_not(in_range(d + side)))
            def _(side=side, sweep=sweep):
                halo[sweep, 1 + side] = jnp.zeros(halo.shape[2:], halo.dtype)
        for side in (-1, 1):
            p = 1 + side

            @pl.when(in_range(d + side))
            def _(p=p):
                arrival(p, b).wait_recv()
                for m in range(1, nb):
                    forward(p, m).start()
        for delta, m in partners:
            pl.when(in_range(d + delta))(lambda delta=delta, m=m: direct(delta, m).wait_send())
        for m in range(1, nb):
            arrival(1, (b + m) % nb).wait_recv()
        for side in (-1, 1):
            p = 1 + side

            @pl.when(in_range(d + side))
            def _(p=p):
                for m in range(1, nb):
                    forward(p, m).wait_send()
                for m in range(1, nb):
                    arrival(p, (b + m) % nb).wait_recv()

        candidates = jnp.concatenate([halo[sweep, p] for p in range(3)], axis=1)
        if sweep == 0:
            jac_copy.wait()
        acc = jnp.zeros((elems * rows, LANES), jnp.float32)
        for k in range(faces):
            picked = jnp.dot(candidates, select[k], preferred_element_type=jnp.float32)
            acc = acc + jnp.dot(
                jac_v[:, k].reshape(elems * rows, -1),
                picked.astype(jnp.bfloat16),
                preferred_element_type=jnp.float32,
            )
        upd[...] = acc.reshape(upd.shape)
        product = jnp.zeros((rows, LANES), jnp.float32)
        for e in range(elems):
            mine = (lane >= RHS * e) & (lane < RHS * e + RHS)
            product = product + jnp.where(mine, upd[e], 0.0)
        image = start_ref[2] * adjoint + product
        send_r[sweep] = (start_ref[1] - image).astype(jnp.bfloat16)

        def blk_copy(m, sweep=sweep):
            return pltpu.make_async_remote_copy(
                src_ref=send_r.at[sweep],
                dst_ref=full_r.at[sweep, own_rows],
                send_sem=bk_send.at[sweep, m],
                recv_sem=bk_recv.at[sweep, b],
                device_id=(d, (b + m) % nb),
                device_id_type=MESH,
            )

        for m in range(1, nb):
            blk_copy(m).start()
        full_r[sweep, own_rows] = send_r[sweep]
        for m in range(1, nb):
            blk_copy(m).wait_send()
        for m in range(1, nb):
            src_b = (b + m) % nb
            pltpu.make_async_remote_copy(
                src_ref=send_r.at[sweep],
                dst_ref=full_r.at[sweep, pl.ds(pl.multiple_of(src_b * rows, 16), rows)],
                send_sem=bk_send.at[sweep, 0],
                recv_sem=bk_recv.at[sweep, src_b],
                device_id=(d, src_b),
                device_id_type=MESH,
            ).wait_recv()
        upd[...] = jnp.dot(
            inv_ref[...], full_r[sweep], preferred_element_type=jnp.float32
        ).reshape(upd.shape)
        update = jnp.zeros((rows, LANES), jnp.float32)
        for e in range(elems):
            mine = (lane >= RHS * e) & (lane < RHS * e + RHS)
            update = update + jnp.where(mine, upd[e], 0.0)
        adjoint = adjoint + update
    out_ref[...] = adjoint

    square = jnp.concatenate([adjoint, jnp.zeros((LANES - rows, LANES), jnp.float32)], axis=0)
    final_half = jnp.transpose(square)[:, :rows].astype(jnp.bfloat16)
    row = lax.broadcasted_iota(jnp.int32, (LANES, shape_ref.shape[2]), 0)
    weighted = jnp.zeros((LANES, shape_ref.shape[2]), jnp.float32)
    for e in range(elems):
        part = jnp.dot(final_half, shape_ref[e], preferred_element_type=jnp.float32)
        weighted = weighted + jnp.where((row >= RHS * e) & (row < RHS * e + RHS), part, 0.0)
    wpart[pl.ds(0, LANES)] = -weighted
    chunk = wsum_ref.shape[0]
    owners = pl.cdiv(elems * RHS, chunk)

    def wcopy(c, src_b):
        return pltpu.make_async_remote_copy(
            src_ref=wpart.at[pl.ds(c * chunk, chunk)],
            dst_ref=wpart.at[pl.ds(LANES + src_b * chunk, chunk)],
            send_sem=ws_send.at[c],
            recv_sem=ws_recv.at[src_b],
            device_id=(d, c),
            device_id_type=MESH,
        )

    for m in range(1, nb):
        c = (b + m) % nb
        pl.when(c < owners)(lambda c=c: wcopy(c, b).start())
    for m in range(1, nb):
        c = (b + m) % nb
        pl.when(c < owners)(lambda c=c: wcopy(c, b).wait_send())
    total = jnp.zeros(wsum_ref.shape, jnp.float32)
    for m in range(1, nb):
        src_b = (b + m) % nb

        @pl.when(b < owners)
        def _(src_b=src_b):
            wcopy(b, src_b).wait_recv()

    @pl.when(b < owners)
    def _():
        acc = wpart[pl.ds(pl.multiple_of(b * chunk, 8), chunk)]
        for m in range(1, nb):
            src_b = (b + m) % nb
            acc = acc + wpart[pl.ds(pl.multiple_of(LANES + src_b * chunk, 8), chunk)]
        wsum_ref[...] = acc

    @pl.when(b >= owners)
    def _():
        wsum_ref[...] = jnp.zeros(wsum_ref.shape, jnp.float32)


def sweeps(adjoint_start, right_sides, pseudo_shift, slots, jac_blocks, block_inverse,
           shape_partials, nb):
    elems, rhs, rows = adjoint_start.shape
    cols = jac_blocks.shape[-1]
    faces = jac_blocks.shape[1]

    stacked = jnp.stack([
        adjoint_start,
        right_sides,
        jnp.broadcast_to(pseudo_shift[:, None, None], adjoint_start.shape),
    ])
    stacked = jnp.transpose(stacked, (0, 3, 1, 2)).reshape(3, rows, elems * rhs)
    stacked = jnp.pad(stacked, ((0, 0), (0, 0), (0, LANES - elems * rhs)))
    part, within = slots // elems, slots % elems
    lanes = (part * LANES + within * rhs)[:, :, None] + jnp.arange(rhs, dtype=jnp.int32)
    target = jnp.transpose(lanes, (1, 0, 2)).reshape(faces, elems * rhs)
    target = jnp.pad(target, ((0, 8 - faces), (0, LANES - elems * rhs)), constant_values=-1)
    vmem = pl.BlockSpec(memory_space=pltpu.VMEM)
    chunk = 8 * rhs
    out, wsum = pl.pallas_call(
        _sweeps_kernel,
        out_shape=(
            jax.ShapeDtypeStruct((rows, LANES), jnp.float32),
            jax.ShapeDtypeStruct((chunk, shape_partials.shape[2]), jnp.float32),
        ),
        in_specs=[vmem, vmem, pl.BlockSpec(memory_space=pl.ANY), vmem, vmem],
        out_specs=(vmem, vmem),
        scratch_shapes=[
            pltpu.VMEM((elems, faces, rows, cols), jnp.bfloat16),
            pltpu.VMEM((faces, 3 * LANES, LANES), jnp.bfloat16),
            pltpu.VMEM((SWEEPS, rows, LANES), jnp.bfloat16),
            pltpu.VMEM((SWEEPS, 3, nb * rows, LANES), jnp.bfloat16),
            pltpu.VMEM((SWEEPS, rows, LANES), jnp.bfloat16),
            pltpu.VMEM((SWEEPS, nb * rows, LANES), jnp.bfloat16),
            pltpu.VMEM((elems, rows, LANES), jnp.float32),
            pltpu.SemaphoreType.DMA(()),
            pltpu.SemaphoreType.DMA((SWEEPS, 3, nb)),
            pltpu.SemaphoreType.DMA((SWEEPS, 3, nb)),
            pltpu.SemaphoreType.DMA((SWEEPS, nb)),
            pltpu.SemaphoreType.DMA((SWEEPS, nb)),
            pltpu.SemaphoreType.DMA((SWEEPS, 2, nb)),
            pltpu.VMEM((LANES + nb * chunk, shape_partials.shape[2]), jnp.float32),
            pltpu.SemaphoreType.DMA((nb,)),
            pltpu.SemaphoreType.DMA((nb,)),
        ],
        compiler_params=pltpu.CompilerParams(
            collective_id=0, has_side_effects=True, vmem_limit_bytes=48 * 1024 * 1024
        ),
    )(
        stacked,
        target,
        jac_blocks,
        block_inverse.reshape(elems * rows, cols),
        shape_partials,
    )
    adjoint = jnp.transpose(out[:, : elems * rhs].reshape(rows, elems, rhs), (1, 2, 0))
    return adjoint, wsum


def local(
    adjoint_start,
    right_sides,
    jac_blocks,
    block_inverse,
    neighbours,
    pseudo_shift,
    shape_partials,
    node_ids,
):
    local_count = neighbours.shape[0]
    nb = lax.axis_size("blk")
    part_index = lax.axis_index("dom")
    own = jnp.arange(local_count, dtype=jnp.int32)[:, None] + local_count
    slots = jnp.concatenate([own, neighbours - (part_index - 1) * local_count], axis=1)
    adjoint, wsum = sweeps(
        adjoint_start, right_sides, pseudo_shift, slots, jac_blocks, block_inverse,
        shape_partials, nb,
    )
    node_width = node_ids.shape[1]
    chunk_elems = wsum.shape[0] // RHS
    values = wsum.reshape(chunk_elems, RHS, node_width, 3)
    values = jnp.transpose(values, (0, 2, 1, 3)).reshape(chunk_elems * node_width, RHS * 3)
    my_nodes = lax.dynamic_slice_in_dim(
        node_ids, jnp.minimum(lax.axis_index("blk") * chunk_elems, local_count - chunk_elems),
        chunk_elems,
    )
    node_slots = (my_nodes - (part_index - 1) * NODE_DEV).reshape(-1)
    partial_sums = jax.ops.segment_sum(values, node_slots, 3 * NODE_DEV).T
    chunks = jnp.transpose(
        partial_sums.reshape(RHS * 3, 3, nb, NODE_DEV // nb), (1, 2, 0, 3)
    )
    shape_gradient = node_reduce(chunks, collective_id=1)
    return (adjoint, shape_gradient)


def solution(mesh):
    in_specs = (
        P("dom", None, "blk"),
        P("dom", None, "blk"),
        P("dom", None, "blk", None),
        P("dom", "blk", None),
        P("dom", None),
        P("dom"),
        P("dom", "blk", None),
        P("dom", None),
    )
    out_specs = (P("dom", None, "blk"), P(None, ("dom", "blk")))
    return jax.shard_map(local, mesh=mesh, in_specs=in_specs, out_specs=out_specs, check_vma=False)
```

```python
import functools

import jax
import jax.numpy as jnp
from jax import lax
from jax.experimental import pallas as pl
from jax.experimental.pallas import tpu as pltpu
from jax.sharding import PartitionSpec as P

RHS = 3
SWEEPS = 2
NODE_DEV = 768
MESH = pl.DeviceIdType.MESH


def _halo_partners(nb):
    return [(delta, m) for delta in (-1, 0, 1) for m in range(nb) if (delta, m) != (0, 0)]


def _barrier(partners, in_range, d, b, nb):
    barrier = pltpu.get_barrier_semaphore()
    for delta, m in partners:
        @pl.when(in_range(d + delta))
        def _(delta=delta, m=m):
            pl.semaphore_signal(
                barrier, 1, device_id=(d + delta, (b + m) % nb), device_id_type=MESH
            )
    nd = lax.axis_size("dom")
    has_lower = (d + nd - 1) // nd
    has_upper = (2 * nd - 2 - d) // nd
    peers = [sum(1 for delta, _ in partners if delta == side) for side in (-1, 0, 1)]
    pl.semaphore_wait(barrier, peers[1] + peers[0] * has_lower + peers[2] * has_upper)


def _halo_gather_kernel(x_ref, out_ref, buf, send_sem, recv_sem):
    d, b = lax.axis_index("dom"), lax.axis_index("blk")
    nd, nb = lax.axis_size("dom"), lax.axis_size("blk")
    partners = _halo_partners(nb)

    def in_range(i):
        return (i >= 0) & (i < nd)

    _barrier(partners, in_range, d, b, nb)

    def outgoing(delta, m):
        return pltpu.make_async_remote_copy(
            src_ref=x_ref,
            dst_ref=buf.at[1 - delta, b],
            send_sem=send_sem.at[delta + 1, m],
            recv_sem=recv_sem.at[1 - delta, b],
            device_id=(d + delta, (b + m) % nb),
            device_id_type=MESH,
        )

    for delta, m in partners:
        pl.when(in_range(d + delta))(lambda delta=delta, m=m: outgoing(delta, m).start())
    buf[1, b] = x_ref[...]
    for side in (-1, 1):
        @pl.when(jnp.logical_not(in_range(d + side)))
        def _(side=side):
            buf[1 + side] = jnp.zeros(buf.shape[1:], buf.dtype)
    for delta, m in partners:
        pl.when(in_range(d + delta))(lambda delta=delta, m=m: outgoing(delta, m).wait_send())
    for delta, m in partners:
        p, s = 1 + delta, (b + m) % nb

        @pl.when(in_range(d + delta))
        def _(p=p, s=s):
            pltpu.make_async_remote_copy(
                src_ref=x_ref,
                dst_ref=buf.at[p, s],
                send_sem=send_sem.at[p, 0],
                recv_sem=recv_sem.at[p, s],
                device_id=(d + p - 1, s),
                device_id_type=MESH,
            ).wait_recv()

    out_ref[...] = buf[...]


def _blk_gather_kernel(x_ref, out_ref, buf, send_sem, recv_sem):
    d, b = lax.axis_index("dom"), lax.axis_index("blk")
    nd, nb = lax.axis_size("dom"), lax.axis_size("blk")
    partners = [(0, m) for m in range(1, nb)]
    _barrier(partners, lambda i: (i >= 0) & (i < nd), d, b, nb)

    def outgoing(m):
        return pltpu.make_async_remote_copy(
            src_ref=x_ref,
            dst_ref=buf.at[b],
            send_sem=send_sem.at[m],
            recv_sem=recv_sem.at[b],
            device_id=(d, (b + m) % nb),
            device_id_type=MESH,
        )

    for _, m in partners:
        outgoing(m).start()
    buf[b] = x_ref[...]
    for _, m in partners:
        outgoing(m).wait_send()
    for _, m in partners:
        s = (b + m) % nb
        pltpu.make_async_remote_copy(
            src_ref=x_ref,
            dst_ref=buf.at[s],
            send_sem=send_sem.at[0],
            recv_sem=recv_sem.at[s],
            device_id=(d, s),
            device_id_type=MESH,
        ).wait_recv()
    out_ref[...] = buf[...]


def _node_reduce_kernel(x_ref, out_ref, buf, send_sem, recv_sem):
    d, b = lax.axis_index("dom"), lax.axis_index("blk")
    nd, nb = lax.axis_size("dom"), lax.axis_size("blk")
    partners = _halo_partners(nb)

    def in_range(i):
        return (i >= 0) & (i < nd)

    _barrier(partners, in_range, d, b, nb)

    def outgoing(delta, m):
        p = 1 + delta
        return pltpu.make_async_remote_copy(
            src_ref=x_ref.at[p, (b + m) % nb],
            dst_ref=buf.at[p, b],
            send_sem=send_sem.at[p, m],
            recv_sem=recv_sem.at[p, b],
            device_id=(d + delta, (b + m) % nb),
            device_id_type=MESH,
        )

    for delta, m in partners:
        pl.when(in_range(d + delta))(lambda delta=delta, m=m: outgoing(delta, m).start())
    out_ref[...] = x_ref[1, b]
    for delta, m in partners:
        pl.when(in_range(d + delta))(lambda delta=delta, m=m: outgoing(delta, m).wait_send())
    for delta, m in partners:
        p, s = 1 + delta, (b + m) % nb

        @pl.when(in_range(d - delta))
        def _(p=p, s=s):
            pltpu.make_async_remote_copy(
                src_ref=x_ref.at[p, s],
                dst_ref=buf.at[p, s],
                send_sem=send_sem.at[p, 0],
                recv_sem=recv_sem.at[p, s],
                device_id=(d - delta, s),
                device_id_type=MESH,
            ).wait_recv()
            out_ref[...] += buf[p, s]


def _exchange(kernel, x, out_shape, buf_shape, sem_shape, collective_id):
    return pl.pallas_call(
        kernel,
        out_shape=jax.ShapeDtypeStruct(out_shape, x.dtype),
        in_specs=[pl.BlockSpec(memory_space=pltpu.VMEM)],
        out_specs=pl.BlockSpec(memory_space=pltpu.VMEM),
        scratch_shapes=[
            pltpu.VMEM(buf_shape, x.dtype),
            pltpu.SemaphoreType.DMA(sem_shape),
            pltpu.SemaphoreType.DMA(sem_shape),
        ],
        compiler_params=pltpu.CompilerParams(
            collective_id=collective_id, has_side_effects=True
        ),
    )(x)


def halo_gather(x, nb, collective_id):
    shape = (3, nb) + x.shape
    out = _exchange(_halo_gather_kernel, x, shape, shape, (3, nb), collective_id)
    e, r, c = x.shape
    return jnp.transpose(out, (0, 2, 3, 1, 4)).reshape(3 * e, r, nb * c)


def blk_gather(x, nb, collective_id):
    shape = (nb,) + x.shape
    out = _exchange(_blk_gather_kernel, x, shape, shape, (nb,), collective_id)
    e, r, c = x.shape
    return jnp.transpose(out, (1, 2, 0, 3)).reshape(e, r, nb * c)


def node_reduce(chunks, collective_id):
    nb = chunks.shape[1]
    return _exchange(
        _node_reduce_kernel, chunks, chunks.shape[2:], chunks.shape, (3, nb), collective_id
    )


LANES = 128


def _sweeps_kernel(
    start_ref, target_ref, jac_hbm, inv_ref, shape_ref, out_ref, wsum_ref,
    jac_v, select, send_a, halo, send_r, full_r, upd, jac_sem, hs_send, hs_recv, bk_send, bk_recv,
    fw_send, wpart, ws_send, ws_recv,
):
    d, b = lax.axis_index("dom"), lax.axis_index("blk")
    nd, nb = lax.axis_size("dom"), lax.axis_size("blk")
    rows = start_ref.shape[1]
    elems = jac_v.shape[0]
    faces = jac_v.shape[1]

    def in_range(i):
        return (i >= 0) & (i < nd)

    partners = [(0, m) for m in range(1, nb)] + [(-1, 0), (1, 0)]
    jac_copy = pltpu.make_async_copy(jac_hbm, jac_v, jac_sem)
    jac_copy.start()
    _barrier(partners, in_range, d, b, nb)
    lane = lax.broadcasted_iota(jnp.int32, (rows, LANES), 1)
    cand_row = lax.broadcasted_iota(jnp.int32, (3 * LANES, LANES), 0)
    for k in range(faces):
        select[k] = (cand_row == target_ref[pl.ds(k, 1), :]).astype(jnp.bfloat16)

    def row_block(i):
        return pl.ds(pl.multiple_of(i * rows, 16), rows)

    own_rows = row_block(b)
    adjoint = start_ref[0]
    for sweep in range(SWEEPS):
        send_a[sweep] = adjoint.astype(jnp.bfloat16)

        def direct(delta, m, sweep=sweep):
            return pltpu.make_async_remote_copy(
                src_ref=send_a.at[sweep],
                dst_ref=halo.at[sweep, 1 - delta, own_rows],
                send_sem=hs_send.at[sweep, delta + 1, m],
                recv_sem=hs_recv.at[sweep, 1 - delta, b],
                device_id=(d + delta, (b + m) % nb),
                device_id_type=MESH,
            )

        def forward(p, m, sweep=sweep):
            return pltpu.make_async_remote_copy(
                src_ref=halo.at[sweep, p, own_rows],
                dst_ref=halo.at[sweep, p, own_rows],
                send_sem=fw_send.at[sweep, p // 2, m],
                recv_sem=hs_recv.at[sweep, p, b],
                device_id=(d, (b + m) % nb),
                device_id_type=MESH,
            )

        def arrival(p, src_b, sweep=sweep):
            return pltpu.make_async_remote_copy(
                src_ref=send_a.at[sweep],
                dst_ref=halo.at[sweep, p, row_block(src_b)],
                send_sem=hs_send.at[sweep, p, 0],
                recv_sem=hs_recv.at[sweep, p, src_b],
                device_id=(d, src_b),
                device_id_type=MESH,
            )

        for delta, m in partners:
            pl.when(in_range(d + delta))(lambda delta=delta, m=m: direct(delta, m).start())
        halo[sweep, 1, own_rows] = send_a[sweep]
        for side in (-1, 1):
            @pl.when(jnp.logical_not(in_range(d + side)))
            def _(side=side, sweep=sweep):
                halo[sweep, 1 + side] = jnp.zeros(halo.shape[2:], halo.dtype)
        for side in (-1, 1):
            p = 1 + side

            @pl.when(in_range(d + side))
            def _(p=p):
                arrival(p, b).wait_recv()
                for m in range(1, nb):
                    forward(p, m).start()
        for delta, m in partners:
            pl.when(in_range(d + delta))(lambda delta=delta, m=m: direct(delta, m).wait_send())
        for m in range(1, nb):
            arrival(1, (b + m) % nb).wait_recv()
        for side in (-1, 1):
            p = 1 + side

            @pl.when(in_range(d + side))
            def _(p=p):
                for m in range(1, nb):
                    forward(p, m).wait_send()
                for m in range(1, nb):
                    arrival(p, (b + m) % nb).wait_recv()

        candidates = jnp.concatenate([halo[sweep, p] for p in range(3)], axis=1)
        if sweep == 0:
            jac_copy.wait()
        acc = jnp.zeros((elems * rows, LANES), jnp.float32)
        for k in range(faces):
            picked = jnp.dot(candidates, select[k], preferred_element_type=jnp.float32)
            acc = acc + jnp.dot(
                jac_v[:, k].reshape(elems * rows, -1),
                picked.astype(jnp.bfloat16),
                preferred_element_type=jnp.float32,
            )
        upd[...] = acc.reshape(upd.shape)
        product = jnp.zeros((rows, LANES), jnp.float32)
        for e in range(elems):
            mine = (lane >= RHS * e) & (lane < RHS * e + RHS)
            product = product + jnp.where(mine, upd[e], 0.0)
        image = start_ref[2] * adjoint + product
        send_r[sweep] = (start_ref[1] - image).astype(jnp.bfloat16)

        def blk_copy(m, sweep=sweep):
            return pltpu.make_async_remote_copy(
                src_ref=send_r.at[sweep],
                dst_ref=full_r.at[sweep, own_rows],
                send_sem=bk_send.at[sweep, m],
                recv_sem=bk_recv.at[sweep, b],
                device_id=(d, (b + m) % nb),
                device_id_type=MESH,
            )

        for m in range(1, nb):
            blk_copy(m).start()
        full_r[sweep, own_rows] = send_r[sweep]
        for m in range(1, nb):
            blk_copy(m).wait_send()
        for m in range(1, nb):
            src_b = (b + m) % nb
            pltpu.make_async_remote_copy(
                src_ref=send_r.at[sweep],
                dst_ref=full_r.at[sweep, pl.ds(pl.multiple_of(src_b * rows, 16), rows)],
                send_sem=bk_send.at[sweep, 0],
                recv_sem=bk_recv.at[sweep, src_b],
                device_id=(d, src_b),
                device_id_type=MESH,
            ).wait_recv()
        upd[...] = jnp.dot(
            inv_ref[...], full_r[sweep], preferred_element_type=jnp.float32
        ).reshape(upd.shape)
        update = jnp.zeros((rows, LANES), jnp.float32)
        for e in range(elems):
            mine = (lane >= RHS * e) & (lane < RHS * e + RHS)
            update = update + jnp.where(mine, upd[e], 0.0)
        adjoint = adjoint + update
    out_ref[...] = adjoint

    square = jnp.concatenate([adjoint, jnp.zeros((LANES - rows, LANES), jnp.float32)], axis=0)
    final_f32 = jnp.transpose(square)[:, :rows]
    window = 16
    row = lax.broadcasted_iota(jnp.int32, (window, shape_ref.shape[2]), 0)
    wpart[pl.ds(0, LANES)] = jnp.zeros((LANES, shape_ref.shape[2]), jnp.float32)
    for e in range(elems):
        low = (RHS * e) // 8 * 8
        part = jnp.dot(
            final_f32[low:low + window].astype(jnp.bfloat16),
            shape_ref[e],
            preferred_element_type=jnp.float32,
        )
        mine = (row + low >= RHS * e) & (row + low < RHS * e + RHS)
        wpart[pl.ds(low, window)] = wpart[pl.ds(low, window)] - jnp.where(mine, part, 0.0)
    chunk = wsum_ref.shape[0]
    owners = pl.cdiv(elems * RHS, chunk)

    def wcopy(c, src_b):
        return pltpu.make_async_remote_copy(
            src_ref=wpart.at[pl.ds(c * chunk, chunk)],
            dst_ref=wpart.at[pl.ds(LANES + src_b * chunk, chunk)],
            send_sem=ws_send.at[c],
            recv_sem=ws_recv.at[src_b],
            device_id=(d, c),
            device_id_type=MESH,
        )

    for m in range(1, nb):
        c = (b + m) % nb
        pl.when(c < owners)(lambda c=c: wcopy(c, b).start())
    for m in range(1, nb):
        c = (b + m) % nb
        pl.when(c < owners)(lambda c=c: wcopy(c, b).wait_send())
    total = jnp.zeros(wsum_ref.shape, jnp.float32)
    for m in range(1, nb):
        src_b = (b + m) % nb

        @pl.when(b < owners)
        def _(src_b=src_b):
            wcopy(b, src_b).wait_recv()

    @pl.when(b < owners)
    def _():
        acc = wpart[pl.ds(pl.multiple_of(b * chunk, 8), chunk)]
        for m in range(1, nb):
            src_b = (b + m) % nb
            acc = acc + wpart[pl.ds(pl.multiple_of(LANES + src_b * chunk, 8), chunk)]
        wsum_ref[...] = acc

    @pl.when(b >= owners)
    def _():
        wsum_ref[...] = jnp.zeros(wsum_ref.shape, jnp.float32)


def sweeps(adjoint_start, right_sides, pseudo_shift, slots, jac_blocks, block_inverse,
           shape_partials, nb):
    elems, rhs, rows = adjoint_start.shape
    cols = jac_blocks.shape[-1]
    faces = jac_blocks.shape[1]

    stacked = jnp.stack([
        adjoint_start,
        right_sides,
        jnp.broadcast_to(pseudo_shift[:, None, None], adjoint_start.shape),
    ])
    stacked = jnp.transpose(stacked, (0, 3, 1, 2)).reshape(3, rows, elems * rhs)
    stacked = jnp.pad(stacked, ((0, 0), (0, 0), (0, LANES - elems * rhs)))
    part, within = slots // elems, slots % elems
    lanes = (part * LANES + within * rhs)[:, :, None] + jnp.arange(rhs, dtype=jnp.int32)
    target = jnp.transpose(lanes, (1, 0, 2)).reshape(faces, elems * rhs)
    target = jnp.pad(target, ((0, 8 - faces), (0, LANES - elems * rhs)), constant_values=-1)
    vmem = pl.BlockSpec(memory_space=pltpu.VMEM)
    chunk = 8 * rhs
    out, wsum = pl.pallas_call(
        _sweeps_kernel,
        out_shape=(
            jax.ShapeDtypeStruct((rows, LANES), jnp.float32),
            jax.ShapeDtypeStruct((chunk, shape_partials.shape[2]), jnp.float32),
        ),
        in_specs=[vmem, vmem, pl.BlockSpec(memory_space=pl.ANY), vmem, vmem],
        out_specs=(vmem, vmem),
        scratch_shapes=[
            pltpu.VMEM((elems, faces, rows, cols), jnp.bfloat16),
            pltpu.VMEM((faces, 3 * LANES, LANES), jnp.bfloat16),
            pltpu.VMEM((SWEEPS, rows, LANES), jnp.bfloat16),
            pltpu.VMEM((SWEEPS, 3, nb * rows, LANES), jnp.bfloat16),
            pltpu.VMEM((SWEEPS, rows, LANES), jnp.bfloat16),
            pltpu.VMEM((SWEEPS, nb * rows, LANES), jnp.bfloat16),
            pltpu.VMEM((elems, rows, LANES), jnp.float32),
            pltpu.SemaphoreType.DMA(()),
            pltpu.SemaphoreType.DMA((SWEEPS, 3, nb)),
            pltpu.SemaphoreType.DMA((SWEEPS, 3, nb)),
            pltpu.SemaphoreType.DMA((SWEEPS, nb)),
            pltpu.SemaphoreType.DMA((SWEEPS, nb)),
            pltpu.SemaphoreType.DMA((SWEEPS, 2, nb)),
            pltpu.VMEM((LANES + nb * chunk, shape_partials.shape[2]), jnp.float32),
            pltpu.SemaphoreType.DMA((nb,)),
            pltpu.SemaphoreType.DMA((nb,)),
        ],
        compiler_params=pltpu.CompilerParams(
            collective_id=0, has_side_effects=True, vmem_limit_bytes=48 * 1024 * 1024
        ),
    )(
        stacked,
        target,
        jac_blocks,
        block_inverse.reshape(elems * rows, cols),
        shape_partials,
    )
    adjoint = jnp.transpose(out[:, : elems * rhs].reshape(rows, elems, rhs), (1, 2, 0))
    return adjoint, wsum


def local(
    adjoint_start,
    right_sides,
    jac_blocks,
    block_inverse,
    neighbours,
    pseudo_shift,
    shape_partials,
    node_ids,
):
    local_count = neighbours.shape[0]
    nb = lax.axis_size("blk")
    part_index = lax.axis_index("dom")
    own = jnp.arange(local_count, dtype=jnp.int32)[:, None] + local_count
    slots = jnp.concatenate([own, neighbours - (part_index - 1) * local_count], axis=1)
    adjoint, wsum = sweeps(
        adjoint_start, right_sides, pseudo_shift, slots, jac_blocks, block_inverse,
        shape_partials, nb,
    )
    node_width = node_ids.shape[1]
    chunk_elems = wsum.shape[0] // RHS
    values = wsum.reshape(chunk_elems, RHS, node_width, 3)
    values = jnp.transpose(values, (0, 2, 1, 3)).reshape(chunk_elems * node_width, RHS * 3)
    my_nodes = lax.dynamic_slice_in_dim(
        node_ids, jnp.minimum(lax.axis_index("blk") * chunk_elems, local_count - chunk_elems),
        chunk_elems,
    )
    node_slots = (my_nodes - (part_index - 1) * NODE_DEV).reshape(-1)
    partial_sums = jax.ops.segment_sum(values, node_slots, 3 * NODE_DEV).T
    chunks = jnp.transpose(
        partial_sums.reshape(RHS * 3, 3, nb, NODE_DEV // nb), (1, 2, 0, 3)
    )
    shape_gradient = node_reduce(chunks, collective_id=1)
    return (adjoint, shape_gradient)


def solution(mesh):
    in_specs = (
        P("dom", None, "blk"),
        P("dom", None, "blk"),
        P("dom", None, "blk", None),
        P("dom", "blk", None),
        P("dom", None),
        P("dom"),
        P("dom", "blk", None),
        P("dom", None),
    )
    out_specs = (P("dom", None, "blk"), P(None, ("dom", "blk")))
    return jax.shard_map(local, mesh=mesh, in_specs=in_specs, out_specs=out_specs, check_vma=False)
```

```python
import functools

import jax
import jax.numpy as jnp
from jax import lax
from jax.experimental import pallas as pl
from jax.experimental.pallas import tpu as pltpu
from jax.sharding import PartitionSpec as P

RHS = 3
SWEEPS = 2
NODE_DEV = 768
MESH = pl.DeviceIdType.MESH


def _halo_partners(nb):
    return [(delta, m) for delta in (-1, 0, 1) for m in range(nb) if (delta, m) != (0, 0)]


def _barrier(partners, in_range, d, b, nb):
    barrier = pltpu.get_barrier_semaphore()
    for delta, m in partners:
        @pl.when(in_range(d + delta))
        def _(delta=delta, m=m):
            pl.semaphore_signal(
                barrier, 1, device_id=(d + delta, (b + m) % nb), device_id_type=MESH
            )
    nd = lax.axis_size("dom")
    has_lower = (d + nd - 1) // nd
    has_upper = (2 * nd - 2 - d) // nd
    peers = [sum(1 for delta, _ in partners if delta == side) for side in (-1, 0, 1)]
    pl.semaphore_wait(barrier, peers[1] + peers[0] * has_lower + peers[2] * has_upper)


def _halo_gather_kernel(x_ref, out_ref, buf, send_sem, recv_sem):
    d, b = lax.axis_index("dom"), lax.axis_index("blk")
    nd, nb = lax.axis_size("dom"), lax.axis_size("blk")
    partners = _halo_partners(nb)

    def in_range(i):
        return (i >= 0) & (i < nd)

    _barrier(partners, in_range, d, b, nb)

    def outgoing(delta, m):
        return pltpu.make_async_remote_copy(
            src_ref=x_ref,
            dst_ref=buf.at[1 - delta, b],
            send_sem=send_sem.at[delta + 1, m],
            recv_sem=recv_sem.at[1 - delta, b],
            device_id=(d + delta, (b + m) % nb),
            device_id_type=MESH,
        )

    for delta, m in partners:
        pl.when(in_range(d + delta))(lambda delta=delta, m=m: outgoing(delta, m).start())
    buf[1, b] = x_ref[...]
    for side in (-1, 1):
        @pl.when(jnp.logical_not(in_range(d + side)))
        def _(side=side):
            buf[1 + side] = jnp.zeros(buf.shape[1:], buf.dtype)
    for delta, m in partners:
        pl.when(in_range(d + delta))(lambda delta=delta, m=m: outgoing(delta, m).wait_send())
    for delta, m in partners:
        p, s = 1 + delta, (b + m) % nb

        @pl.when(in_range(d + delta))
        def _(p=p, s=s):
            pltpu.make_async_remote_copy(
                src_ref=x_ref,
                dst_ref=buf.at[p, s],
                send_sem=send_sem.at[p, 0],
                recv_sem=recv_sem.at[p, s],
                device_id=(d + p - 1, s),
                device_id_type=MESH,
            ).wait_recv()

    out_ref[...] = buf[...]


def _blk_gather_kernel(x_ref, out_ref, buf, send_sem, recv_sem):
    d, b = lax.axis_index("dom"), lax.axis_index("blk")
    nd, nb = lax.axis_size("dom"), lax.axis_size("blk")
    partners = [(0, m) for m in range(1, nb)]
    _barrier(partners, lambda i: (i >= 0) & (i < nd), d, b, nb)

    def outgoing(m):
        return pltpu.make_async_remote_copy(
            src_ref=x_ref,
            dst_ref=buf.at[b],
            send_sem=send_sem.at[m],
            recv_sem=recv_sem.at[b],
            device_id=(d, (b + m) % nb),
            device_id_type=MESH,
        )

    for _, m in partners:
        outgoing(m).start()
    buf[b] = x_ref[...]
    for _, m in partners:
        outgoing(m).wait_send()
    for _, m in partners:
        s = (b + m) % nb
        pltpu.make_async_remote_copy(
            src_ref=x_ref,
            dst_ref=buf.at[s],
            send_sem=send_sem.at[0],
            recv_sem=recv_sem.at[s],
            device_id=(d, s),
            device_id_type=MESH,
        ).wait_recv()
    out_ref[...] = buf[...]


def _node_reduce_kernel(x_ref, out_ref, buf, send_sem, recv_sem):
    d, b = lax.axis_index("dom"), lax.axis_index("blk")
    nd, nb = lax.axis_size("dom"), lax.axis_size("blk")
    partners = _halo_partners(nb)

    def in_range(i):
        return (i >= 0) & (i < nd)

    _barrier(partners, in_range, d, b, nb)

    def outgoing(delta, m):
        p = 1 + delta
        return pltpu.make_async_remote_copy(
            src_ref=x_ref.at[p, (b + m) % nb],
            dst_ref=buf.at[p, b],
            send_sem=send_sem.at[p, m],
            recv_sem=recv_sem.at[p, b],
            device_id=(d + delta, (b + m) % nb),
            device_id_type=MESH,
        )

    for delta, m in partners:
        pl.when(in_range(d + delta))(lambda delta=delta, m=m: outgoing(delta, m).start())
    out_ref[...] = x_ref[1, b]
    for delta, m in partners:
        pl.when(in_range(d + delta))(lambda delta=delta, m=m: outgoing(delta, m).wait_send())
    for delta, m in partners:
        p, s = 1 + delta, (b + m) % nb

        @pl.when(in_range(d - delta))
        def _(p=p, s=s):
            pltpu.make_async_remote_copy(
                src_ref=x_ref.at[p, s],
                dst_ref=buf.at[p, s],
                send_sem=send_sem.at[p, 0],
                recv_sem=recv_sem.at[p, s],
                device_id=(d - delta, s),
                device_id_type=MESH,
            ).wait_recv()
            out_ref[...] += buf[p, s]


def _exchange(kernel, x, out_shape, buf_shape, sem_shape, collective_id):
    return pl.pallas_call(
        kernel,
        out_shape=jax.ShapeDtypeStruct(out_shape, x.dtype),
        in_specs=[pl.BlockSpec(memory_space=pltpu.VMEM)],
        out_specs=pl.BlockSpec(memory_space=pltpu.VMEM),
        scratch_shapes=[
            pltpu.VMEM(buf_shape, x.dtype),
            pltpu.SemaphoreType.DMA(sem_shape),
            pltpu.SemaphoreType.DMA(sem_shape),
        ],
        compiler_params=pltpu.CompilerParams(
            collective_id=collective_id, has_side_effects=True
        ),
    )(x)


def halo_gather(x, nb, collective_id):
    shape = (3, nb) + x.shape
    out = _exchange(_halo_gather_kernel, x, shape, shape, (3, nb), collective_id)
    e, r, c = x.shape
    return jnp.transpose(out, (0, 2, 3, 1, 4)).reshape(3 * e, r, nb * c)


def blk_gather(x, nb, collective_id):
    shape = (nb,) + x.shape
    out = _exchange(_blk_gather_kernel, x, shape, shape, (nb,), collective_id)
    e, r, c = x.shape
    return jnp.transpose(out, (1, 2, 0, 3)).reshape(e, r, nb * c)


def node_reduce(chunks, collective_id):
    nb = chunks.shape[1]
    return _exchange(
        _node_reduce_kernel, chunks, chunks.shape[2:], chunks.shape, (3, nb), collective_id
    )


LANES = 128


def _sweeps_kernel(
    start_ref, target_ref, jac_hbm, inv_hbm, shape_hbm, out_ref, wsum_ref,
    jac_v, inv_ref, shape_ref, select, send_a, halo, send_r, full_r, upd, jac_sem, hs_send, hs_recv, bk_send, bk_recv,
    fw_send, wpart, ws_send, ws_recv,
):
    d, b = lax.axis_index("dom"), lax.axis_index("blk")
    nd, nb = lax.axis_size("dom"), lax.axis_size("blk")
    rows = start_ref.shape[1]
    elems = jac_v.shape[0]
    faces = jac_v.shape[1]

    def in_range(i):
        return (i >= 0) & (i < nd)

    partners = [(0, m) for m in range(1, nb)] + [(-1, 0), (1, 0)]
    jac_copy = pltpu.make_async_copy(jac_hbm, jac_v, jac_sem.at[0])
    inv_copy = pltpu.make_async_copy(inv_hbm, inv_ref, jac_sem.at[1])
    shape_copy = pltpu.make_async_copy(shape_hbm, shape_ref, jac_sem.at[2])
    jac_copy.start()
    inv_copy.start()
    shape_copy.start()
    _barrier(partners, in_range, d, b, nb)
    lane = lax.broadcasted_iota(jnp.int32, (rows, LANES), 1)
    cand_row = lax.broadcasted_iota(jnp.int32, (3 * LANES, LANES), 0)
    for k in range(faces):
        select[k] = (cand_row == target_ref[pl.ds(k, 1), :]).astype(jnp.bfloat16)

    def row_block(i):
        return pl.ds(pl.multiple_of(i * rows, 16), rows)

    own_rows = row_block(b)
    adjoint = start_ref[0]
    for sweep in range(SWEEPS):
        send_a[sweep] = adjoint.astype(jnp.bfloat16)

        def direct(delta, m, sweep=sweep):
            return pltpu.make_async_remote_copy(
                src_ref=send_a.at[sweep],
                dst_ref=halo.at[sweep, 1 - delta, own_rows],
                send_sem=hs_send.at[sweep, delta + 1, m],
                recv_sem=hs_recv.at[sweep, 1 - delta, b],
                device_id=(d + delta, (b + m) % nb),
                device_id_type=MESH,
            )

        def forward(p, m, sweep=sweep):
            return pltpu.make_async_remote_copy(
                src_ref=halo.at[sweep, p, own_rows],
                dst_ref=halo.at[sweep, p, own_rows],
                send_sem=fw_send.at[sweep, p // 2, m],
                recv_sem=hs_recv.at[sweep, p, b],
                device_id=(d, (b + m) % nb),
                device_id_type=MESH,
            )

        def arrival(p, src_b, sweep=sweep):
            return pltpu.make_async_remote_copy(
                src_ref=send_a.at[sweep],
                dst_ref=halo.at[sweep, p, row_block(src_b)],
                send_sem=hs_send.at[sweep, p, 0],
                recv_sem=hs_recv.at[sweep, p, src_b],
                device_id=(d, src_b),
                device_id_type=MESH,
            )

        for delta, m in partners:
            pl.when(in_range(d + delta))(lambda delta=delta, m=m: direct(delta, m).start())
        halo[sweep, 1, own_rows] = send_a[sweep]
        for side in (-1, 1):
            @pl.when(jnp.logical_not(in_range(d + side)))
            def _(side=side, sweep=sweep):
                halo[sweep, 1 + side] = jnp.zeros(halo.shape[2:], halo.dtype)
        for side in (-1, 1):
            p = 1 + side

            @pl.when(in_range(d + side))
            def _(p=p):
                arrival(p, b).wait_recv()
                for m in range(1, nb):
                    forward(p, m).start()
        for delta, m in partners:
            pl.when(in_range(d + delta))(lambda delta=delta, m=m: direct(delta, m).wait_send())
        for m in range(1, nb):
            arrival(1, (b + m) % nb).wait_recv()
        for side in (-1, 1):
            p = 1 + side

            @pl.when(in_range(d + side))
            def _(p=p):
                for m in range(1, nb):
                    forward(p, m).wait_send()
                for m in range(1, nb):
                    arrival(p, (b + m) % nb).wait_recv()

        candidates = jnp.concatenate([halo[sweep, p] for p in range(3)], axis=1)
        if sweep == 0:
            jac_copy.wait()
        acc = jnp.zeros((elems * rows, LANES), jnp.float32)
        for k in range(faces):
            picked = jnp.dot(candidates, select[k], preferred_element_type=jnp.float32)
            acc = acc + jnp.dot(
                jac_v[:, k].reshape(elems * rows, -1),
                picked.astype(jnp.bfloat16),
                preferred_element_type=jnp.float32,
            )
        upd[...] = acc.reshape(upd.shape)
        product = jnp.zeros((rows, LANES), jnp.float32)
        for e in range(elems):
            mine = (lane >= RHS * e) & (lane < RHS * e + RHS)
            product = product + jnp.where(mine, upd[e], 0.0)
        image = start_ref[2] * adjoint + product
        send_r[sweep] = (start_ref[1] - image).astype(jnp.bfloat16)

        def blk_copy(m, sweep=sweep):
            return pltpu.make_async_remote_copy(
                src_ref=send_r.at[sweep],
                dst_ref=full_r.at[sweep, own_rows],
                send_sem=bk_send.at[sweep, m],
                recv_sem=bk_recv.at[sweep, b],
                device_id=(d, (b + m) % nb),
                device_id_type=MESH,
            )

        for m in range(1, nb):
            blk_copy(m).start()
        full_r[sweep, own_rows] = send_r[sweep]
        for m in range(1, nb):
            blk_copy(m).wait_send()
        for m in range(1, nb):
            src_b = (b + m) % nb
            pltpu.make_async_remote_copy(
                src_ref=send_r.at[sweep],
                dst_ref=full_r.at[sweep, pl.ds(pl.multiple_of(src_b * rows, 16), rows)],
                send_sem=bk_send.at[sweep, 0],
                recv_sem=bk_recv.at[sweep, src_b],
                device_id=(d, src_b),
                device_id_type=MESH,
            ).wait_recv()
        if sweep == 0:
            inv_copy.wait()
        upd[...] = jnp.dot(
            inv_ref[...], full_r[sweep], preferred_element_type=jnp.float32
        ).reshape(upd.shape)
        update = jnp.zeros((rows, LANES), jnp.float32)
        for e in range(elems):
            mine = (lane >= RHS * e) & (lane < RHS * e + RHS)
            update = update + jnp.where(mine, upd[e], 0.0)
        adjoint = adjoint + update
    out_ref[...] = adjoint

    square = jnp.concatenate([adjoint, jnp.zeros((LANES - rows, LANES), jnp.float32)], axis=0)
    final_f32 = jnp.transpose(square)[:, :rows]
    window = 16
    row = lax.broadcasted_iota(jnp.int32, (window, shape_ref.shape[2]), 0)
    wpart[pl.ds(0, LANES)] = jnp.zeros((LANES, shape_ref.shape[2]), jnp.float32)
    shape_copy.wait()
    for e in range(elems):
        low = (RHS * e) // 8 * 8
        part = jnp.dot(
            final_f32[low:low + window].astype(jnp.bfloat16),
            shape_ref[e],
            preferred_element_type=jnp.float32,
        )
        mine = (row + low >= RHS * e) & (row + low < RHS * e + RHS)
        wpart[pl.ds(low, window)] = wpart[pl.ds(low, window)] - jnp.where(mine, part, 0.0)
    chunk = wsum_ref.shape[0]
    owners = pl.cdiv(elems * RHS, chunk)

    def wcopy(c, src_b):
        return pltpu.make_async_remote_copy(
            src_ref=wpart.at[pl.ds(c * chunk, chunk)],
            dst_ref=wpart.at[pl.ds(LANES + src_b * chunk, chunk)],
            send_sem=ws_send.at[c],
            recv_sem=ws_recv.at[src_b],
            device_id=(d, c),
            device_id_type=MESH,
        )

    for m in range(1, nb):
        c = (b + m) % nb
        pl.when(c < owners)(lambda c=c: wcopy(c, b).start())
    for m in range(1, nb):
        c = (b + m) % nb
        pl.when(c < owners)(lambda c=c: wcopy(c, b).wait_send())
    total = jnp.zeros(wsum_ref.shape, jnp.float32)
    for m in range(1, nb):
        src_b = (b + m) % nb

        @pl.when(b < owners)
        def _(src_b=src_b):
            wcopy(b, src_b).wait_recv()

    @pl.when(b < owners)
    def _():
        acc = wpart[pl.ds(pl.multiple_of(b * chunk, 8), chunk)]
        for m in range(1, nb):
            src_b = (b + m) % nb
            acc = acc + wpart[pl.ds(pl.multiple_of(LANES + src_b * chunk, 8), chunk)]
        wsum_ref[...] = acc

    @pl.when(b >= owners)
    def _():
        wsum_ref[...] = jnp.zeros(wsum_ref.shape, jnp.float32)


def sweeps(adjoint_start, right_sides, pseudo_shift, slots, jac_blocks, block_inverse,
           shape_partials, nb):
    elems, rhs, rows = adjoint_start.shape
    cols = jac_blocks.shape[-1]
    faces = jac_blocks.shape[1]

    stacked = jnp.stack([
        adjoint_start,
        right_sides,
        jnp.broadcast_to(pseudo_shift[:, None, None], adjoint_start.shape),
    ])
    stacked = jnp.transpose(stacked, (0, 3, 1, 2)).reshape(3, rows, elems * rhs)
    stacked = jnp.pad(stacked, ((0, 0), (0, 0), (0, LANES - elems * rhs)))
    part, within = slots // elems, slots % elems
    lanes = (part * LANES + within * rhs)[:, :, None] + jnp.arange(rhs, dtype=jnp.int32)
    target = jnp.transpose(lanes, (1, 0, 2)).reshape(faces, elems * rhs)
    target = jnp.pad(target, ((0, 8 - faces), (0, LANES - elems * rhs)), constant_values=-1)
    vmem = pl.BlockSpec(memory_space=pltpu.VMEM)
    hbm = pl.BlockSpec(memory_space=pl.ANY)
    chunk = 8 * rhs
    out, wsum = pl.pallas_call(
        _sweeps_kernel,
        out_shape=(
            jax.ShapeDtypeStruct((rows, LANES), jnp.float32),
            jax.ShapeDtypeStruct((chunk, shape_partials.shape[2]), jnp.float32),
        ),
        in_specs=[vmem, vmem, hbm, hbm, hbm],
        out_specs=(vmem, vmem),
        scratch_shapes=[
            pltpu.VMEM((elems, faces, rows, cols), jnp.bfloat16),
            pltpu.VMEM((elems * rows, cols), jnp.bfloat16),
            pltpu.VMEM(shape_partials.shape, shape_partials.dtype),
            pltpu.VMEM((faces, 3 * LANES, LANES), jnp.bfloat16),
            pltpu.VMEM((SWEEPS, rows, LANES), jnp.bfloat16),
            pltpu.VMEM((SWEEPS, 3, nb * rows, LANES), jnp.bfloat16),
            pltpu.VMEM((SWEEPS, rows, LANES), jnp.bfloat16),
            pltpu.VMEM((SWEEPS, nb * rows, LANES), jnp.bfloat16),
            pltpu.VMEM((elems, rows, LANES), jnp.float32),
            pltpu.SemaphoreType.DMA((3,)),
            pltpu.SemaphoreType.DMA((SWEEPS, 3, nb)),
            pltpu.SemaphoreType.DMA((SWEEPS, 3, nb)),
            pltpu.SemaphoreType.DMA((SWEEPS, nb)),
            pltpu.SemaphoreType.DMA((SWEEPS, nb)),
            pltpu.SemaphoreType.DMA((SWEEPS, 2, nb)),
            pltpu.VMEM((LANES + nb * chunk, shape_partials.shape[2]), jnp.float32),
            pltpu.SemaphoreType.DMA((nb,)),
            pltpu.SemaphoreType.DMA((nb,)),
        ],
        compiler_params=pltpu.CompilerParams(
            collective_id=0, has_side_effects=True, vmem_limit_bytes=67043328 - 640 * 1024
        ),
    )(
        stacked,
        target,
        jac_blocks,
        block_inverse.reshape(elems * rows, cols),
        shape_partials,
    )
    adjoint = jnp.transpose(out[:, : elems * rhs].reshape(rows, elems, rhs), (1, 2, 0))
    return adjoint, wsum


def local(
    adjoint_start,
    right_sides,
    jac_blocks,
    block_inverse,
    neighbours,
    pseudo_shift,
    shape_partials,
    node_ids,
):
    local_count = neighbours.shape[0]
    nb = lax.axis_size("blk")
    part_index = lax.axis_index("dom")
    own = jnp.arange(local_count, dtype=jnp.int32)[:, None] + local_count
    slots = jnp.concatenate([own, neighbours - (part_index - 1) * local_count], axis=1)
    adjoint, wsum = sweeps(
        adjoint_start, right_sides, pseudo_shift, slots, jac_blocks, block_inverse,
        shape_partials, nb,
    )
    node_width = node_ids.shape[1]
    chunk_elems = wsum.shape[0] // RHS
    values = wsum.reshape(chunk_elems, RHS, node_width, 3)
    values = jnp.transpose(values, (0, 2, 1, 3)).reshape(chunk_elems * node_width, RHS * 3)
    my_nodes = lax.dynamic_slice_in_dim(
        node_ids, jnp.minimum(lax.axis_index("blk") * chunk_elems, local_count - chunk_elems),
        chunk_elems,
    )
    node_slots = (my_nodes - (part_index - 1) * NODE_DEV).reshape(-1)
    partial_sums = jax.ops.segment_sum(values, node_slots, 3 * NODE_DEV).T
    chunks = jnp.transpose(
        partial_sums.reshape(RHS * 3, 3, nb, NODE_DEV // nb), (1, 2, 0, 3)
    )
    shape_gradient = node_reduce(chunks, collective_id=1)
    return (adjoint, shape_gradient)


def solution(mesh):
    in_specs = (
        P("dom", None, "blk"),
        P("dom", None, "blk"),
        P("dom", None, "blk", None),
        P("dom", "blk", None),
        P("dom", None),
        P("dom"),
        P("dom", "blk", None),
        P("dom", None),
    )
    out_specs = (P("dom", None, "blk"), P(None, ("dom", "blk")))
    return jax.shard_map(local, mesh=mesh, in_specs=in_specs, out_specs=out_specs, check_vma=False)
```
